256 devices in a mesh: ctx: 64 (over x, z, core), head: 4 (over y).
Axes of the slice: x: 4, y: 4, z: 8, core: 2. Of those that a mesh axis runs over, the one named last changes fastest.
Arguments:
- tokens_in: bfloat16 [16384, 2048], P('ctx'), may hold values from -6 to 6
- w_qkv: bfloat16 [3, 2048, 2048], P(None, None, 'head'), may hold values from -0.125 to 0.125
- conv_weight: float32 [3, 4, 2048], P(None, None, 'head'), may hold values from -2.5 to 2.5
- beta_weight: bfloat16 [16, 2048], P('head'), may hold values from -0.125 to 0.125
- beta_bias: float32 [16], P('head'), may hold values from -4 to 1
- norm_gain: float32 [2048], P('head'), may hold values from 0.1 to 1.9
- w_out: bfloat16 [2048, 2048], P('head'), may hold values from -0.125 to 0.125
Outputs:
- layer_out: bfloat16 [16384, 2048], P(('ctx', 'head'))
The draws below stay inside these ranges and needn't reach their ends.
All inputs are finite; a program needn't handle non-finite values.
Results may differ from the reference program's by a relative error of at most 0.019.
Values may be sent and summed in bfloat16 or wider, within the bound.
No kernel may reach another device: no remote copies, remote signals or barrier semaphores. Data moves between devices by JAX's collectives and lax.ppermute only.
A program may use at most 128 MiB of HBM per device.

```python
import jax
import jax.numpy as jnp
from jax import lax

D = 2048
HEADS = 16
DK = 128
CONV = 4
BLOCK = 128
TOKENS = 16384


def steps_of(rng, extent, cuts, least, top_value):
    def one(dim, blocks):
        draws = jax.random.uniform(jax.random.fold_in(jax.random.fold_in(rng, 6), dim), (blocks,), jnp.float32, least / len(cuts), top_value / len(cuts))
        return jnp.repeat(jnp.exp(draws), extent[dim] // blocks).reshape((-1,) + (1,) * (len(extent) - dim - 1))

    level = one(*cuts[0])
    for cut in cuts[1:]:
        level = level * one(*cut)
    return level


def normal_values(rng, shape, scale, limit, pieces=(), kind=jnp.bfloat16):
    loudness = steps_of(rng, shape, pieces, -0.22, 0.18) if pieces else 1.0
    array = jax.random.normal(rng, shape, jnp.float32) * scale * loudness
    return jnp.minimum(jnp.maximum(array, -limit), limit).astype(kind)


def setup_inputs(seed: int = 0) -> dict:
    key_list = jax.random.split(jax.random.key(seed), 8)
    return {
        "tokens_in": normal_values(key_list[0], (TOKENS, D), 1.0, 6.0, ((0, 64),)),
        "w_qkv": normal_values(key_list[1], (3, D, HEADS * DK), D ** -0.5, 0.125, ((2, 4),)),
        "conv_weight": normal_values(key_list[2], (3, CONV, HEADS * DK), 0.5, 2.5, ((2, 4),), jnp.float32),
        "beta_weight": normal_values(key_list[3], (HEADS, D), D ** -0.5, 0.125, ((0, 4),)),
        "beta_bias": jnp.clip(-4.0 + 5.0 * jax.random.uniform(key_list[4], (HEADS,), jnp.float32) ** steps_of(key_list[4], (HEADS,), ((0, 4),), -0.2, 0.2), -4.0, 1.0),
        "norm_gain": jnp.clip(1.0 + 0.18 * jax.random.normal(key_list[5], (HEADS * DK,), jnp.float32), 0.1, 1.9),
        "w_out": normal_values(key_list[6], (HEADS * DK, D), (HEADS * DK) ** -0.5, 0.125, ((0, 4),)),
    }


precise = lax.Precision.HIGHEST

def conv_silu(projected, kernel):
    taps = kernel.shape[0]
    length = projected.shape[0]
    padded = jnp.concatenate([jnp.zeros((taps - 1, projected.shape[1]), jnp.float32), projected.astype(jnp.float32)], axis=0)
    total = jnp.zeros((length, projected.shape[1]), jnp.float32)
    for offset in range(taps):
        total = total + kernel[offset][None, :] * padded[offset:offset + length]
    return jax.nn.silu(total)

def unit_rows(vector):
    return vector / jnp.sqrt(lax.optimization_barrier(jnp.sum(vector * vector, axis=-1, keepdims=True)) + 1e-06)

def block_terms(queries, keys, values, betas):
    size = keys.shape[-2]
    width = keys.shape[-1]
    strict = jnp.tril(jnp.ones((size, size), jnp.float32), -1)
    inclusive = jnp.tril(jnp.ones((size, size), jnp.float32))
    gram = jnp.einsum('...ik,...jk->...ij', keys, keys, precision=precise)
    system = jnp.eye(size, dtype=jnp.float32) + betas[..., :, None] * gram * strict
    weighted = betas[..., :, None] * jnp.concatenate([values, keys], axis=-1)
    solved = jax.scipy.linalg.solve_triangular(system, weighted, lower=True, unit_diagonal=True)
    scores = jnp.einsum('...ik,...jk->...ij', queries, keys, precision=precise) * inclusive
    return (solved[..., :width], solved[..., width:], scores)

def head_output(index, tokens_in, w_qkv, conv_weight, beta_weight, beta_bias, norm_gain):
    first = index * DK
    columns = lax.dynamic_slice_in_dim(w_qkv, first, DK, 2)
    mixed = []
    for which in range(3):
        projected = jnp.dot(tokens_in.astype(jnp.float32), columns[which].astype(jnp.float32), preferred_element_type=jnp.float32).astype(jnp.bfloat16)
        kernel = lax.dynamic_slice_in_dim(conv_weight[which], first, DK, 1)
        mixed.append(conv_silu(projected, kernel))
    queries = unit_rows(mixed[0])
    keys = unit_rows(mixed[1])
    values = mixed[2]
    logits = jnp.dot(tokens_in.astype(jnp.float32), beta_weight[index].astype(jnp.float32), preferred_element_type=jnp.float32)
    betas = jax.nn.sigmoid(logits + beta_bias[index])
    count = TOKENS // BLOCK
    queries = queries.reshape(count, BLOCK, DK)
    keys = keys.reshape(count, BLOCK, DK)
    values = values.reshape(count, BLOCK, DK)
    betas = betas.reshape(count, BLOCK)
    u_terms, w_terms, scores = block_terms(queries, keys, values, betas)

    def advance(state, items):
        u_block, w_block, key_block, query_block, score_block = items
        delta = u_block - jnp.dot(w_block, state.T, precision=precise)
        result = jnp.dot(query_block, state.T, precision=precise) + jnp.dot(score_block, delta, precision=precise)
        state = state + jnp.dot(delta.T, key_block, precision=precise)
        return (state, result)
    _, outputs = lax.scan(advance, jnp.zeros((DK, DK), jnp.float32), (u_terms, w_terms, keys, queries, scores))
    outputs = outputs.reshape(TOKENS, DK)
    gain = lax.dynamic_slice_in_dim(norm_gain, first, DK, 0)
    normed = outputs * lax.rsqrt(lax.optimization_barrier(jnp.mean(outputs * outputs, axis=-1, keepdims=True)) + 1e-06) * gain[None, :]
    return normed.astype(jnp.bfloat16)

def reference(tokens_in, w_qkv, conv_weight, beta_weight, beta_bias, norm_gain, w_out):

    def one_head(index):
        return head_output(index, tokens_in, w_qkv, conv_weight, beta_weight, beta_bias, norm_gain)
    stacked = lax.map(one_head, jnp.arange(HEADS, dtype=jnp.int32))
    joined = stacked.transpose(1, 0, 2).reshape(TOKENS, HEADS * DK)
    return jnp.dot(joined.astype(jnp.float32), w_out.astype(jnp.float32), preferred_element_type=jnp.float32).astype(jnp.bfloat16)
```

```python
import functools

import jax
import jax.numpy as jnp
from jax import lax
from jax.experimental import pallas as pl
from jax.experimental.pallas import tpu as pltpu
from jax.sharding import PartitionSpec as P

DK = 128
BLOCK = 128
WIDTH = 2 * BLOCK
EDGE = 16
EPS = 1e-06
FAN = 4

f32 = jnp.float32
bf16 = jnp.bfloat16


def dot(a, b):
    return lax.dot_general(a, b, (((1,), (0,)), ((), ())), preferred_element_type=f32)


def dot_t(a, b):
    return lax.dot_general(a, b, (((1,), (1,)), ((), ())), preferred_element_type=f32)


def params(megabytes=48):
    return pltpu.CompilerParams(vmem_limit_bytes=megabytes << 20)


def whole(count):
    return [pl.BlockSpec(memory_space=pltpu.VMEM)] * count


def shape(dims, kind):
    return jax.ShapeDtypeStruct(dims, kind)


def project_kernel(tokens_ref, w_ref, beta_w_ref, beta_b_ref, out_ref, edge_ref, betas_ref):
    length = tokens_ref.shape[0]
    result = dot(tokens_ref[...], w_ref[0]).astype(bf16)
    out_ref[0] = result
    edge_ref[0] = result[length - EDGE :]

    @pl.when((pl.program_id(0) == 0) & (pl.program_id(1) == 0))
    def _():
        logits = dot_t(tokens_ref[...], beta_w_ref[...]) + beta_b_ref[...]
        betas_ref[...] = 1.0 / (1.0 + jnp.exp(-logits))


def project(tokens, w_qkv, beta_weight, beta_bias):
    length, depth = tokens.shape
    columns = w_qkv.shape[2]
    heads = beta_weight.shape[0]
    part = columns // 2
    return pl.pallas_call(
        project_kernel,
        grid=(3, 2),
        in_specs=[
            pl.BlockSpec((length, depth), lambda s, n: (0, 0)),
            pl.BlockSpec((1, depth, part), lambda s, n: (s, 0, n)),
            pl.BlockSpec((heads, depth), lambda s, n: (0, 0)),
            pl.BlockSpec((1, heads), lambda s, n: (0, 0)),
        ],
        out_specs=[
            pl.BlockSpec((1, length, part), lambda s, n: (s, 0, n)),
            pl.BlockSpec((1, EDGE, part), lambda s, n: (s, 0, n)),
            pl.BlockSpec((length, heads), lambda s, n: (0, 0)),
        ],
        out_shape=[
            shape((3, length, columns), bf16),
            shape((3, EDGE, columns), bf16),
            shape((length, heads), f32),
        ],
        compiler_params=params(),
        name="project",
    )(tokens, w_qkv, beta_weight, beta_bias[None, :])


def grid_index(rows, columns):
    row = lax.broadcasted_iota(jnp.int32, (rows, columns), 0)
    column = lax.broadcasted_iota(jnp.int32, (rows, columns), 1)
    return row, column


def on_diagonal(pair, left):
    zero = jnp.zeros_like(pair)
    return jnp.concatenate([jnp.where(left, pair, zero), jnp.where(left, zero, pair)], axis=0)


def inverse_pairs(systems):
    row, wide = grid_index(BLOCK, 2 * BLOCK)
    column = wide % BLOCK
    left = wide < BLOCK
    eye = jnp.where(row == column, 1.0, 0.0).astype(f32)

    def below(size):
        same = (row // (2 * size)) == (column // (2 * size))
        return same & ((row % (2 * size)) >= size) & ((column % (2 * size)) < size)

    found = [eye - jnp.where(below(1), system, 0.0) for system in systems]
    size = 2
    while size < BLOCK:
        mask = below(size)
        steps = [jnp.where(mask, system, 0.0).astype(bf16) for system in systems]
        small = [x.astype(bf16) for x in found]
        half = [dot(x, on_diagonal(n, left)).astype(bf16) for x, n in zip(small, steps)]
        found = [
            x - dot(y, on_diagonal(b, left)) for x, y, b in zip(found, half, small)
        ]
        size *= 2
    small = [x.astype(bf16) for x in found]
    high = [system.astype(bf16) for system in systems]
    low = [(system - h.astype(f32)).astype(bf16) for system, h in zip(systems, high)]
    rest = [
        (eye - x.astype(f32)) - dot(x, on_diagonal(h, left)) - dot(x, on_diagonal(l, left))
        for x, h, l in zip(small, high, low)
    ]
    fixed = [
        x.astype(f32) + dot(r.astype(bf16), on_diagonal(x, left)) for x, r in zip(small, rest)
    ]
    return [x - eye for x in fixed]


def local_kernel(
    proj_ref, edge_ref, conv_ref, betas_ref,
    queries_ref, keys_t_ref, uw_ref, map0, map1, map2, map3, padded, maps
):
    length = proj_ref.shape[1]
    heads = betas_ref.shape[1]
    me = lax.axis_index("ctx") % FAN
    for s in range(3):
        padded[s, :EDGE] = edge_ref[s].astype(f32)
        padded[s, EDGE:] = proj_ref[s].astype(f32)
    row, column = grid_index(length, length)
    strict = row > column
    systems, corners, right, keys_t = [], [], [], []
    for h in range(heads):
        lanes = slice(h * DK, (h + 1) * DK)
        mixed = []
        for s in range(3):
            total = jnp.zeros((length, DK), f32)
            for j in range(4):
                start = EDGE - 3 + j
                total = total + conv_ref[s, j : j + 1, lanes] * padded[s, start : start + length, lanes]
            mixed.append(total / (1.0 + jnp.exp(-total)))
        query, key, value = mixed
        query = query * lax.rsqrt(jnp.sum(query * query, axis=-1, keepdims=True) + EPS)
        key = key * lax.rsqrt(jnp.sum(key * key, axis=-1, keepdims=True) + EPS)
        queries_ref[:, lanes] = query.astype(bf16)
        small = key.astype(bf16)
        small_t = key.T.astype(bf16)
        keys_t_ref[h] = small_t
        keys_t.append(small_t)
        beta = betas_ref[:, h : h + 1]
        system = jnp.where(strict, beta * dot(small, small_t), 0.0)
        systems.append(jnp.concatenate([system[:BLOCK, :BLOCK], system[BLOCK:, BLOCK:]], axis=1))
        corners.append(system[BLOCK:, :BLOCK].astype(bf16))
        right.append(beta * jnp.concatenate([value, small.astype(f32)], axis=1))
    lowers = [x.astype(bf16) for x in inverse_pairs(systems)]
    firsts = [
        r[:BLOCK] + dot(low[:, :BLOCK], r[:BLOCK].astype(bf16)) for low, r in zip(lowers, right)
    ]
    seconds = [
        r[BLOCK:] - dot(corner, first.astype(bf16))
        for corner, r, first in zip(corners, right, firsts)
    ]
    seconds = [r + dot(low[:, BLOCK:], r.astype(bf16)) for low, r in zip(lowers, seconds)]
    for h in range(heads):
        uw = jnp.concatenate([firsts[h], seconds[h]], axis=0).astype(bf16)
        uw_ref[h] = uw
        maps[h] = dot(keys_t[h], uw).astype(bf16)
    for s, out in enumerate((map0, map1, map2, map3)):
        out[...] = maps[me ^ s]


def local_maps(projected, edge, conv_weight, betas):
    length, columns = projected.shape[1:]
    heads = betas.shape[1]
    one = shape((DK, 2 * DK), bf16)
    return pl.pallas_call(
        local_kernel,
        in_specs=whole(4),
        out_specs=whole(7),
        out_shape=[
            shape((length, columns), bf16),
            shape((heads, DK, length), bf16),
            shape((heads, length, 2 * DK), bf16),
            one, one, one, one,
        ],
        scratch_shapes=[
            pltpu.VMEM((3, EDGE + length, columns), f32),
            pltpu.VMEM((heads, DK, 2 * DK), bf16),
        ],
        compiler_params=params(),
        name="local_maps",
    )(projected, edge, conv_weight, betas)


def inner_kernel(queries_ref, keys_t_ref, uw_ref, base_ref, gate_ref):
    length = queries_ref.shape[0]
    row, column = grid_index(length, length)
    for h in range(keys_t_ref.shape[0]):
        lanes = slice(h * DK, (h + 1) * DK)
        query = queries_ref[:, lanes]
        scores = jnp.where(row >= column, dot(query, keys_t_ref[h]), 0.0).astype(bf16)
        both = dot(scores, uw_ref[h])
        base_ref[:, lanes] = both[:, :DK]
        gate_ref[:, lanes] = (query.astype(f32) - both[:, DK:]).astype(bf16)


def inner_outputs(queries, keys_t, uw):
    length, columns = queries.shape
    heads = keys_t.shape[0]
    return pl.pallas_call(
        inner_kernel,
        in_specs=whole(3),
        out_specs=whole(2),
        out_shape=[shape((length, columns), f32), shape((length, columns), bf16)],
        compiler_params=params(),
        cost_estimate=pl.CostEstimate(
            flops=2 * heads * length * length * 3 * DK, bytes_accessed=2 << 20, transcendentals=0
        ),
        name="inner_outputs",
    )(queries, keys_t, uw)


def then(earlier, later):
    return earlier + later - dot(later[:, DK:].astype(bf16), earlier.astype(bf16))


def advance(state, later):
    return state + later[:, :DK] - dot(later[:, DK:].astype(bf16), state.astype(bf16))


def group_kernel(m0, m1, m2, m3, out_ref, kept):
    me = lax.axis_index("ctx") % FAN
    for s, ref in enumerate((m0, m1, m2, m3)):
        kept[me ^ s] = ref[...].astype(f32)
    out_ref[...] = then(then(kept[0], kept[1]), then(kept[2], kept[3])).astype(bf16)


def group_map(parts):
    return pl.pallas_call(
        group_kernel,
        in_specs=whole(4),
        out_specs=pl.BlockSpec(memory_space=pltpu.VMEM),
        out_shape=shape((DK, 2 * DK), bf16),
        scratch_shapes=[pltpu.VMEM((FAN, DK, 2 * DK), f32)],
        compiler_params=params(),
        name="group_map",
    )(*parts)


def row_kernel(m0, m1, m2, m3, total_ref, before_ref, kept):
    me = (lax.axis_index("ctx") // FAN) % FAN
    for s, ref in enumerate((m0, m1, m2, m3)):
        kept[(me + FAN - s) % FAN] = ref[...].astype(f32)
    two = then(kept[0], kept[1])
    three = then(two, kept[2])
    total_ref[...] = then(three, kept[3]).astype(bf16)
    zero = jnp.zeros((DK, 2 * DK), f32)
    one = kept[0]
    before = jnp.where(me == 0, zero, jnp.where(me == 1, one, jnp.where(me == 2, two, three)))
    before_ref[...] = before.astype(bf16)


def row_map(parts):
    return pl.pallas_call(
        row_kernel,
        in_specs=whole(4),
        out_specs=whole(2),
        out_shape=[shape((DK, 2 * DK), bf16)] * 2,
        scratch_shapes=[pltpu.VMEM((FAN, DK, 2 * DK), f32)],
        compiler_params=params(),
        name="row_map",
    )(*parts)


def start_kernel(r1, r2, r3, before_ref, m0, m1, m2, m3, s0, s1, s2, s3, kept, states):
    me = lax.axis_index("ctx") % FAN
    state = r3[:, :DK].astype(f32)
    state = advance(state, r2[...].astype(f32))
    state = advance(state, r1[...].astype(f32))
    state = advance(state, before_ref[...].astype(f32))
    for s, ref in enumerate((m0, m1, m2, m3)):
        kept[me ^ s] = ref[...]
    for j in range(FAN):
        states[j] = state.astype(bf16)
        if j < FAN - 1:
            state = advance(state, kept[j].astype(f32))
    for s, out in enumerate((s0, s1, s2, s3)):
        out[...] = states[me ^ s]


def start_states(rows, before, parts):
    return pl.pallas_call(
        start_kernel,
        in_specs=whole(8),
        out_specs=whole(4),
        out_shape=[shape((DK, DK), bf16)] * 4,
        scratch_shapes=[
            pltpu.VMEM((FAN, DK, 2 * DK), bf16),
            pltpu.VMEM((FAN, DK, DK), bf16),
        ],
        compiler_params=params(),
        name="start_states",
    )(*rows, before, *parts)


def finish_kernel(base_ref, gate_ref, s0, s1, s2, s3, gain_ref, w_ref, out_ref, states):
    me = lax.axis_index("ctx") % FAN
    for s, ref in enumerate((s0, s1, s2, s3)):
        states[me ^ s] = ref[...]
    pieces = []
    for h in range(FAN):
        lanes = slice(h * DK, (h + 1) * DK)
        heads_out = base_ref[:, lanes] + dot(gate_ref[:, lanes], states[h])
        scale = lax.rsqrt(jnp.mean(heads_out * heads_out, axis=-1, keepdims=True) + EPS)
        pieces.append((heads_out * scale * gain_ref[:, lanes]).astype(bf16))
    normed = jnp.concatenate(pieces, axis=1)
    out_ref[...] = dot(normed, w_ref[...]).astype(bf16)


def finish(base, gate, states, norm_gain, w_out):
    length, columns = base.shape
    return pl.pallas_call(
        finish_kernel,
        in_specs=whole(8),
        out_specs=pl.BlockSpec(memory_space=pltpu.VMEM),
        out_shape=shape((length, w_out.shape[1]), bf16),
        scratch_shapes=[pltpu.VMEM((FAN, DK, DK), bf16)],
        compiler_params=params(),
        name="finish",
    )(base, gate, *states, norm_gain[None, :], w_out)


def swaps(count, by):
    return [(i, i ^ by) for i in range(count)]


def row_shift(count, by):
    return [
        (i, i - (i // FAN % FAN) * FAN + (i // FAN + by) % FAN * FAN) for i in range(count)
    ]


def plane_shift(count, by):
    step = by * FAN * FAN
    return [(i, i + step) for i in range(count - step)]


def per_device(tokens_in, w_qkv, conv_weight, beta_weight, beta_bias, norm_gain, w_out):
    peers = lax.axis_size("ctx")
    projected, edge, betas = project(tokens_in, w_qkv, beta_weight, beta_bias)
    edge = lax.ppermute(edge, "ctx", [(i, i + 1) for i in range(peers - 1)])
    queries, keys_t, uw, *maps = local_maps(projected, edge, conv_weight, betas)
    parts = [maps[0]] + [lax.ppermute(maps[s], "ctx", swaps(peers, s)) for s in range(1, FAN)]
    base, gate = inner_outputs(queries, keys_t, uw)
    mine = group_map(parts)
    rows = [mine] + [lax.ppermute(mine, "ctx", row_shift(peers, s)) for s in range(1, FAN)]
    total, before = row_map(rows)
    planes = [lax.ppermute(total, "ctx", plane_shift(peers, s)) for s in range(1, FAN)]
    starts = start_states(planes, before, parts)
    states = [starts[0]] + [
        lax.ppermute(starts[s], "ctx", swaps(peers, s)) for s in range(1, FAN)
    ]
    partial = finish(base, gate, states, norm_gain, w_out)
    return lax.psum_scatter(partial, "head", scatter_dimension=0, tiled=True)


def solution(mesh):
    return jax.shard_map(
        per_device,
        mesh=mesh,
        in_specs=(
            P("ctx", None),
            P(None, None, "head"),
            P(None, None, "head"),
            P("head", None),
            P("head"),
            P("head"),
            P("head", None),
        ),
        out_specs=P(("ctx", "head"), None),
        check_vma=False,
    )
```

```python
import jax
import jax.numpy as jnp
from jax import lax
from jax.experimental import pallas as pl
from jax.experimental.pallas import tpu as pltpu
from jax.sharding import PartitionSpec as P

DK = 128
BLOCK = 128
WIDTH = 2 * BLOCK
EDGE = 16
EPS = 1e-06
FAN = 4

f32 = jnp.float32
bf16 = jnp.bfloat16


def dot(a, b):
    return lax.dot_general(a, b, (((1,), (0,)), ((), ())), preferred_element_type=f32)


def dot_t(a, b):
    return lax.dot_general(a, b, (((1,), (1,)), ((), ())), preferred_element_type=f32)


def params(megabytes=48):
    return pltpu.CompilerParams(vmem_limit_bytes=megabytes << 20)


def whole(count):
    return [pl.BlockSpec(memory_space=pltpu.VMEM)] * count


def shape(dims, kind):
    return jax.ShapeDtypeStruct(dims, kind)


PIECES = 2


def project_kernel(
    tokens_hbm, w_hbm, beta_w_hbm, beta_b_ref, out_ref, edge_ref, betas_ref,
    tokens_ref, w_ref, beta_w_ref, small_sems, w_sems
):
    length, depth = tokens_ref.shape
    part = depth // PIECES
    first = pltpu.make_async_copy(tokens_hbm, tokens_ref, small_sems.at[0])
    first.start()
    copies = []
    for s in range(3):
        for k in range(PIECES):
            rows = pl.ds(k * part, part)
            copy = pltpu.make_async_copy(
                w_hbm.at[s, rows], w_ref.at[s, rows], w_sems.at[s * PIECES + k]
            )
            copy.start()
            copies.append(copy)
    last = pltpu.make_async_copy(beta_w_hbm, beta_w_ref, small_sems.at[1])
    last.start()
    first.wait()
    for s in range(3):
        total = None
        for k in range(PIECES):
            rows = slice(k * part, (k + 1) * part)
            copies[s * PIECES + k].wait()
            term = dot(tokens_ref[:, rows], w_ref[s, rows])
            total = term if total is None else total + term
        result = total.astype(bf16)
        out_ref[s] = result
        edge_ref[s] = result[length - EDGE :]
    last.wait()
    logits = dot_t(tokens_ref[...], beta_w_ref[...]) + beta_b_ref[...]
    betas_ref[...] = 1.0 / (1.0 + jnp.exp(-logits))


def project(tokens, w_qkv, beta_weight, beta_bias):
    length, depth = tokens.shape
    columns = w_qkv.shape[2]
    heads = beta_weight.shape[0]
    far = pl.BlockSpec(memory_space=pltpu.HBM)
    return pl.pallas_call(
        project_kernel,
        in_specs=[far, far, far, pl.BlockSpec(memory_space=pltpu.VMEM)],
        out_specs=whole(3),
        out_shape=[
            shape((3, length, columns), bf16),
            shape((3, EDGE, columns), bf16),
            shape((length, heads), f32),
        ],
        scratch_shapes=[
            pltpu.VMEM(tokens.shape, bf16),
            pltpu.VMEM(w_qkv.shape, bf16),
            pltpu.VMEM(beta_weight.shape, bf16),
            pltpu.SemaphoreType.DMA((2,)),
            pltpu.SemaphoreType.DMA((3 * PIECES,)),
        ],
        compiler_params=params(),
        name="project",
    )(tokens, w_qkv, beta_weight, beta_bias[None, :])


def grid_index(rows, columns):
    row = lax.broadcasted_iota(jnp.int32, (rows, columns), 0)
    column = lax.broadcasted_iota(jnp.int32, (rows, columns), 1)
    return row, column


def on_diagonal(pair, left):
    zero = jnp.zeros_like(pair)
    return jnp.concatenate([jnp.where(left, pair, zero), jnp.where(left, zero, pair)], axis=0)


def inverse_pairs(systems):
    row, wide = grid_index(BLOCK, 2 * BLOCK)
    column = wide % BLOCK
    left = wide < BLOCK
    eye = jnp.where(row == column, 1.0, 0.0).astype(f32)

    def below(size):
        same = (row // (2 * size)) == (column // (2 * size))
        return same & ((row % (2 * size)) >= size) & ((column % (2 * size)) < size)

    found = [eye - jnp.where(below(1), system, 0.0) for system in systems]
    size = 2
    while size < BLOCK:
        mask = below(size)
        steps = [jnp.where(mask, system, 0.0).astype(bf16) for system in systems]
        small = [x.astype(bf16) for x in found]
        half = [dot(x, on_diagonal(n, left)).astype(bf16) for x, n in zip(small, steps)]
        found = [
            x - dot(y, on_diagonal(b, left)) for x, y, b in zip(found, half, small)
        ]
        size *= 2
    small = [x.astype(bf16) for x in found]
    high = [system.astype(bf16) for system in systems]
    low = [(system - h.astype(f32)).astype(bf16) for system, h in zip(systems, high)]
    rest = [
        (eye - x.astype(f32)) - dot(x, on_diagonal(h, left)) - dot(x, on_diagonal(l, left))
        for x, h, l in zip(small, high, low)
    ]
    fixed = [
        x.astype(f32) + dot(r.astype(bf16), on_diagonal(x, left)) for x, r in zip(small, rest)
    ]
    return [x - eye for x in fixed]


def local_kernel(
    proj_ref, edge_ref, conv_ref, betas_ref,
    queries_ref, keys_t_ref, uw_ref, keep_ref, send_ref, padded, maps
):
    length = proj_ref.shape[1]
    heads = betas_ref.shape[1]
    core = lax.axis_index("ctx") % 2
    for s in range(3):
        padded[s, :EDGE] = edge_ref[s].astype(f32)
        padded[s, EDGE:] = proj_ref[s].astype(f32)
    row, column = grid_index(length, length)
    strict = row > column
    systems, corners, right, keys_t = [], [], [], []
    for h in range(heads):
        lanes = slice(h * DK, (h + 1) * DK)
        mixed = []
        for s in range(3):
            total = jnp.zeros((length, DK), f32)
            for j in range(4):
                start = EDGE - 3 + j
                total = total + conv_ref[s, j : j + 1, lanes] * padded[s, start : start + length, lanes]
            mixed.append(total / (1.0 + jnp.exp(-total)))
        query, key, value = mixed
        query = query * lax.rsqrt(jnp.sum(query * query, axis=-1, keepdims=True) + EPS)
        key = key * lax.rsqrt(jnp.sum(key * key, axis=-1, keepdims=True) + EPS)
        queries_ref[:, lanes] = query.astype(bf16)
        small = key.astype(bf16)
        small_t = key.T.astype(bf16)
        keys_t_ref[h] = small_t
        keys_t.append(small_t)
        beta = betas_ref[:, h : h + 1]
        system = jnp.where(strict, beta * dot(small, small_t), 0.0)
        systems.append(jnp.concatenate([system[:BLOCK, :BLOCK], system[BLOCK:, BLOCK:]], axis=1))
        corners.append(system[BLOCK:, :BLOCK].astype(bf16))
        right.append(beta * jnp.concatenate([value, small.astype(f32)], axis=1))
    lowers = [x.astype(bf16) for x in inverse_pairs(systems)]
    firsts = [
        r[:BLOCK] + dot(low[:, :BLOCK], r[:BLOCK].astype(bf16)) for low, r in zip(lowers, right)
    ]
    seconds = [
        r[BLOCK:] - dot(corner, first.astype(bf16))
        for corner, r, first in zip(corners, right, firsts)
    ]
    seconds = [r + dot(low[:, BLOCK:], r.astype(bf16)) for low, r in zip(lowers, seconds)]
    for h in range(heads):
        uw = jnp.concatenate([firsts[h], seconds[h]], axis=0).astype(bf16)
        uw_ref[h] = uw
        maps[h] = dot(keys_t[h], uw).astype(bf16)
    for j in range(heads // 2):
        keep_ref[j] = maps[2 * j + core]
        send_ref[j] = maps[2 * j + 1 - core]


def local_maps(projected, edge, conv_weight, betas):
    length, columns = projected.shape[1:]
    heads = betas.shape[1]
    two = shape((heads // 2, DK, 2 * DK), bf16)
    return pl.pallas_call(
        local_kernel,
        in_specs=whole(4),
        out_specs=whole(5),
        out_shape=[
            shape((length, columns), bf16),
            shape((heads, DK, length), bf16),
            shape((heads, length, 2 * DK), bf16),
            two, two,
        ],
        scratch_shapes=[
            pltpu.VMEM((3, EDGE + length, columns), f32),
            pltpu.VMEM((heads, DK, 2 * DK), bf16),
        ],
        compiler_params=params(),
        name="local_maps",
    )(projected, edge, conv_weight, betas)


def inner_kernel(queries_ref, keys_t_ref, uw_ref, base_ref, gate_ref):
    length = queries_ref.shape[0]
    row, column = grid_index(length, length)
    for h in range(keys_t_ref.shape[0]):
        lanes = slice(h * DK, (h + 1) * DK)
        query = queries_ref[:, lanes]
        scores = jnp.where(row >= column, dot(query, keys_t_ref[h]), 0.0).astype(bf16)
        both = dot(scores, uw_ref[h])
        base_ref[:, lanes] = both[:, :DK]
        gate_ref[:, lanes] = (query.astype(f32) - both[:, DK:]).astype(bf16)


def inner_outputs(queries, keys_t, uw):
    length, columns = queries.shape
    heads = keys_t.shape[0]
    return pl.pallas_call(
        inner_kernel,
        in_specs=whole(3),
        out_specs=whole(2),
        out_shape=[shape((length, columns), f32), shape((length, columns), bf16)],
        compiler_params=params(),
        cost_estimate=pl.CostEstimate(
            flops=2 * heads * length * length * 3 * DK, bytes_accessed=2 << 20, transcendentals=0
        ),
        name="inner_outputs",
    )(queries, keys_t, uw)


def then(earlier, later):
    return earlier + later - dot(later[:, DK:].astype(bf16), earlier.astype(bf16))


def advance(state, later):
    return state + later[:, :DK] - dot(later[:, DK:].astype(bf16), state.astype(bf16))


MAP = shape((DK, 2 * DK), bf16)
STATE = shape((DK, DK), bf16)


def small_call(kernel, outs, name, scratch=()):
    return pl.pallas_call(
        kernel,
        out_specs=whole(len(outs)),
        out_shape=list(outs),
        scratch_shapes=list(scratch),
        compiler_params=params(),
        name=name,
    )


def ordered(mine, other, late):
    return jnp.where(late, other, mine), jnp.where(late, mine, other)


def bit(position):
    return (lax.axis_index("ctx") // position) % 2


def chip_kernel(own_ref, other_ref, keep_ref, send_ref, kept):
    late = bit(1) == 1
    for j in range(2):
        first, second = ordered(own_ref[j].astype(f32), other_ref[j].astype(f32), late)
        kept[j] = then(first, second).astype(bf16)
    keep_ref[...] = kept[bit(2)]
    send_ref[...] = kept[1 - bit(2)]


def pair_kernel(own_ref, other_ref, total_ref):
    late = bit(2) == 1
    first, second = ordered(own_ref[...].astype(f32), other_ref[...].astype(f32), late)
    total_ref[...] = then(first, second).astype(bf16)


def near_kernel(own_ref, other_ref, total_ref, before_ref):
    late = bit(4) == 1
    own, other = own_ref[...].astype(f32), other_ref[...].astype(f32)
    first, second = ordered(own, other, late)
    total_ref[...] = then(first, second).astype(bf16)
    before_ref[...] = jnp.where(late, other, jnp.zeros_like(other)).astype(bf16)


def far_kernel(own_ref, other_ref, near_ref, total_ref, before_ref):
    late = bit(8) == 1
    own, other = own_ref[...].astype(f32), other_ref[...].astype(f32)
    near = near_ref[...].astype(f32)
    first, second = ordered(own, other, late)
    total_ref[...] = then(first, second).astype(bf16)
    before_ref[...] = jnp.where(late, then(other, near), near).astype(bf16)


def rows_kernel(own_ref, other_ref, total_ref):
    late = bit(16) == 1
    first, second = ordered(own_ref[...].astype(f32), other_ref[...].astype(f32), late)
    total_ref[...] = advance(first[:, :DK], second).astype(bf16)


def pair_start_kernel(rows_ref, row_ref, before_ref, own_ref, other_ref, keep_ref, send_ref):
    state = rows_ref[...].astype(f32)
    late_row = bit(16) == 1
    row = row_ref[...].astype(f32)
    state = jnp.where(late_row, advance(state, row), state)
    state = advance(state, before_ref[...].astype(f32))
    late = bit(2) == 1
    first = jnp.where(late, other_ref[...], own_ref[...]).astype(f32)
    after = advance(state, first)
    keep_ref[...] = jnp.where(late, after, state).astype(bf16)
    send_ref[...] = jnp.where(late, state, after).astype(bf16)


def chip_start_kernel(own_state, other_state, own_maps, other_maps, keep_ref, send_ref):
    late = bit(1) == 1
    upper = bit(2) == 1
    own, other = own_state[...].astype(f32), other_state[...].astype(f32)
    for j, state in enumerate(ordered(own, other, upper)):
        first = jnp.where(late, other_maps[j], own_maps[j]).astype(f32)
        after = advance(state, first)
        keep_ref[j] = jnp.where(late, after, state).astype(bf16)
        send_ref[j] = jnp.where(late, state, after).astype(bf16)


def finish_kernel(
    base_ref, gate_ref, own_ref, other_ref, gain_ref, w_ref, mine_ref, one, two, three, states, normed
):
    core = bit(1)
    here = lax.axis_index("head")
    for j in range(2):
        states[2 * j + core] = own_ref[j]
        states[2 * j + 1 - core] = other_ref[j]
    for h in range(4):
        lanes = slice(h * DK, (h + 1) * DK)
        heads_out = base_ref[:, lanes] + dot(gate_ref[:, lanes], states[h])
        scale = lax.rsqrt(jnp.mean(heads_out * heads_out, axis=-1, keepdims=True) + EPS)
        normed[:, lanes] = (heads_out * scale * gain_ref[:, lanes]).astype(bf16)
    rows = mine_ref.shape[0]
    for s, ref in enumerate((mine_ref, one, two, three)):
        start = pl.multiple_of((here + s) % 4 * rows, rows)
        ref[...] = dot(normed[pl.ds(start, rows), :], w_ref[...]).astype(ref.dtype)


def finish(base, gate, own, other, norm_gain, w_out):
    length, columns = base.shape
    rows, width = length // 4, w_out.shape[1]
    part = shape((rows, width), bf16)
    return small_call(
        finish_kernel,
        [shape((rows, width), f32), part, part, part],
        "finish",
        [pltpu.VMEM((4, DK, DK), bf16), pltpu.VMEM((length, columns), bf16)],
    )(base, gate, own, other, norm_gain[None, :], w_out)


def swapped(x, by):
    return lax.ppermute(x, "ctx", [(i, i ^ by) for i in range(lax.axis_size("ctx"))])


def per_device(tokens_in, w_qkv, conv_weight, beta_weight, beta_bias, norm_gain, w_out):
    peers = lax.axis_size("ctx")
    projected, edge, betas = project(tokens_in, w_qkv, beta_weight, beta_bias)
    edge = lax.ppermute(edge, "ctx", [(i, i + 1) for i in range(peers - 1)])
    queries, keys_t, uw, maps, send = local_maps(projected, edge, conv_weight, betas)
    sibling = swapped(send, 1)
    base, gate = inner_outputs(queries, keys_t, uw)
    chip, send = small_call(
        chip_kernel, [MAP, MAP], "chip_map", [pltpu.VMEM((2, DK, 2 * DK), bf16)]
    )(maps, sibling)
    neighbour = swapped(send, 2)
    (pair,) = small_call(pair_kernel, [MAP], "pair_map")(chip, neighbour)
    four, near = small_call(near_kernel, [MAP, MAP], "near_map")(pair, swapped(pair, 4))
    row, before = small_call(far_kernel, [MAP, MAP], "far_map")(four, swapped(four, 8), near)
    other_row = swapped(row, 16)
    (two_rows,) = small_call(rows_kernel, [STATE], "rows_state")(row, other_row)
    rows = lax.ppermute(two_rows, "ctx", [(i, i + 32) for i in range(peers - 32)])
    state, send = small_call(pair_start_kernel, [STATE, STATE], "pair_start")(
        rows, other_row, before, chip, neighbour
    )
    back = swapped(send, 2)
    both = shape((2, DK, DK), bf16)
    own, send = small_call(chip_start_kernel, [both, both], "chip_start")(
        state, back, maps, sibling
    )
    other = swapped(send, 1)
    mine, *parts = finish(base, gate, own, other, norm_gain, w_out)
    around = lax.axis_size("head")
    for s in (2, 1, 3):
        moved = lax.ppermute(parts[s - 1], "head", [(i, (i + s) % around) for i in range(around)])
        mine = mine + moved.astype(f32)
    return mine.astype(bf16)


def solution(mesh):
    return jax.shard_map(
        per_device,
        mesh=mesh,
        in_specs=(
            P("ctx", None),
            P(None, None, "head"),
            P(None, None, "head"),
            P("head", None),
            P("head"),
            P("head"),
            P("head", None),
        ),
        out_specs=P(("ctx", "head"), None),
        check_vma=False,
    )
```

```python
import jax
import jax.numpy as jnp
from jax import lax
from jax.experimental import pallas as pl
from jax.experimental.pallas import tpu as pltpu
from jax.sharding import PartitionSpec as P

DK = 128
BLOCK = 128
WIDTH = 2 * BLOCK
EDGE = 16
EPS = 1e-06
FAN = 4

f32 = jnp.float32
bf16 = jnp.bfloat16


def dot(a, b):
    return lax.dot_general(a, b, (((1,), (0,)), ((), ())), preferred_element_type=f32)


def dot_t(a, b):
    return lax.dot_general(a, b, (((1,), (1,)), ((), ())), preferred_element_type=f32)


def params(megabytes=48):
    return pltpu.CompilerParams(vmem_limit_bytes=megabytes << 20)


def whole(count):
    return [pl.BlockSpec(memory_space=pltpu.VMEM)] * count


def shape(dims, kind):
    return jax.ShapeDtypeStruct(dims, kind)


def project_kernel(
    tokens_hbm, w_hbm, beta_w_hbm, out_ref, edge_ref, logits_ref,
    tokens_ref, w_ref, beta_w_ref, small_sems, w_sems
):
    length = tokens_ref.shape[0]
    first = pltpu.make_async_copy(tokens_hbm, tokens_ref, small_sems.at[0])
    last = pltpu.make_async_copy(beta_w_hbm, beta_w_ref, small_sems.at[1])
    copies = [pltpu.make_async_copy(w_hbm.at[s], w_ref.at[s], w_sems.at[s]) for s in range(3)]
    first.start()
    last.start()
    copies[0].start()
    copies[1].start()
    last.wait()
    first.wait()
    logits_ref[...] = dot_t(tokens_ref[...], beta_w_ref[...])
    for s in range(3):
        copies[s].wait()
        if s == 0:
            copies[2].start()
        result = dot(tokens_ref[...], w_ref[s]).astype(bf16)
        out_ref[s] = result
        edge_ref[s] = result[length - EDGE :]


def project(tokens, w_qkv, beta_weight):
    length, depth = tokens.shape
    columns = w_qkv.shape[2]
    heads = beta_weight.shape[0]
    operands = [
        pltpu.with_memory_space_constraint(x, pltpu.HBM) for x in (tokens, w_qkv, beta_weight)
    ]
    return pl.pallas_call(
        project_kernel,
        in_specs=[pl.BlockSpec(memory_space=pltpu.HBM)] * 3,
        out_specs=whole(3),
        out_shape=[
            shape((3, length, columns), bf16),
            shape((3, EDGE, columns), bf16),
            shape((length, heads), f32),
        ],
        scratch_shapes=[
            pltpu.VMEM(tokens.shape, bf16),
            pltpu.VMEM(w_qkv.shape, bf16),
            pltpu.VMEM(beta_weight.shape, bf16),
            pltpu.SemaphoreType.DMA((2,)),
            pltpu.SemaphoreType.DMA((3,)),
        ],
        compiler_params=params(),
        name="project",
    )(*operands)


def grid_index(rows, columns):
    row = lax.broadcasted_iota(jnp.int32, (rows, columns), 0)
    column = lax.broadcasted_iota(jnp.int32, (rows, columns), 1)
    return row, column


def on_diagonal(pair, left):
    zero = jnp.zeros_like(pair)
    return jnp.concatenate([jnp.where(left, pair, zero), jnp.where(left, zero, pair)], axis=0)


def inverse_pairs(systems):
    row, wide = grid_index(BLOCK, 2 * BLOCK)
    column = wide % BLOCK
    left = wide < BLOCK
    eye = jnp.where(row == column, 1.0, 0.0).astype(f32)

    def below(size):
        same = (row // (2 * size)) == (column // (2 * size))
        return same & ((row % (2 * size)) >= size) & ((column % (2 * size)) < size)

    found = [eye - jnp.where(below(1), system, 0.0) for system in systems]
    size = 2
    while size < BLOCK:
        mask = below(size)
        steps = [jnp.where(mask, system, 0.0).astype(bf16) for system in systems]
        small = [x.astype(bf16) for x in found]
        half = [dot(x, on_diagonal(n, left)).astype(bf16) for x, n in zip(small, steps)]
        found = [
            x - dot(y, on_diagonal(b, left)) for x, y, b in zip(found, half, small)
        ]
        size *= 2
    small = [x.astype(bf16) for x in found]
    high = [system.astype(bf16) for system in systems]
    low = [(system - h.astype(f32)).astype(bf16) for system, h in zip(systems, high)]
    rest = [
        (eye - x.astype(f32)) - dot(x, on_diagonal(h, left)) - dot(x, on_diagonal(l, left))
        for x, h, l in zip(small, high, low)
    ]
    fixed = [
        x.astype(f32) + dot(r.astype(bf16), on_diagonal(x, left)) for x, r in zip(small, rest)
    ]
    return [x - eye for x in fixed]


def local_kernel(
    proj_ref, edge_ref, conv_ref, logits_ref, bias_ref,
    queries_ref, keys_t_ref, uw_ref, keep_ref, send_ref, padded, maps
):
    length = proj_ref.shape[1]
    heads = logits_ref.shape[1]
    betas = 1.0 / (1.0 + jnp.exp(-(logits_ref[...] + bias_ref[...])))
    core = lax.axis_index("ctx") % 2
    for s in range(3):
        padded[s, :EDGE] = edge_ref[s].astype(f32)
        padded[s, EDGE:] = proj_ref[s].astype(f32)
    row, column = grid_index(length, length)
    strict = row > column
    systems, corners, right, keys_t = [], [], [], []
    for h in range(heads):
        lanes = slice(h * DK, (h + 1) * DK)
        mixed = []
        for s in range(3):
            total = jnp.zeros((length, DK), f32)
            for j in range(4):
                start = EDGE - 3 + j
                total = total + conv_ref[s, j : j + 1, lanes] * padded[s, start : start + length, lanes]
            mixed.append(total / (1.0 + jnp.exp(-total)))
        query, key, value = mixed
        query = query * lax.rsqrt(jnp.sum(query * query, axis=-1, keepdims=True) + EPS)
        key = key * lax.rsqrt(jnp.sum(key * key, axis=-1, keepdims=True) + EPS)
        queries_ref[h] = query.astype(bf16)
        small = key.astype(bf16)
        small_t = key.T.astype(bf16)
        keys_t_ref[h] = small_t
        keys_t.append(small_t)
        beta = betas[:, h : h + 1]
        system = jnp.where(strict, beta * dot(small, small_t), 0.0)
        systems.append(jnp.concatenate([system[:BLOCK, :BLOCK], system[BLOCK:, BLOCK:]], axis=1))
        corners.append(system[BLOCK:, :BLOCK].astype(bf16))
        right.append(beta * jnp.concatenate([value, small.astype(f32)], axis=1))
    lowers = [x.astype(bf16) for x in inverse_pairs(systems)]
    firsts = [
        r[:BLOCK] + dot(low[:, :BLOCK], r[:BLOCK].astype(bf16)) for low, r in zip(lowers, right)
    ]
    seconds = [
        r[BLOCK:] - dot(corner, first.astype(bf16))
        for corner, r, first in zip(corners, right, firsts)
    ]
    seconds = [r + dot(low[:, BLOCK:], r.astype(bf16)) for low, r in zip(lowers, seconds)]
    for h in range(heads):
        uw = jnp.concatenate([firsts[h], seconds[h]], axis=0).astype(bf16)
        uw_ref[h] = uw
        maps[h] = dot(keys_t[h], uw).astype(bf16)
    for j in range(heads // 2):
        keep_ref[j] = maps[2 * j + core]
        send_ref[j] = maps[2 * j + 1 - core]


def local_maps(projected, edge, conv_weight, logits, beta_bias):
    length, columns = projected.shape[1:]
    heads = logits.shape[1]
    two = shape((heads // 2, DK, 2 * DK), bf16)
    return pl.pallas_call(
        local_kernel,
        in_specs=whole(5),
        out_specs=whole(5),
        out_shape=[
            shape((heads, length, DK), bf16),
            shape((heads, DK, length), bf16),
            shape((heads, length, 2 * DK), bf16),
            two, two,
        ],
        scratch_shapes=[
            pltpu.VMEM((3, EDGE + length, columns), f32),
            pltpu.VMEM((heads, DK, 2 * DK), bf16),
        ],
        compiler_params=params(),
        name="local_maps",
    )(projected, edge, conv_weight, logits, beta_bias[None, :])


def inner_kernel(queries_ref, keys_t_ref, uw_ref, base_ref, gate_ref, base_out, gate_out):
    length = queries_ref.shape[1]
    row, column = grid_index(length, length)
    core = bit(1)
    for j in range(2):
        for h, base, gate in (
            (2 * j + core, base_ref, gate_ref),
            (2 * j + 1 - core, base_out, gate_out),
        ):
            query = queries_ref[h]
            scores = jnp.where(row >= column, dot(query, keys_t_ref[h]), 0.0).astype(bf16)
            both = dot(scores, uw_ref[h])
            base[j] = both[:, :DK]
            gate[j] = (query.astype(f32) - both[:, DK:]).astype(bf16)


def inner_outputs(queries, keys_t, uw):
    heads, length, _ = queries.shape
    outs = [shape((2, length, DK), f32), shape((2, length, DK), bf16)]
    return pl.pallas_call(
        inner_kernel,
        in_specs=whole(3),
        out_specs=whole(4),
        out_shape=outs + outs,
        compiler_params=params(),
        cost_estimate=pl.CostEstimate(
            flops=2 * heads * length * length * 3 * DK, bytes_accessed=2 << 20, transcendentals=0
        ),
        name="inner_outputs",
    )(queries, keys_t, uw)


def then(earlier, later):
    return earlier + later - dot(later[:, DK:].astype(bf16), earlier.astype(bf16))


def advance(state, later):
    return state + later[:, :DK] - dot(later[:, DK:].astype(bf16), state.astype(bf16))


MAP = shape((DK, 2 * DK), bf16)
STATE = shape((DK, DK), bf16)


def small_call(kernel, outs, name, scratch=()):
    return pl.pallas_call(
        kernel,
        out_specs=whole(len(outs)),
        out_shape=list(outs),
        scratch_shapes=list(scratch),
        compiler_params=params(),
        name=name,
    )


def ordered(mine, other, late):
    return jnp.where(late, other, mine), jnp.where(late, mine, other)


def bit(position):
    return (lax.axis_index("ctx") // position) % 2


def chip_kernel(own_ref, other_ref, keep_ref, send_ref, kept):
    late = bit(1) == 1
    for j in range(2):
        first, second = ordered(own_ref[j].astype(f32), other_ref[j].astype(f32), late)
        kept[j] = then(first, second).astype(bf16)
    keep_ref[...] = kept[bit(2)]
    send_ref[...] = kept[1 - bit(2)]


def pair_kernel(own_ref, other_ref, total_ref):
    late = bit(2) == 1
    first, second = ordered(own_ref[...].astype(f32), other_ref[...].astype(f32), late)
    total_ref[...] = then(first, second).astype(bf16)


def near_kernel(own_ref, other_ref, total_ref, before_ref):
    late = bit(4) == 1
    own, other = own_ref[...].astype(f32), other_ref[...].astype(f32)
    first, second = ordered(own, other, late)
    total_ref[...] = then(first, second).astype(bf16)
    before_ref[...] = jnp.where(late, other, jnp.zeros_like(other)).astype(bf16)


def far_kernel(own_ref, other_ref, near_ref, total_ref, before_ref):
    late = bit(8) == 1
    own, other = own_ref[...].astype(f32), other_ref[...].astype(f32)
    near = near_ref[...].astype(f32)
    first, second = ordered(own, other, late)
    total_ref[...] = then(first, second).astype(bf16)
    before_ref[...] = jnp.where(late, then(other, near), near).astype(bf16)


def rows_kernel(own_ref, other_ref, total_ref):
    late = bit(16) == 1
    first, second = ordered(own_ref[...].astype(f32), other_ref[...].astype(f32), late)
    total_ref[...] = advance(first[:, :DK], second).astype(bf16)


def pair_start_kernel(rows_ref, row_ref, before_ref, own_ref, other_ref, keep_ref, send_ref):
    state = rows_ref[...].astype(f32)
    late_row = bit(16) == 1
    row = row_ref[...].astype(f32)
    state = jnp.where(late_row, advance(state, row), state)
    state = advance(state, before_ref[...].astype(f32))
    late = bit(2) == 1
    first = jnp.where(late, other_ref[...], own_ref[...]).astype(f32)
    after = advance(state, first)
    keep_ref[...] = jnp.where(late, after, state).astype(bf16)
    send_ref[...] = jnp.where(late, state, after).astype(bf16)


def finish_kernel(
    own_state, other_state, own_maps, other_maps, base_ref, gate_ref, base_in, gate_in, gain_ref,
    mine_ref, one, two, three, normed
):
    late, upper = bit(1) == 1, bit(2) == 1
    core = bit(1)
    here = lax.axis_index("head")
    own, other = own_state[...].astype(f32), other_state[...].astype(f32)
    for j, state in enumerate(ordered(own, other, upper)):
        first = jnp.where(late, other_maps[j], own_maps[j]).astype(f32)
        after = advance(state, first)
        gain = gain_ref[2 * j + core]
        for slot, start, base, gate in (
            (0, jnp.where(late, after, state), base_ref, gate_ref),
            (1, jnp.where(late, state, after), base_in, gate_in),
        ):
            heads_out = base[j] + dot(gate[j], start.astype(bf16))
            scale = lax.rsqrt(jnp.mean(heads_out * heads_out, axis=-1, keepdims=True) + EPS)
            normed[slot, :, j * DK : (j + 1) * DK] = (heads_out * scale * gain).astype(bf16)
    rows = mine_ref.shape[1]
    for s, ref in enumerate((mine_ref, one, two, three)):
        start = pl.multiple_of((here + s) % 4 * rows, rows)
        for slot in range(2):
            ref[slot] = normed[slot, pl.ds(start, rows), :]


def finish(states, maps, inner, inner_in, norm_gain):
    length = inner[0].shape[1]
    part = shape((2, length // 4, 2 * DK), bf16)
    return small_call(
        finish_kernel, [part] * 4, "finish", [pltpu.VMEM((2, length, 2 * DK), bf16)]
    )(*states, *maps, *inner, *inner_in, norm_gain.reshape(4, 1, DK))


def merge_kernel(mine_ref, one, two, three, w_hbm, keep_ref, send_ref, w_ref, sems):
    here = lax.axis_index("head")
    copies = [
        pltpu.make_async_copy(w_hbm.at[(here + 4 - s) % 4], w_ref.at[s], sems.at[s])
        for s in range(4)
    ]
    for copy in copies:
        copy.start()
    _, rows, width = mine_ref.shape
    total = None
    for s, ref in enumerate((mine_ref, one, two, three)):
        copies[s].wait()
        term = dot(ref[...].reshape(2 * rows, width), w_ref[s])
        total = term if total is None else total + term
    keep_ref[...] = total[:rows]
    send_ref[...] = total[rows:].astype(bf16)


def merge(parts, weights):
    rows = parts[0].shape[1]
    width = weights.shape[-1]
    far = pl.BlockSpec(memory_space=pltpu.HBM)
    return pl.pallas_call(
        merge_kernel,
        in_specs=whole(4) + [far],
        out_specs=whole(2),
        out_shape=[shape((rows, width), f32), shape((rows, width), bf16)],
        scratch_shapes=[pltpu.VMEM(weights.shape, bf16), pltpu.SemaphoreType.DMA((4,))],
        compiler_params=params(),
        name="merge",
    )(*parts, pltpu.with_memory_space_constraint(weights, pltpu.HBM))


def permuted(x, target):
    pairs = [(i, target(i)) for i in range(lax.axis_size("ctx"))]
    return lax.ppermute(x, "ctx", [p for p in pairs if p[1] is not None])


def swapped(x, by):
    return permuted(x, lambda i: i ^ by)


def per_device(tokens_in, w_qkv, conv_weight, beta_weight, beta_bias, norm_gain, w_out):
    peers, around = lax.axis_size("ctx"), lax.axis_size("head")
    width = w_out.shape[1]
    half = lax.dynamic_index_in_dim(w_out.reshape(2, 2, DK, width), bit(1), 1, keepdims=False)
    weights = lax.all_gather(half.reshape(2 * DK, width), "head")
    projected, edge, logits = project(tokens_in, w_qkv, beta_weight)
    edge = permuted(edge, lambda i: i + 1 if i + 1 < peers else None)
    queries, keys_t, uw, maps, send = local_maps(projected, edge, conv_weight, logits, beta_bias)
    sibling = swapped(send, 1)
    base, gate, *sent = inner_outputs(queries, keys_t, uw)
    inner_in = [swapped(x, 1) for x in sent]
    chip, send = small_call(
        chip_kernel, [MAP, MAP], "chip_map", [pltpu.VMEM((2, DK, 2 * DK), bf16)]
    )(maps, sibling)
    neighbour = swapped(send, 2)
    (pair,) = small_call(pair_kernel, [MAP], "pair_map")(chip, neighbour)
    four, near = small_call(near_kernel, [MAP, MAP], "near_map")(pair, swapped(pair, 4))
    row, before = small_call(far_kernel, [MAP, MAP], "far_map")(four, swapped(four, 12), near)
    other_row = swapped(row, 16)
    (two_rows,) = small_call(rows_kernel, [STATE], "rows_state")(row, other_row)
    rows = permuted(two_rows, lambda i: i ^ 48 if i < 32 else None)
    state, send = small_call(pair_start_kernel, [STATE, STATE], "pair_start")(
        rows, other_row, before, chip, neighbour
    )
    back = swapped(send, 2)
    mine, *parts = finish((state, back), (maps, sibling), (base, gate), inner_in, norm_gain)
    moved = [
        lax.ppermute(part, "head", [(i, (i + s + 1) % around) for i in range(around)])
        for s, part in enumerate(parts)
    ]
    keep, send = merge([mine, *moved], weights)
    return (keep + swapped(send, 1).astype(f32)).astype(bf16)


def solution(mesh):
    return jax.shard_map(
        per_device,
        mesh=mesh,
        in_specs=(
            P("ctx", None),
            P(None, None, "head"),
            P(None, None, "head"),
            P("head", None),
            P("head"),
            P("head"),
            P("head", None),
        ),
        out_specs=P(("ctx", "head"), None),
        check_vma=False,
    )
```

```python
import jax
import jax.numpy as jnp
from jax import lax
from jax.experimental import pallas as pl
from jax.experimental.pallas import tpu as pltpu
from jax.sharding import PartitionSpec as P

DK = 128
BLOCK = 128
WIDTH = 2 * BLOCK
EDGE = 16
EPS = 1e-06
FAN = 4

f32 = jnp.float32
bf16 = jnp.bfloat16


def dot(a, b):
    return lax.dot_general(a, b, (((1,), (0,)), ((), ())), preferred_element_type=f32)


def dot_t(a, b):
    return lax.dot_general(a, b, (((1,), (1,)), ((), ())), preferred_element_type=f32)


def params(megabytes=48):
    return pltpu.CompilerParams(vmem_limit_bytes=megabytes << 20)


def whole(count):
    return [pl.BlockSpec(memory_space=pltpu.VMEM)] * count


def shape(dims, kind):
    return jax.ShapeDtypeStruct(dims, kind)


def project_kernel(
    tokens_hbm, w_hbm, beta_w_hbm, out_ref, edge_ref, logits_ref,
    tokens_ref, w_ref, beta_w_ref, small_sems, w_sems
):
    length = tokens_ref.shape[0]
    first = pltpu.make_async_copy(tokens_hbm, tokens_ref, small_sems.at[0])
    last = pltpu.make_async_copy(beta_w_hbm, beta_w_ref, small_sems.at[1])
    copies = [pltpu.make_async_copy(w_hbm.at[s], w_ref.at[s], w_sems.at[s]) for s in range(3)]
    first.start()
    last.start()
    copies[0].start()
    copies[1].start()
    last.wait()
    first.wait()
    logits_ref[...] = dot_t(tokens_ref[...], beta_w_ref[...])
    for s in range(3):
        copies[s].wait()
        if s == 0:
            copies[2].start()
        result = dot(tokens_ref[...], w_ref[s]).astype(bf16)
        out_ref[s] = result
        edge_ref[s] = result[length - EDGE :]


def project(tokens, w_qkv, beta_weight):
    length, depth = tokens.shape
    columns = w_qkv.shape[2]
    heads = beta_weight.shape[0]
    operands = [
        pltpu.with_memory_space_constraint(x, pltpu.HBM) for x in (tokens, w_qkv, beta_weight)
    ]
    return pl.pallas_call(
        project_kernel,
        in_specs=[pl.BlockSpec(memory_space=pltpu.HBM)] * 3,
        out_specs=whole(3),
        out_shape=[
            shape((3, length, columns), bf16),
            shape((3, EDGE, columns), bf16),
            shape((length, heads), f32),
        ],
        scratch_shapes=[
            pltpu.VMEM(tokens.shape, bf16),
            pltpu.VMEM(w_qkv.shape, bf16),
            pltpu.VMEM(beta_weight.shape, bf16),
            pltpu.SemaphoreType.DMA((2,)),
            pltpu.SemaphoreType.DMA((3,)),
        ],
        compiler_params=params(),
        name="project",
    )(*operands)


def grid_index(rows, columns):
    row = lax.broadcasted_iota(jnp.int32, (rows, columns), 0)
    column = lax.broadcasted_iota(jnp.int32, (rows, columns), 1)
    return row, column


def on_diagonal(pair, left):
    zero = jnp.zeros_like(pair)
    return jnp.concatenate([jnp.where(left, pair, zero), jnp.where(left, zero, pair)], axis=0)


def inverse_pairs(systems):
    row, wide = grid_index(BLOCK, 2 * BLOCK)
    column = wide % BLOCK
    left = wide < BLOCK
    eye = jnp.where(row == column, 1.0, 0.0).astype(f32)

    def below(size):
        same = (row // (2 * size)) == (column // (2 * size))
        return same & ((row % (2 * size)) >= size) & ((column % (2 * size)) < size)

    found = [eye - jnp.where(below(1), system, 0.0) for system in systems]
    size = 2
    while size < BLOCK:
        mask = below(size)
        steps = [jnp.where(mask, system, 0.0).astype(bf16) for system in systems]
        small = [x.astype(bf16) for x in found]
        half = [dot(x, on_diagonal(n, left)).astype(bf16) for x, n in zip(small, steps)]
        found = [
            x - dot(y, on_diagonal(b, left)) for x, y, b in zip(found, half, small)
        ]
        size *= 2
    small = [x.astype(bf16) for x in found]
    high = [system.astype(bf16) for system in systems]
    low = [(system - h.astype(f32)).astype(bf16) for system, h in zip(systems, high)]
    rest = [
        (eye - x.astype(f32)) - dot(x, on_diagonal(h, left)) - dot(x, on_diagonal(l, left))
        for x, h, l in zip(small, high, low)
    ]
    fixed = [
        x.astype(f32) + dot(r.astype(bf16), on_diagonal(x, left)) for x, r in zip(small, rest)
    ]
    return [x - eye for x in fixed]


def local_kernel(
    proj_ref, edge_ref, conv_ref, logits_ref, bias_ref,
    queries_ref, keys_t_ref, uw_ref, keep_ref, send_ref, padded, maps
):
    length = proj_ref.shape[1]
    heads = logits_ref.shape[1]
    betas = 1.0 / (1.0 + jnp.exp(-(logits_ref[...] + bias_ref[...])))
    core = lax.axis_index("ctx") % 2
    first = lax.axis_index("ctx") == 0
    for s in range(3):
        edge = edge_ref[s].astype(f32)
        padded[s, :EDGE] = jnp.where(first, jnp.zeros_like(edge), edge)
        padded[s, EDGE:] = proj_ref[s].astype(f32)
    row, column = grid_index(length, length)
    strict = row > column
    systems, corners, right, keys_t = [], [], [], []
    for h in range(heads):
        lanes = slice(h * DK, (h + 1) * DK)
        mixed = []
        for s in range(3):
            total = jnp.zeros((length, DK), f32)
            for j in range(4):
                start = EDGE - 3 + j
                total = total + conv_ref[s, j : j + 1, lanes] * padded[s, start : start + length, lanes]
            mixed.append(total / (1.0 + jnp.exp(-total)))
        query, key, value = mixed
        query = query * lax.rsqrt(jnp.sum(query * query, axis=-1, keepdims=True) + EPS)
        key = key * lax.rsqrt(jnp.sum(key * key, axis=-1, keepdims=True) + EPS)
        queries_ref[h] = query.astype(bf16)
        small = key.astype(bf16)
        small_t = key.T.astype(bf16)
        keys_t_ref[h] = small_t
        keys_t.append(small_t)
        beta = betas[:, h : h + 1]
        system = jnp.where(strict, beta * dot(small, small_t), 0.0)
        systems.append(jnp.concatenate([system[:BLOCK, :BLOCK], system[BLOCK:, BLOCK:]], axis=1))
        corners.append(system[BLOCK:, :BLOCK].astype(bf16))
        right.append(beta * jnp.concatenate([value, small.astype(f32)], axis=1))
    lowers = [x.astype(bf16) for x in inverse_pairs(systems)]
    firsts = [
        r[:BLOCK] + dot(low[:, :BLOCK], r[:BLOCK].astype(bf16)) for low, r in zip(lowers, right)
    ]
    seconds = [
        r[BLOCK:] - dot(corner, first.astype(bf16))
        for corner, r, first in zip(corners, right, firsts)
    ]
    seconds = [r + dot(low[:, BLOCK:], r.astype(bf16)) for low, r in zip(lowers, seconds)]
    for h in range(heads):
        uw = jnp.concatenate([firsts[h], seconds[h]], axis=0).astype(bf16)
        uw_ref[h] = uw
        maps[h] = dot(keys_t[h], uw).astype(bf16)
    for j in range(heads // 2):
        keep_ref[j] = maps[2 * j + core]
        send_ref[j] = maps[2 * j + 1 - core]


def local_maps(projected, edge, conv_weight, logits, beta_bias):
    length, columns = projected.shape[1:]
    heads = logits.shape[1]
    two = shape((heads // 2, DK, 2 * DK), bf16)
    return pl.pallas_call(
        local_kernel,
        in_specs=whole(5),
        out_specs=whole(5),
        out_shape=[
            shape((heads, length, DK), bf16),
            shape((heads, DK, length), bf16),
            shape((heads, length, 2 * DK), bf16),
            two, two,
        ],
        scratch_shapes=[
            pltpu.VMEM((3, EDGE + length, columns), f32),
            pltpu.VMEM((heads, DK, 2 * DK), bf16),
        ],
        compiler_params=params(),
        name="local_maps",
    )(projected, edge, conv_weight, logits, beta_bias[None, :])


def inner_kernel(queries_ref, keys_t_ref, uw_ref, base_ref, gate_ref, base_out, gate_out):
    length = queries_ref.shape[1]
    row, column = grid_index(length, length)
    core = bit(1)
    for j in range(2):
        for h, base, gate in (
            (2 * j + core, base_ref, gate_ref),
            (2 * j + 1 - core, base_out, gate_out),
        ):
            query = queries_ref[h]
            scores = jnp.where(row >= column, dot(query, keys_t_ref[h]), 0.0).astype(bf16)
            both = dot(scores, uw_ref[h])
            base[j] = both[:, :DK]
            gate[j] = (query.astype(f32) - both[:, DK:]).astype(bf16)


def inner_outputs(queries, keys_t, uw):
    heads, length, _ = queries.shape
    outs = [shape((2, length, DK), f32), shape((2, length, DK), bf16)]
    return pl.pallas_call(
        inner_kernel,
        in_specs=whole(3),
        out_specs=whole(4),
        out_shape=outs + outs,
        compiler_params=params(),
        cost_estimate=pl.CostEstimate(
            flops=2 * heads * length * length * 3 * DK, bytes_accessed=2 << 20, transcendentals=0
        ),
        name="inner_outputs",
    )(queries, keys_t, uw)


def then(earlier, later):
    return earlier + later - dot(later[:, DK:].astype(bf16), earlier.astype(bf16))


def advance(state, later):
    return state + later[:, :DK] - dot(later[:, DK:].astype(bf16), state.astype(bf16))


MAP = shape((DK, 2 * DK), bf16)
STATE = shape((DK, DK), bf16)


def small_call(kernel, outs, name, scratch=()):
    return pl.pallas_call(
        kernel,
        out_specs=whole(len(outs)),
        out_shape=list(outs),
        scratch_shapes=list(scratch),
        compiler_params=params(),
        name=name,
    )


def ordered(mine, other, late):
    return jnp.where(late, other, mine), jnp.where(late, mine, other)


def bit(position):
    return (lax.axis_index("ctx") // position) % 2


def chip_kernel(own_ref, other_ref, keep_ref, send_ref, kept):
    late = bit(1) == 1
    for j in range(2):
        first, second = ordered(own_ref[j].astype(f32), other_ref[j].astype(f32), late)
        kept[j] = then(first, second).astype(bf16)
    keep_ref[...] = kept[bit(2)]
    send_ref[...] = kept[1 - bit(2)]


def four_kernel(own_ref, pair_ref, across_ref, diagonal_ref, total_ref, before_ref):
    upper, late = bit(2) == 1, bit(4) == 1
    own, pair, across, diagonal = (
        ref[...].astype(f32) for ref in (own_ref, pair_ref, across_ref, diagonal_ref)
    )
    mine = then(*ordered(own, pair, upper))
    other = then(*ordered(across, diagonal, upper))
    total_ref[...] = then(*ordered(mine, other, late)).astype(bf16)
    before_ref[...] = jnp.where(late, other, jnp.zeros_like(other)).astype(bf16)


def far_kernel(own_ref, other_ref, near_ref, total_ref, before_ref):
    late = bit(8) == 1
    own, other = own_ref[...].astype(f32), other_ref[...].astype(f32)
    near = near_ref[...].astype(f32)
    first, second = ordered(own, other, late)
    total_ref[...] = then(first, second).astype(bf16)
    before_ref[...] = jnp.where(late, then(other, near), near).astype(bf16)


def rows_kernel(own_ref, other_ref, total_ref):
    late = bit(16) == 1
    first, second = ordered(own_ref[...].astype(f32), other_ref[...].astype(f32), late)
    total_ref[...] = advance(first[:, :DK], second).astype(bf16)


def pair_start_kernel(rows_ref, row_ref, before_ref, own_ref, other_ref, keep_ref, send_ref):
    state = rows_ref[...].astype(f32)
    state = jnp.where(bit(32) == 1, state, jnp.zeros_like(state))
    late_row = bit(16) == 1
    row = row_ref[...].astype(f32)
    state = jnp.where(late_row, advance(state, row), state)
    state = advance(state, before_ref[...].astype(f32))
    late = bit(2) == 1
    first = jnp.where(late, other_ref[...], own_ref[...]).astype(f32)
    after = advance(state, first)
    keep_ref[...] = jnp.where(late, after, state).astype(bf16)
    send_ref[...] = jnp.where(late, state, after).astype(bf16)


def finish_kernel(
    own_state, other_state, own_maps, other_maps, base_ref, gate_ref, base_in, gate_in, gain_ref,
    mine_ref, one, two, three, normed
):
    late, upper = bit(1) == 1, bit(2) == 1
    core = bit(1)
    here = lax.axis_index("head")
    own, other = own_state[...].astype(f32), other_state[...].astype(f32)
    for j, state in enumerate(ordered(own, other, upper)):
        first = jnp.where(late, other_maps[j], own_maps[j]).astype(f32)
        after = advance(state, first)
        gain = gain_ref[2 * j + core]
        for slot, start, base, gate in (
            (0, jnp.where(late, after, state), base_ref, gate_ref),
            (1, jnp.where(late, state, after), base_in, gate_in),
        ):
            heads_out = base[j] + dot(gate[j], start.astype(bf16))
            scale = lax.rsqrt(jnp.mean(heads_out * heads_out, axis=-1, keepdims=True) + EPS)
            normed[slot, :, j * DK : (j + 1) * DK] = (heads_out * scale * gain).astype(bf16)
    rows = mine_ref.shape[1]
    for s, ref in enumerate((mine_ref, one, two, three)):
        start = pl.multiple_of((here + s) % 4 * rows, rows)
        for slot in range(2):
            ref[slot] = normed[slot, pl.ds(start, rows), :]


def finish(states, maps, inner, inner_in, norm_gain):
    length = inner[0].shape[1]
    part = shape((2, length // 4, 2 * DK), bf16)
    return small_call(
        finish_kernel, [part] * 4, "finish", [pltpu.VMEM((2, length, 2 * DK), bf16)]
    )(*states, *maps, *inner, *inner_in, norm_gain.reshape(4, 1, DK))


def rows_kernel_of(w_hbm, out_ref, sems):
    copies = [
        pltpu.make_async_copy(
            w_hbm.at[pl.ds(pl.multiple_of((2 * j + bit(1)) * DK, DK), DK)], out_ref.at[j], sems.at[j]
        )
        for j in range(2)
    ]
    for copy in copies:
        copy.start()
    for copy in copies:
        copy.wait()


def own_rows(w_out):
    return pl.pallas_call(
        rows_kernel_of,
        in_specs=[pl.BlockSpec(memory_space=pltpu.HBM)],
        out_specs=pl.BlockSpec(memory_space=pltpu.VMEM),
        out_shape=shape((2, DK, w_out.shape[1]), bf16),
        scratch_shapes=[pltpu.SemaphoreType.DMA((2,))],
        compiler_params=params(),
        name="own_rows",
    )(pltpu.with_memory_space_constraint(w_out, pltpu.HBM))


def merge_kernel(*refs):
    parts, weights, (keep_ref, send_ref) = refs[:4], refs[4:8], refs[8:]
    _, rows, width = parts[0].shape
    total = None
    for ref, weight in zip(parts, weights):
        term = dot(ref[...].reshape(2 * rows, width), weight[...].reshape(width, -1))
        total = term if total is None else total + term
    keep_ref[...] = total[:rows]
    send_ref[...] = total[rows:].astype(bf16)


def merge(parts, weights):
    rows, width = parts[0].shape[1], weights[0].shape[-1]
    return small_call(
        merge_kernel, [shape((rows, width), f32), shape((rows, width), bf16)], "merge"
    )(*parts, *weights)


def swapped(x, by):
    return lax.ppermute(x, "ctx", [(i, i ^ by) for i in range(lax.axis_size("ctx"))])


def turned(x, axis, by):
    count = lax.axis_size(axis)
    return lax.ppermute(x, axis, [(i, (i + by) % count) for i in range(count)])


def per_device(tokens_in, w_qkv, conv_weight, beta_weight, beta_bias, norm_gain, w_out):
    w_own = own_rows(w_out)
    w_one, w_three, w_two = (turned(w_own, "head", s) for s in (1, 3, 2))
    projected, edge, logits = project(tokens_in, w_qkv, beta_weight)
    edge = turned(edge, "ctx", 1)
    queries, keys_t, uw, maps, send = local_maps(projected, edge, conv_weight, logits, beta_bias)
    sibling = swapped(send, 1)
    base, gate, *sent = inner_outputs(queries, keys_t, uw)
    inner_in = [swapped(x, 1) for x in sent]
    chip, send = small_call(
        chip_kernel, [MAP, MAP], "chip_map", [pltpu.VMEM((2, DK, 2 * DK), bf16)]
    )(maps, sibling)
    pair, across, diagonal = swapped(send, 2), swapped(chip, 4), swapped(send, 6)
    four, near = small_call(four_kernel, [MAP, MAP], "four_map")(chip, pair, across, diagonal)
    row, before = small_call(far_kernel, [MAP, MAP], "far_map")(four, swapped(four, 12), near)
    other_row = swapped(row, 16)
    (two_rows,) = small_call(rows_kernel, [STATE], "rows_state")(row, other_row)
    rows = swapped(two_rows, 48)
    state, send = small_call(pair_start_kernel, [STATE, STATE], "pair_start")(
        rows, other_row, before, chip, pair
    )
    back = swapped(send, 2)
    mine, one, two, three = finish(
        (state, back), (maps, sibling), (base, gate), inner_in, norm_gain
    )
    one, three, two = turned(one, "head", 1), turned(three, "head", 3), turned(two, "head", 2)
    keep, send = merge([mine, one, two, three], [w_own, w_one, w_two, w_three])
    return (keep + swapped(send, 1).astype(f32)).astype(bf16)


def solution(mesh):
    return jax.shard_map(
        per_device,
        mesh=mesh,
        in_specs=(
            P("ctx", None),
            P(None, None, "head"),
            P(None, None, "head"),
            P("head", None),
            P("head"),
            P("head"),
            P("head", None),
        ),
        out_specs=P(("ctx", "head"), None),
        check_vma=False,
    )
```

```python
import jax
import jax.numpy as jnp
from jax import lax
from jax.experimental import pallas as pl
from jax.experimental.pallas import tpu as pltpu
from jax.sharding import PartitionSpec as P

DK = 128
BLOCK = 128
WIDTH = 2 * BLOCK
EDGE = 16
EPS = 1e-06
FAN = 4

f32 = jnp.float32
bf16 = jnp.bfloat16


def dot(a, b):
    return lax.dot_general(a, b, (((1,), (0,)), ((), ())), preferred_element_type=f32)


def dot_t(a, b):
    return lax.dot_general(a, b, (((1,), (1,)), ((), ())), preferred_element_type=f32)


def params(megabytes=48):
    return pltpu.CompilerParams(vmem_limit_bytes=megabytes << 20)


def whole(count):
    return [pl.BlockSpec(memory_space=pltpu.VMEM)] * count


def shape(dims, kind):
    return jax.ShapeDtypeStruct(dims, kind)


def project_kernel(
    tokens_hbm, w_hbm, beta_w_hbm, w_out_hbm, out_ref, edge_ref, logits_ref, w_own_ref,
    tokens_ref, w_ref, beta_w_ref, small_sems, w_sems
):
    length = tokens_ref.shape[0]
    first = pltpu.make_async_copy(tokens_hbm, tokens_ref, small_sems.at[0])
    last = pltpu.make_async_copy(beta_w_hbm, beta_w_ref, small_sems.at[1])
    copies = [pltpu.make_async_copy(w_hbm.at[s], w_ref.at[s], w_sems.at[s]) for s in range(3)]
    rows = [
        pltpu.make_async_copy(
            w_out_hbm.at[pl.ds(pl.multiple_of((2 * j + bit(1)) * DK, DK), DK)],
            w_own_ref.at[j],
            small_sems.at[2 + j],
        )
        for j in range(2)
    ]
    first.start()
    last.start()
    copies[0].start()
    copies[1].start()
    last.wait()
    first.wait()
    logits_ref[...] = dot_t(tokens_ref[...], beta_w_ref[...])
    for s in range(3):
        copies[s].wait()
        if s == 0:
            copies[2].start()
        if s == 1:
            rows[0].start()
            rows[1].start()
        result = dot(tokens_ref[...], w_ref[s]).astype(bf16)
        out_ref[s] = result
        edge_ref[s] = result[length - EDGE :]
    rows[0].wait()
    rows[1].wait()


def project(tokens, w_qkv, beta_weight, w_out):
    length, depth = tokens.shape
    columns = w_qkv.shape[2]
    heads = beta_weight.shape[0]
    operands = [
        pltpu.with_memory_space_constraint(x, pltpu.HBM) for x in (tokens, w_qkv, beta_weight, w_out)
    ]
    return pl.pallas_call(
        project_kernel,
        in_specs=[pl.BlockSpec(memory_space=pltpu.HBM)] * 4,
        out_specs=whole(4),
        out_shape=[
            shape((3, length, columns), bf16),
            shape((3, EDGE, columns), bf16),
            shape((length, heads), f32),
            shape((2, DK, w_out.shape[1]), bf16),
        ],
        scratch_shapes=[
            pltpu.VMEM(tokens.shape, bf16),
            pltpu.VMEM(w_qkv.shape, bf16),
            pltpu.VMEM(beta_weight.shape, bf16),
            pltpu.SemaphoreType.DMA((4,)),
            pltpu.SemaphoreType.DMA((3,)),
        ],
        compiler_params=params(),
        name="project",
    )(*operands)


def grid_index(rows, columns):
    row = lax.broadcasted_iota(jnp.int32, (rows, columns), 0)
    column = lax.broadcasted_iota(jnp.int32, (rows, columns), 1)
    return row, column


def on_diagonal(pair, left):
    zero = jnp.zeros_like(pair)
    return jnp.concatenate([jnp.where(left, pair, zero), jnp.where(left, zero, pair)], axis=0)


def inverse_pairs(systems):
    row, wide = grid_index(BLOCK, 2 * BLOCK)
    column = wide % BLOCK
    left = wide < BLOCK
    eye = jnp.where(row == column, 1.0, 0.0).astype(f32)

    def below(size):
        same = (row // (2 * size)) == (column // (2 * size))
        return same & ((row % (2 * size)) >= size) & ((column % (2 * size)) < size)

    found = [eye - jnp.where(below(1), system, 0.0) for system in systems]
    size = 2
    while size < BLOCK:
        mask = below(size)
        steps = [jnp.where(mask, system, 0.0).astype(bf16) for system in systems]
        small = [x.astype(bf16) for x in found]
        half = [dot(x, on_diagonal(n, left)).astype(bf16) for x, n in zip(small, steps)]
        found = [
            x - dot(y, on_diagonal(b, left)) for x, y, b in zip(found, half, small)
        ]
        size *= 2
    small = [x.astype(bf16) for x in found]
    high = [system.astype(bf16) for system in systems]
    low = [(system - h.astype(f32)).astype(bf16) for system, h in zip(systems, high)]
    rest = [
        (eye - x.astype(f32)) - dot(x, on_diagonal(h, left)) - dot(x, on_diagonal(l, left))
        for x, h, l in zip(small, high, low)
    ]
    fixed = [
        x.astype(f32) + dot(r.astype(bf16), on_diagonal(x, left)) for x, r in zip(small, rest)
    ]
    return [x - eye for x in fixed]


def local_kernel(
    proj_ref, edge_ref, conv_ref, logits_ref, bias_ref,
    queries_ref, keys_t_ref, uw_ref, keep_ref, send_ref, padded, maps
):
    length = proj_ref.shape[1]
    heads = logits_ref.shape[1]
    betas = 1.0 / (1.0 + jnp.exp(-(logits_ref[...] + bias_ref[...])))
    core = lax.axis_index("ctx") % 2
    first = lax.axis_index("ctx") == 0
    for s in range(3):
        edge = edge_ref[s].astype(f32)
        padded[s, :EDGE] = jnp.where(first, jnp.zeros_like(edge), edge)
        padded[s, EDGE:] = proj_ref[s].astype(f32)
    row, column = grid_index(length, length)
    strict = row > column
    systems, corners, right, keys_t = [], [], [], []
    for h in range(heads):
        lanes = slice(h * DK, (h + 1) * DK)
        mixed = []
        for s in range(3):
            total = jnp.zeros((length, DK), f32)
            for j in range(4):
                start = EDGE - 3 + j
                total = total + conv_ref[s, j : j + 1, lanes] * padded[s, start : start + length, lanes]
            mixed.append(total / (1.0 + jnp.exp(-total)))
        query, key, value = mixed
        query = query * lax.rsqrt(jnp.sum(query * query, axis=-1, keepdims=True) + EPS)
        key = key * lax.rsqrt(jnp.sum(key * key, axis=-1, keepdims=True) + EPS)
        queries_ref[h] = query.astype(bf16)
        small = key.astype(bf16)
        small_t = key.T.astype(bf16)
        keys_t_ref[h] = small_t
        keys_t.append(small_t)
        beta = betas[:, h : h + 1]
        system = jnp.where(strict, beta * dot(small, small_t), 0.0)
        systems.append(jnp.concatenate([system[:BLOCK, :BLOCK], system[BLOCK:, BLOCK:]], axis=1))
        corners.append(system[BLOCK:, :BLOCK].astype(bf16))
        right.append(beta * jnp.concatenate([value, small.astype(f32)], axis=1))
    lowers = [x.astype(bf16) for x in inverse_pairs(systems)]
    firsts = [
        r[:BLOCK] + dot(low[:, :BLOCK], r[:BLOCK].astype(bf16)) for low, r in zip(lowers, right)
    ]
    seconds = [
        r[BLOCK:] - dot(corner, first.astype(bf16))
        for corner, r, first in zip(corners, right, firsts)
    ]
    seconds = [r + dot(low[:, BLOCK:], r.astype(bf16)) for low, r in zip(lowers, seconds)]
    for h in range(heads):
        uw = jnp.concatenate([firsts[h], seconds[h]], axis=0).astype(bf16)
        uw_ref[h] = uw
        maps[h] = dot(keys_t[h], uw).astype(bf16)
    for j in range(heads // 2):
        keep_ref[j] = maps[2 * j + core]
        send_ref[j] = maps[2 * j + 1 - core]


def local_maps(projected, edge, conv_weight, logits, beta_bias):
    length, columns = projected.shape[1:]
    heads = logits.shape[1]
    two = shape((heads // 2, DK, 2 * DK), bf16)
    return pl.pallas_call(
        local_kernel,
        in_specs=whole(5),
        out_specs=whole(5),
        out_shape=[
            shape((heads, length, DK), bf16),
            shape((heads, DK, length), bf16),
            shape((heads, length, 2 * DK), bf16),
            two, two,
        ],
        scratch_shapes=[
            pltpu.VMEM((3, EDGE + length, columns), f32),
            pltpu.VMEM((heads, DK, 2 * DK), bf16),
        ],
        compiler_params=params(),
        name="local_maps",
    )(projected, edge, conv_weight, logits, beta_bias[None, :])


def inner_kernel(queries_ref, keys_t_ref, uw_ref, base_ref, gate_ref, both_out):
    length = queries_ref.shape[1]
    row, column = grid_index(length, length)
    core = bit(1)
    for j in range(2):
        for h, base, gate in (
            (2 * j + core, base_ref.at[j], gate_ref.at[j]),
            (2 * j + 1 - core, both_out.at[0, j], both_out.at[1, j]),
        ):
            query = queries_ref[h]
            scores = jnp.where(row >= column, dot(query, keys_t_ref[h]), 0.0).astype(bf16)
            both = dot(scores, uw_ref[h])
            base[...] = both[:, :DK].astype(base.dtype)
            gate[...] = (query.astype(f32) - both[:, DK:]).astype(bf16)


def inner_outputs(queries, keys_t, uw):
    heads, length, _ = queries.shape
    outs = [shape((2, length, DK), f32), shape((2, length, DK), bf16)]
    outs.append(shape((2, 2, length, DK), bf16))
    return pl.pallas_call(
        inner_kernel,
        in_specs=whole(3),
        out_specs=whole(3),
        out_shape=outs,
        compiler_params=params(),
        cost_estimate=pl.CostEstimate(
            flops=2 * heads * length * length * 3 * DK, bytes_accessed=2 << 20, transcendentals=0
        ),
        name="inner_outputs",
    )(queries, keys_t, uw)


def then(earlier, later):
    return earlier + later - dot(later[:, DK:].astype(bf16), earlier.astype(bf16))


def advance(state, later):
    return state + later[:, :DK] - dot(later[:, DK:].astype(bf16), state.astype(bf16))


MAP = shape((DK, 2 * DK), bf16)
STATE = shape((DK, DK), bf16)


def small_call(kernel, outs, name, scratch=()):
    return pl.pallas_call(
        kernel,
        out_specs=whole(len(outs)),
        out_shape=list(outs),
        scratch_shapes=list(scratch),
        compiler_params=params(),
        name=name,
    )


def ordered(mine, other, late):
    return jnp.where(late, other, mine), jnp.where(late, mine, other)


def bit(position):
    return (lax.axis_index("ctx") // position) % 2


def chip_kernel(own_ref, other_ref, keep_ref, send_ref, kept):
    late = bit(1) == 1
    for j in range(2):
        first, second = ordered(own_ref[j].astype(f32), other_ref[j].astype(f32), late)
        kept[j] = then(first, second).astype(bf16)
    keep_ref[...] = kept[bit(2)]
    send_ref[...] = kept[1 - bit(2)]


def four_kernel(own_ref, pair_ref, across_ref, diagonal_ref, total_ref, before_ref):
    upper, late = bit(2) == 1, bit(4) == 1
    own, pair, across, diagonal = (
        ref[...].astype(f32) for ref in (own_ref, pair_ref, across_ref, diagonal_ref)
    )
    mine = then(*ordered(own, pair, upper))
    other = then(*ordered(across, diagonal, upper))
    total_ref[...] = then(*ordered(mine, other, late)).astype(bf16)
    before_ref[...] = jnp.where(late, other, jnp.zeros_like(other)).astype(bf16)


def far_kernel(own_ref, other_ref, near_ref, total_ref, before_ref):
    late = bit(8) == 1
    own, other = own_ref[...].astype(f32), other_ref[...].astype(f32)
    near = near_ref[...].astype(f32)
    first, second = ordered(own, other, late)
    total_ref[...] = then(first, second).astype(bf16)
    before_ref[...] = jnp.where(late, then(other, near), near).astype(bf16)


def rows_kernel(own_ref, other_ref, total_ref):
    late = bit(16) == 1
    first, second = ordered(own_ref[...].astype(f32), other_ref[...].astype(f32), late)
    total_ref[...] = advance(first[:, :DK], second).astype(bf16)


def pair_start_kernel(rows_ref, row_ref, before_ref, own_ref, other_ref, keep_ref, send_ref):
    state = rows_ref[...].astype(f32)
    state = jnp.where(bit(32) == 1, state, jnp.zeros_like(state))
    late_row = bit(16) == 1
    row = row_ref[...].astype(f32)
    state = jnp.where(late_row, advance(state, row), state)
    state = advance(state, before_ref[...].astype(f32))
    late = bit(2) == 1
    first = jnp.where(late, other_ref[...], own_ref[...]).astype(f32)
    after = advance(state, first)
    keep_ref[...] = jnp.where(late, after, state).astype(bf16)
    send_ref[...] = jnp.where(late, state, after).astype(bf16)


def finish_kernel(
    own_state, other_state, own_maps, other_maps, base_ref, gate_ref, both_in, gain_ref,
    mine_ref, one, two, three, normed
):
    late, upper = bit(1) == 1, bit(2) == 1
    core = bit(1)
    here = lax.axis_index("head")
    own, other = own_state[...].astype(f32), other_state[...].astype(f32)
    for j, state in enumerate(ordered(own, other, upper)):
        first = jnp.where(late, other_maps[j], own_maps[j]).astype(f32)
        after = advance(state, first)
        gain = gain_ref[2 * j + core]
        for slot, start, base, gate in (
            (0, jnp.where(late, after, state), base_ref.at[j], gate_ref.at[j]),
            (1, jnp.where(late, state, after), both_in.at[0, j], both_in.at[1, j]),
        ):
            heads_out = base[...].astype(f32) + dot(gate[...], start.astype(bf16))
            scale = lax.rsqrt(jnp.mean(heads_out * heads_out, axis=-1, keepdims=True) + EPS)
            normed[slot, :, j * DK : (j + 1) * DK] = (heads_out * scale * gain).astype(bf16)
    rows = mine_ref.shape[1]
    for s, ref in enumerate((mine_ref, one, two, three)):
        start = pl.multiple_of((here + s) % 4 * rows, rows)
        for slot in range(2):
            ref[slot] = normed[slot, pl.ds(start, rows), :]


def finish(states, maps, inner, inner_in, norm_gain):
    length = inner[0].shape[1]
    part = shape((2, length // 4, 2 * DK), bf16)
    return small_call(
        finish_kernel, [part] * 4, "finish", [pltpu.VMEM((2, length, 2 * DK), bf16)]
    )(*states, *maps, *inner, inner_in, norm_gain.reshape(4, 1, DK))


def merge_kernel(*refs):
    parts, weights, (keep_ref, send_ref) = refs[:4], refs[4:8], refs[8:]
    _, rows, width = parts[0].shape
    total = None
    for ref, weight in zip(parts, weights):
        term = dot(ref[...].reshape(2 * rows, width), weight[...].reshape(width, -1))
        total = term if total is None else total + term
    keep_ref[...] = total[:rows]
    send_ref[...] = total[rows:].astype(bf16)


def merge(parts, weights):
    rows, width = parts[0].shape[1], weights[0].shape[-1]
    return small_call(
        merge_kernel, [shape((rows, width), f32), shape((rows, width), bf16)], "merge"
    )(*parts, *weights)


def swapped(x, by):
    return lax.ppermute(x, "ctx", [(i, i ^ by) for i in range(lax.axis_size("ctx"))])


def turned(x, axis, by):
    count = lax.axis_size(axis)
    return lax.ppermute(x, axis, [(i, (i + by) % count) for i in range(count)])


def per_device(tokens_in, w_qkv, conv_weight, beta_weight, beta_bias, norm_gain, w_out):
    projected, edge, logits, w_own = project(tokens_in, w_qkv, beta_weight, w_out)
    edge = turned(edge, "ctx", 1)
    w_one, w_three = turned(w_own, "head", 1), turned(w_own, "head", 3)
    queries, keys_t, uw, maps, send = local_maps(projected, edge, conv_weight, logits, beta_bias)
    sibling = swapped(send, 1)
    chip, send = small_call(
        chip_kernel, [MAP, MAP], "chip_map", [pltpu.VMEM((2, DK, 2 * DK), bf16)]
    )(maps, sibling)
    pair, across, diagonal = swapped(send, 2), swapped(chip, 4), swapped(send, 6)
    four, near = small_call(four_kernel, [MAP, MAP], "four_map")(chip, pair, across, diagonal)
    near, w_own, w_one, w_three = lax.optimization_barrier((near, w_own, w_one, w_three))
    w_two = turned(w_own, "head", 2)
    row, before = small_call(far_kernel, [MAP, MAP], "far_map")(four, swapped(four, 12), near)
    other_row = swapped(row, 16)
    before, queries = lax.optimization_barrier((before, queries))
    base, gate, both = inner_outputs(queries, keys_t, uw)
    inner_in = swapped(both, 1)
    (two_rows,) = small_call(rows_kernel, [STATE], "rows_state")(row, other_row)
    rows = swapped(two_rows, 48)
    state, send = small_call(pair_start_kernel, [STATE, STATE], "pair_start")(
        rows, other_row, before, chip, pair
    )
    back = swapped(send, 2)
    mine, one, two, three = finish(
        (state, back), (maps, sibling), (base, gate), inner_in, norm_gain
    )
    one, three, two = turned(one, "head", 1), turned(three, "head", 3), turned(two, "head", 2)
    keep, send = merge([mine, one, two, three], [w_own, w_one, w_two, w_three])
    return (keep + swapped(send, 1).astype(f32)).astype(bf16)


def solution(mesh):
    return jax.shard_map(
        per_device,
        mesh=mesh,
        in_specs=(
            P("ctx", None),
            P(None, None, "head"),
            P(None, None, "head"),
            P("head", None),
            P("head"),
            P("head"),
            P("head", None),
        ),
        out_specs=P(("ctx", "head"), None),
        check_vma=False,
    )
```

```python
import jax
import jax.numpy as jnp
from jax import lax
from jax.experimental import pallas as pl
from jax.experimental.pallas import tpu as pltpu
from jax.sharding import PartitionSpec as P

DK = 128
BLOCK = 128
WIDTH = 2 * BLOCK
EDGE = 8
EPS = 1e-06
FAN = 4

f32 = jnp.float32
bf16 = jnp.bfloat16


def dot(a, b):
    return lax.dot_general(a, b, (((1,), (0,)), ((), ())), preferred_element_type=f32)


def dot_t(a, b):
    return lax.dot_general(a, b, (((1,), (1,)), ((), ())), preferred_element_type=f32)


def params(megabytes=24):
    return pltpu.CompilerParams(vmem_limit_bytes=megabytes << 20)


def whole(count):
    return [pl.BlockSpec(memory_space=pltpu.VMEM)] * count


def shape(dims, kind):
    return jax.ShapeDtypeStruct(dims, kind)


def project_kernel(
    tokens_hbm, w_hbm, beta_w_hbm, w_out_hbm, out_ref, w_ref, logits_ref, w_own_ref,
    tokens_ref, beta_w_ref, small_sems, w_sems
):
    first = pltpu.make_async_copy(tokens_hbm, tokens_ref, small_sems.at[0])
    last = pltpu.make_async_copy(beta_w_hbm, beta_w_ref, small_sems.at[1])
    copies = [pltpu.make_async_copy(w_hbm.at[s], w_ref.at[s], w_sems.at[s]) for s in range(3)]
    rows = [
        pltpu.make_async_copy(
            w_out_hbm.at[pl.ds(pl.multiple_of((2 * j + bit(1)) * DK, DK), DK)],
            w_own_ref.at[j],
            small_sems.at[2 + j],
        )
        for j in range(2)
    ]
    first.start()
    last.start()
    copies[0].start()
    copies[1].start()
    last.wait()
    first.wait()
    logits_ref[...] = dot_t(tokens_ref[...], beta_w_ref[...])
    for s in range(3):
        copies[s].wait()
        if s == 0:
            copies[2].start()
        if s == 1:
            rows[0].start()
            rows[1].start()
        out_ref[s] = dot(tokens_ref[...], w_ref[s]).astype(bf16)
    rows[0].wait()
    rows[1].wait()


def project(tokens, w_qkv, beta_weight, w_out):
    length, depth = tokens.shape
    columns = w_qkv.shape[2]
    heads = beta_weight.shape[0]
    operands = [
        pltpu.with_memory_space_constraint(x, pltpu.HBM) for x in (tokens, w_qkv, beta_weight, w_out)
    ]
    return pl.pallas_call(
        project_kernel,
        in_specs=[pl.BlockSpec(memory_space=pltpu.HBM)] * 4,
        out_specs=whole(4),
        out_shape=[
            shape((3, length, columns), bf16),
            shape(w_qkv.shape, bf16),
            shape((length, heads), f32),
            shape((2, DK, w_out.shape[1]), bf16),
        ],
        scratch_shapes=[
            pltpu.VMEM(tokens.shape, bf16),
            pltpu.VMEM(beta_weight.shape, bf16),
            pltpu.SemaphoreType.DMA((4,)),
            pltpu.SemaphoreType.DMA((3,)),
        ],
        compiler_params=params(),
        name="project",
    )(*operands)


def grid_index(rows, columns):
    row = lax.broadcasted_iota(jnp.int32, (rows, columns), 0)
    column = lax.broadcasted_iota(jnp.int32, (rows, columns), 1)
    return row, column


def on_diagonal(pair, left):
    zero = jnp.zeros_like(pair)
    return jnp.concatenate([jnp.where(left, pair, zero), jnp.where(left, zero, pair)], axis=0)


def inverse_pairs(systems):
    row, wide = grid_index(BLOCK, 2 * BLOCK)
    column = wide % BLOCK
    left = wide < BLOCK
    eye = jnp.where(row == column, 1.0, 0.0).astype(f32)

    def below(size):
        same = (row // (2 * size)) == (column // (2 * size))
        return same & ((row % (2 * size)) >= size) & ((column % (2 * size)) < size)

    found = [eye - jnp.where(below(1), system, 0.0) for system in systems]
    size = 2
    while size < BLOCK:
        mask = below(size)
        steps = [jnp.where(mask, system, 0.0).astype(bf16) for system in systems]
        small = [x.astype(bf16) for x in found]
        half = [dot(x, on_diagonal(n, left)).astype(bf16) for x, n in zip(small, steps)]
        found = [
            x - dot(y, on_diagonal(b, left)) for x, y, b in zip(found, half, small)
        ]
        size *= 2
    small = [x.astype(bf16) for x in found]
    high = [system.astype(bf16) for system in systems]
    low = [(system - h.astype(f32)).astype(bf16) for system, h in zip(systems, high)]
    rest = [
        (eye - x.astype(f32)) - dot(x, on_diagonal(h, left)) - dot(x, on_diagonal(l, left))
        for x, h, l in zip(small, high, low)
    ]
    fixed = [
        x.astype(f32) + dot(r.astype(bf16), on_diagonal(x, left)) for x, r in zip(small, rest)
    ]
    return [x - eye for x in fixed]


def local_kernel(
    proj_ref, w_ref, edge_ref, conv_ref, logits_ref, bias_ref,
    queries_ref, keys_t_ref, uw_ref, keep_ref, send_ref, padded, maps
):
    length = proj_ref.shape[1]
    heads = logits_ref.shape[1]
    betas = 1.0 / (1.0 + jnp.exp(-(logits_ref[...] + bias_ref[...])))
    core = lax.axis_index("ctx") % 2
    first = lax.axis_index("ctx") == 0
    for s in range(3):
        edge = dot(edge_ref[...], w_ref[s]).astype(bf16).astype(f32)
        padded[s, :EDGE] = jnp.where(first, jnp.zeros_like(edge), edge)
        padded[s, EDGE:] = proj_ref[s].astype(f32)
    row, column = grid_index(length, length)
    strict = row > column
    systems, corners, right, keys_t = [], [], [], []
    for h in range(heads):
        lanes = slice(h * DK, (h + 1) * DK)
        mixed = []
        for s in range(3):
            total = jnp.zeros((length, DK), f32)
            for j in range(4):
                start = EDGE - 3 + j
                total = total + conv_ref[s, j : j + 1, lanes] * padded[s, start : start + length, lanes]
            mixed.append(total / (1.0 + jnp.exp(-total)))
        query, key, value = mixed
        query = query * lax.rsqrt(jnp.sum(query * query, axis=-1, keepdims=True) + EPS)
        key = key * lax.rsqrt(jnp.sum(key * key, axis=-1, keepdims=True) + EPS)
        queries_ref[h] = query.astype(bf16)
        small = key.astype(bf16)
        small_t = key.T.astype(bf16)
        keys_t_ref[h] = small_t
        keys_t.append(small_t)
        beta = betas[:, h : h + 1]
        system = jnp.where(strict, beta * dot(small, small_t), 0.0)
        systems.append(jnp.concatenate([system[:BLOCK, :BLOCK], system[BLOCK:, BLOCK:]], axis=1))
        corners.append(system[BLOCK:, :BLOCK].astype(bf16))
        right.append(beta * jnp.concatenate([value, small.astype(f32)], axis=1))
    lowers = [x.astype(bf16) for x in inverse_pairs(systems)]
    firsts = [
        r[:BLOCK] + dot(low[:, :BLOCK], r[:BLOCK].astype(bf16)) for low, r in zip(lowers, right)
    ]
    seconds = [
        r[BLOCK:] - dot(corner, first.astype(bf16))
        for corner, r, first in zip(corners, right, firsts)
    ]
    seconds = [r + dot(low[:, BLOCK:], r.astype(bf16)) for low, r in zip(lowers, seconds)]
    for h in range(heads):
        uw = jnp.concatenate([firsts[h], seconds[h]], axis=0).astype(bf16)
        uw_ref[h] = uw
        maps[h] = dot(keys_t[h], uw).astype(bf16)
    for j in range(heads // 2):
        keep_ref[j] = maps[2 * j + core]
        send_ref[j] = maps[2 * j + 1 - core]


def local_maps(projected, weights, edge, conv_weight, logits, beta_bias):
    length, columns = projected.shape[1:]
    heads = logits.shape[1]
    two = shape((heads // 2, DK, 2 * DK), bf16)
    return pl.pallas_call(
        local_kernel,
        in_specs=whole(6),
        out_specs=whole(5),
        out_shape=[
            shape((heads, length, DK), bf16),
            shape((heads, DK, length), bf16),
            shape((heads, length, 2 * DK), bf16),
            two, two,
        ],
        scratch_shapes=[
            pltpu.VMEM((3, EDGE + length, columns), f32),
            pltpu.VMEM((heads, DK, 2 * DK), bf16),
        ],
        compiler_params=params(),
        name="local_maps",
    )(projected, weights, edge, conv_weight, logits, beta_bias[None, :])


def inner_kernel(queries_ref, keys_t_ref, uw_ref, base_ref, gate_ref, both_out):
    length = queries_ref.shape[1]
    row, column = grid_index(length, length)
    core = bit(1)
    for j in range(2):
        for h, base, gate in (
            (2 * j + core, base_ref.at[j], gate_ref.at[j]),
            (2 * j + 1 - core, both_out.at[0, j], both_out.at[1, j]),
        ):
            query = queries_ref[h]
            scores = jnp.where(row >= column, dot(query, keys_t_ref[h]), 0.0).astype(bf16)
            both = dot(scores, uw_ref[h])
            base[...] = both[:, :DK].astype(base.dtype)
            gate[...] = (query.astype(f32) - both[:, DK:]).astype(bf16)


def inner_outputs(queries, keys_t, uw):
    heads, length, _ = queries.shape
    outs = [shape((2, length, DK), f32), shape((2, length, DK), bf16)]
    outs.append(shape((2, 2, length, DK), bf16))
    return pl.pallas_call(
        inner_kernel,
        in_specs=whole(3),
        out_specs=whole(3),
        out_shape=outs,
        compiler_params=params(),
        cost_estimate=pl.CostEstimate(
            flops=2 * heads * length * length * 3 * DK, bytes_accessed=2 << 20, transcendentals=0
        ),
        name="inner_outputs",
    )(queries, keys_t, uw)


def then(earlier, later):
    return earlier + later - dot(later[:, DK:].astype(bf16), earlier.astype(bf16))


def advance(state, later):
    return state + later[:, :DK] - dot(later[:, DK:].astype(bf16), state.astype(bf16))


MAP = shape((DK, 2 * DK), bf16)
STATE = shape((DK, DK), bf16)


def small_call(kernel, outs, name, scratch=()):
    return pl.pallas_call(
        kernel,
        out_specs=whole(len(outs)),
        out_shape=list(outs),
        scratch_shapes=list(scratch),
        compiler_params=params(),
        name=name,
    )


def ordered(mine, other, late):
    return jnp.where(late, other, mine), jnp.where(late, mine, other)


def bit(position):
    return (lax.axis_index("ctx") // position) % 2


def chip_kernel(own_ref, other_ref, keep_ref, send_ref, kept):
    late = bit(1) == 1
    for j in range(2):
        first, second = ordered(own_ref[j].astype(f32), other_ref[j].astype(f32), late)
        kept[j] = then(first, second).astype(bf16)
    keep_ref[...] = kept[bit(2)]
    send_ref[...] = kept[1 - bit(2)]


def four_kernel(own_ref, pair_ref, across_ref, diagonal_ref, total_ref, before_ref):
    upper, late = bit(2) == 1, bit(4) == 1
    own, pair, across, diagonal = (
        ref[...].astype(f32) for ref in (own_ref, pair_ref, across_ref, diagonal_ref)
    )
    mine = then(*ordered(own, pair, upper))
    other = then(*ordered(across, diagonal, upper))
    total_ref[...] = then(*ordered(mine, other, late)).astype(bf16)
    before_ref[...] = jnp.where(late, other, jnp.zeros_like(other)).astype(bf16)


def far_kernel(own_ref, other_ref, near_ref, total_ref, before_ref):
    late = bit(8) == 1
    own, other = own_ref[...].astype(f32), other_ref[...].astype(f32)
    near = near_ref[...].astype(f32)
    first, second = ordered(own, other, late)
    total_ref[...] = then(first, second).astype(bf16)
    before_ref[...] = jnp.where(late, then(other, near), near).astype(bf16)


def rows_kernel(own_ref, other_ref, total_ref):
    late = bit(16) == 1
    first, second = ordered(own_ref[...].astype(f32), other_ref[...].astype(f32), late)
    total_ref[...] = advance(first[:, :DK], second).astype(bf16)


def pair_start_kernel(rows_ref, row_ref, before_ref, own_ref, other_ref, keep_ref, send_ref):
    state = rows_ref[...].astype(f32)
    state = jnp.where(bit(32) == 1, state, jnp.zeros_like(state))
    late_row = bit(16) == 1
    row = row_ref[...].astype(f32)
    state = jnp.where(late_row, advance(state, row), state)
    state = advance(state, before_ref[...].astype(f32))
    late = bit(2) == 1
    first = jnp.where(late, other_ref[...], own_ref[...]).astype(f32)
    after = advance(state, first)
    keep_ref[...] = jnp.where(late, after, state).astype(bf16)
    send_ref[...] = jnp.where(late, state, after).astype(bf16)


def finish_kernel(
    own_state, other_state, own_maps, other_maps, base_ref, gate_ref, both_in, gain_ref,
    mine_ref, one, two, three, normed
):
    late, upper = bit(1) == 1, bit(2) == 1
    core = bit(1)
    here = lax.axis_index("head")
    own, other = own_state[...].astype(f32), other_state[...].astype(f32)
    for j, state in enumerate(ordered(own, other, upper)):
        first = jnp.where(late, other_maps[j], own_maps[j]).astype(f32)
        after = advance(state, first)
        gain = gain_ref[2 * j + core]
        for slot, start, base, gate in (
            (0, jnp.where(late, after, state), base_ref.at[j], gate_ref.at[j]),
            (1, jnp.where(late, state, after), both_in.at[0, j], both_in.at[1, j]),
        ):
            heads_out = base[...].astype(f32) + dot(gate[...], start.astype(bf16))
            scale = lax.rsqrt(jnp.mean(heads_out * heads_out, axis=-1, keepdims=True) + EPS)
            normed[slot, :, j * DK : (j + 1) * DK] = (heads_out * scale * gain).astype(bf16)
    rows = mine_ref.shape[1]
    for s, ref in enumerate((mine_ref, one, two, three)):
        start = pl.multiple_of((here + s) % 4 * rows, rows)
        for slot in range(2):
            ref[slot] = normed[slot, pl.ds(start, rows), :]


def finish(states, maps, inner, inner_in, norm_gain):
    length = inner[0].shape[1]
    part = shape((2, length // 4, 2 * DK), bf16)
    return small_call(
        finish_kernel, [part] * 4, "finish", [pltpu.VMEM((2, length, 2 * DK), bf16)]
    )(*states, *maps, *inner, inner_in, norm_gain.reshape(4, 1, DK))


def merge_kernel(
    mine_ref, one, two, three, w_own, w_one, w_two0, w_two1, w_three, keep_ref, send_ref
):
    _, rows, width = mine_ref.shape
    total = None
    for ref, weight in ((mine_ref, w_own), (one, w_one), (three, w_three)):
        term = dot(ref[...].reshape(2 * rows, width), weight[...].reshape(width, -1))
        total = term if total is None else total + term
    both = jnp.concatenate([w_two0[...], w_two1[...]], axis=0)
    total = total + dot(two[...].reshape(2 * rows, width), both)
    keep_ref[...] = total[:rows]
    send_ref[...] = total[rows:].astype(bf16)


def merge(parts, weights):
    rows, width = parts[0].shape[1], weights[0].shape[-1]
    return small_call(
        merge_kernel, [shape((rows, width), f32), shape((rows, width), bf16)], "merge"
    )(*parts, *weights)


def swapped(x, by):
    return lax.ppermute(x, "ctx", [(i, i ^ by) for i in range(lax.axis_size("ctx"))])


def turned(x, axis, by):
    count = lax.axis_size(axis)
    return lax.ppermute(x, axis, [(i, (i + by) % count) for i in range(count)])


def per_device(tokens_in, w_qkv, conv_weight, beta_weight, beta_bias, norm_gain, w_out):
    edge = turned(tokens_in[-EDGE:], "ctx", 1)
    projected, weights, logits, w_own = project(tokens_in, w_qkv, beta_weight, w_out)
    queries, keys_t, uw, maps, send = local_maps(
        projected, weights, edge, conv_weight, logits, beta_bias
    )
    send, w_own = lax.optimization_barrier((send, w_own))
    w_one, w_three = turned(w_own, "head", 1), turned(w_own, "head", 3)
    sibling = swapped(send, 1)
    chip, send = small_call(
        chip_kernel, [MAP, MAP], "chip_map", [pltpu.VMEM((2, DK, 2 * DK), bf16)]
    )(maps, sibling)
    pair, across, diagonal = swapped(send, 2), swapped(chip, 4), swapped(send, 6)
    four, near = small_call(four_kernel, [MAP, MAP], "four_map")(chip, pair, across, diagonal)
    row, before = small_call(far_kernel, [MAP, MAP], "far_map")(four, swapped(four, 12), near)
    other_row = swapped(row, 16)
    base, gate, both = inner_outputs(queries, keys_t, uw)
    inner_in = swapped(both, 1)
    (two_rows,) = small_call(rows_kernel, [STATE], "rows_state")(row, other_row)
    two_rows, w_one, w_three = lax.optimization_barrier((two_rows, w_one, w_three))
    w_two = turned(w_one[0], "head", 1), turned(w_three[1], "head", 3)
    rows = swapped(two_rows, 48)
    state, send = small_call(pair_start_kernel, [STATE, STATE], "pair_start")(
        rows, other_row, before, chip, pair
    )
    back = swapped(send, 2)
    mine, one, two, three = finish(
        (state, back), (maps, sibling), (base, gate), inner_in, norm_gain
    )
    one, three, two = turned(one, "head", 1), turned(three, "head", 3), turned(two, "head", 2)
    keep, send = merge([mine, one, two, three], [w_own, w_one, *w_two, w_three])
    return (keep + swapped(send, 1).astype(f32)).astype(bf16)


def solution(mesh):
    return jax.shard_map(
        per_device,
        mesh=mesh,
        in_specs=(
            P("ctx", None),
            P(None, None, "head"),
            P(None, None, "head"),
            P("head", None),
            P("head"),
            P("head"),
            P("head", None),
        ),
        out_specs=P(("ctx", "head"), None),
        check_vma=False,
    )
```

```python
import jax
import jax.numpy as jnp
from jax import lax
from jax.experimental import pallas as pl
from jax.experimental.pallas import tpu as pltpu
from jax.sharding import PartitionSpec as P

DK = 128
BLOCK = 128
WIDTH = 2 * BLOCK
EDGE = 8
EPS = 1e-06
FAN = 4

f32 = jnp.float32
bf16 = jnp.bfloat16


def dot(a, b):
    return lax.dot_general(a, b, (((1,), (0,)), ((), ())), preferred_element_type=f32)


def dot_t(a, b):
    return lax.dot_general(a, b, (((1,), (1,)), ((), ())), preferred_element_type=f32)


def params(megabytes=24):
    return pltpu.CompilerParams(vmem_limit_bytes=megabytes << 20)


def whole(count):
    return [pl.BlockSpec(memory_space=pltpu.VMEM)] * count


def shape(dims, kind):
    return jax.ShapeDtypeStruct(dims, kind)


def project_kernel(
    tokens_hbm, w_hbm, beta_w_hbm, out_ref, w_ref, logits_ref,
    tokens_ref, beta_w_ref, small_sems, w_sems
):
    first = pltpu.make_async_copy(tokens_hbm, tokens_ref, small_sems.at[0])
    last = pltpu.make_async_copy(beta_w_hbm, beta_w_ref, small_sems.at[1])
    copies = [pltpu.make_async_copy(w_hbm.at[s], w_ref.at[s], w_sems.at[s]) for s in range(3)]
    first.start()
    last.start()
    copies[0].start()
    copies[1].start()
    last.wait()
    first.wait()
    logits_ref[...] = dot_t(tokens_ref[...], beta_w_ref[...])
    for s in range(3):
        copies[s].wait()
        if s == 0:
            copies[2].start()
        out_ref[s] = dot(tokens_ref[...], w_ref[s]).astype(bf16)


def project(tokens, w_qkv, beta_weight):
    length, depth = tokens.shape
    columns = w_qkv.shape[2]
    heads = beta_weight.shape[0]
    operands = [
        pltpu.with_memory_space_constraint(x, pltpu.HBM) for x in (tokens, w_qkv, beta_weight)
    ]
    return pl.pallas_call(
        project_kernel,
        in_specs=[pl.BlockSpec(memory_space=pltpu.HBM)] * 3,
        out_specs=whole(3),
        out_shape=[
            shape((3, length, columns), bf16),
            shape(w_qkv.shape, bf16),
            shape((length, heads), f32),
        ],
        scratch_shapes=[
            pltpu.VMEM(tokens.shape, bf16),
            pltpu.VMEM(beta_weight.shape, bf16),
            pltpu.SemaphoreType.DMA((2,)),
            pltpu.SemaphoreType.DMA((3,)),
        ],
        compiler_params=params(),
        name="project",
    )(*operands)


def grid_index(rows, columns):
    row = lax.broadcasted_iota(jnp.int32, (rows, columns), 0)
    column = lax.broadcasted_iota(jnp.int32, (rows, columns), 1)
    return row, column


def on_diagonal(pair, left):
    zero = jnp.zeros_like(pair)
    return jnp.concatenate([jnp.where(left, pair, zero), jnp.where(left, zero, pair)], axis=0)


def inverse_pairs(systems):
    row, wide = grid_index(BLOCK, 2 * BLOCK)
    column = wide % BLOCK
    left = wide < BLOCK
    eye = jnp.where(row == column, 1.0, 0.0).astype(f32)

    def below(size):
        same = (row // (2 * size)) == (column // (2 * size))
        return same & ((row % (2 * size)) >= size) & ((column % (2 * size)) < size)

    found = [eye - jnp.where(below(1), system, 0.0) for system in systems]
    size = 2
    while size < BLOCK:
        mask = below(size)
        steps = [jnp.where(mask, system, 0.0).astype(bf16) for system in systems]
        small = [x.astype(bf16) for x in found]
        half = [dot(x, on_diagonal(n, left)).astype(bf16) for x, n in zip(small, steps)]
        found = [
            x - dot(y, on_diagonal(b, left)) for x, y, b in zip(found, half, small)
        ]
        size *= 2
    small = [x.astype(bf16) for x in found]
    high = [system.astype(bf16) for system in systems]
    low = [(system - h.astype(f32)).astype(bf16) for system, h in zip(systems, high)]
    rest = [
        (eye - x.astype(f32)) - dot(x, on_diagonal(h, left)) - dot(x, on_diagonal(l, left))
        for x, h, l in zip(small, high, low)
    ]
    fixed = [
        x.astype(f32) + dot(r.astype(bf16), on_diagonal(x, left)) for x, r in zip(small, rest)
    ]
    return [x - eye for x in fixed]


def local_kernel(
    proj_ref, w_ref, edge_ref, conv_ref, logits_ref, bias_ref, w_out_hbm,
    queries_ref, keys_t_ref, uw_ref, keep_ref, send_ref, w_own_ref, padded, maps, sems
):
    rows = [
        pltpu.make_async_copy(
            w_out_hbm.at[pl.ds(pl.multiple_of((2 * j + bit(1)) * DK, DK), DK)],
            w_own_ref.at[j],
            sems.at[j],
        )
        for j in range(2)
    ]
    rows[0].start()
    rows[1].start()
    length = proj_ref.shape[1]
    heads = logits_ref.shape[1]
    betas = 1.0 / (1.0 + jnp.exp(-(logits_ref[...] + bias_ref[...])))
    core = lax.axis_index("ctx") % 2
    first = lax.axis_index("ctx") == 0
    for s in range(3):
        edge = dot(edge_ref[...], w_ref[s]).astype(bf16).astype(f32)
        padded[s, :EDGE] = jnp.where(first, jnp.zeros_like(edge), edge)
        padded[s, EDGE:] = proj_ref[s].astype(f32)
    row, column = grid_index(length, length)
    strict = row > column
    systems, corners, right, keys_t = [], [], [], []
    for h in range(heads):
        lanes = slice(h * DK, (h + 1) * DK)
        mixed = []
        for s in range(3):
            total = jnp.zeros((length, DK), f32)
            for j in range(4):
                start = EDGE - 3 + j
                total = total + conv_ref[s, j : j + 1, lanes] * padded[s, start : start + length, lanes]
            mixed.append(total / (1.0 + jnp.exp(-total)))
        query, key, value = mixed
        query = query * lax.rsqrt(jnp.sum(query * query, axis=-1, keepdims=True) + EPS)
        key = key * lax.rsqrt(jnp.sum(key * key, axis=-1, keepdims=True) + EPS)
        queries_ref[h] = query.astype(bf16)
        small = key.astype(bf16)
        small_t = key.T.astype(bf16)
        keys_t_ref[h] = small_t
        keys_t.append(small_t)
        beta = betas[:, h : h + 1]
        system = jnp.where(strict, beta * dot(small, small_t), 0.0)
        systems.append(jnp.concatenate([system[:BLOCK, :BLOCK], system[BLOCK:, BLOCK:]], axis=1))
        corners.append(system[BLOCK:, :BLOCK].astype(bf16))
        right.append(beta * jnp.concatenate([value, small.astype(f32)], axis=1))
    lowers = [x.astype(bf16) for x in inverse_pairs(systems)]
    firsts = [
        r[:BLOCK] + dot(low[:, :BLOCK], r[:BLOCK].astype(bf16)) for low, r in zip(lowers, right)
    ]
    seconds = [
        r[BLOCK:] - dot(corner, first.astype(bf16))
        for corner, r, first in zip(corners, right, firsts)
    ]
    seconds = [r + dot(low[:, BLOCK:], r.astype(bf16)) for low, r in zip(lowers, seconds)]
    for h in range(heads):
        uw = jnp.concatenate([firsts[h], seconds[h]], axis=0).astype(bf16)
        uw_ref[h] = uw
        maps[h] = dot(keys_t[h], uw).astype(bf16)
    for j in range(heads // 2):
        keep_ref[j] = maps[2 * j + core]
        send_ref[j] = maps[2 * j + 1 - core]
    rows[0].wait()
    rows[1].wait()


def local_maps(projected, weights, edge, conv_weight, logits, beta_bias, w_out):
    length, columns = projected.shape[1:]
    heads = logits.shape[1]
    two = shape((heads // 2, DK, 2 * DK), bf16)
    return pl.pallas_call(
        local_kernel,
        in_specs=whole(6) + [pl.BlockSpec(memory_space=pltpu.HBM)],
        out_specs=whole(6),
        out_shape=[
            shape((heads, length, DK), bf16),
            shape((heads, DK, length), bf16),
            shape((heads, length, 2 * DK), bf16),
            two, two,
            shape((2, DK, w_out.shape[1]), bf16),
        ],
        scratch_shapes=[
            pltpu.VMEM((3, EDGE + length, columns), f32),
            pltpu.VMEM((heads, DK, 2 * DK), bf16),
            pltpu.SemaphoreType.DMA((2,)),
        ],
        compiler_params=params(),
        name="local_maps",
    )(
        projected, weights, edge, conv_weight, logits, beta_bias[None, :],
        pltpu.with_memory_space_constraint(w_out, pltpu.HBM),
    )


def inner_kernel(queries_ref, keys_t_ref, uw_ref, base_ref, gate_ref, both_out):
    length = queries_ref.shape[1]
    row, column = grid_index(length, length)
    core = bit(1)
    for j in range(2):
        for h, base, gate in (
            (2 * j + core, base_ref.at[j], gate_ref.at[j]),
            (2 * j + 1 - core, both_out.at[0, j], both_out.at[1, j]),
        ):
            query = queries_ref[h]
            scores = jnp.where(row >= column, dot(query, keys_t_ref[h]), 0.0).astype(bf16)
            both = dot(scores, uw_ref[h])
            base[...] = both[:, :DK].astype(base.dtype)
            gate[...] = (query.astype(f32) - both[:, DK:]).astype(bf16)


def inner_outputs(queries, keys_t, uw):
    heads, length, _ = queries.shape
    outs = [shape((2, length, DK), f32), shape((2, length, DK), bf16)]
    outs.append(shape((2, 2, length, DK), bf16))
    return pl.pallas_call(
        inner_kernel,
        in_specs=whole(3),
        out_specs=whole(3),
        out_shape=outs,
        compiler_params=params(),
        cost_estimate=pl.CostEstimate(
            flops=2 * heads * length * length * 3 * DK, bytes_accessed=2 << 20, transcendentals=0
        ),
        name="inner_outputs",
    )(queries, keys_t, uw)


def then(earlier, later):
    return earlier + later - dot(later[:, DK:].astype(bf16), earlier.astype(bf16))


def advance(state, later):
    return state + later[:, :DK] - dot(later[:, DK:].astype(bf16), state.astype(bf16))


MAP = shape((DK, 2 * DK), bf16)
STATE = shape((DK, DK), bf16)


LONG = pl.CostEstimate(flops=60_000_000_000, bytes_accessed=1 << 20, transcendentals=0)


def small_call(kernel, outs, name, scratch=(), cost=None):
    return pl.pallas_call(
        kernel,
        out_specs=whole(len(outs)),
        out_shape=list(outs),
        scratch_shapes=list(scratch),
        compiler_params=params(),
        cost_estimate=cost,
        name=name,
    )


def ordered(mine, other, late):
    return jnp.where(late, other, mine), jnp.where(late, mine, other)


def bit(position):
    return (lax.axis_index("ctx") // position) % 2


def chip_kernel(own_ref, other_ref, keep_ref, send_ref, kept):
    late = bit(1) == 1
    for j in range(2):
        first, second = ordered(own_ref[j].astype(f32), other_ref[j].astype(f32), late)
        kept[j] = then(first, second).astype(bf16)
    keep_ref[...] = kept[bit(2)]
    send_ref[...] = kept[1 - bit(2)]


def four_kernel(own_ref, pair_ref, across_ref, diagonal_ref, total_ref, before_ref):
    upper, late = bit(2) == 1, bit(4) == 1
    own, pair, across, diagonal = (
        ref[...].astype(f32) for ref in (own_ref, pair_ref, across_ref, diagonal_ref)
    )
    mine = then(*ordered(own, pair, upper))
    other = then(*ordered(across, diagonal, upper))
    total_ref[...] = then(*ordered(mine, other, late)).astype(bf16)
    before_ref[...] = jnp.where(late, other, jnp.zeros_like(other)).astype(bf16)


def far_kernel(own_ref, other_ref, near_ref, total_ref, before_ref):
    late = bit(8) == 1
    own, other = own_ref[...].astype(f32), other_ref[...].astype(f32)
    near = near_ref[...].astype(f32)
    first, second = ordered(own, other, late)
    total_ref[...] = then(first, second).astype(bf16)
    before_ref[...] = jnp.where(late, then(other, near), near).astype(bf16)


def rows_kernel(own_ref, other_ref, total_ref):
    late = bit(16) == 1
    first, second = ordered(own_ref[...].astype(f32), other_ref[...].astype(f32), late)
    total_ref[...] = advance(first[:, :DK], second).astype(bf16)


def pair_start_kernel(rows_ref, row_ref, before_ref, own_ref, other_ref, keep_ref, send_ref):
    state = rows_ref[...].astype(f32)
    state = jnp.where(bit(32) == 1, state, jnp.zeros_like(state))
    late_row = bit(16) == 1
    row = row_ref[...].astype(f32)
    state = jnp.where(late_row, advance(state, row), state)
    state = advance(state, before_ref[...].astype(f32))
    late = bit(2) == 1
    first = jnp.where(late, other_ref[...], own_ref[...]).astype(f32)
    after = advance(state, first)
    keep_ref[...] = jnp.where(late, after, state).astype(bf16)
    send_ref[...] = jnp.where(late, state, after).astype(bf16)


def finish_kernel(
    own_state, other_state, own_maps, other_maps, base_ref, gate_ref, both_in, gain_ref,
    mine_ref, one, two, three, normed
):
    late, upper = bit(1) == 1, bit(2) == 1
    core = bit(1)
    here = lax.axis_index("head")
    own, other = own_state[...].astype(f32), other_state[...].astype(f32)
    for j, state in enumerate(ordered(own, other, upper)):
        first = jnp.where(late, other_maps[j], own_maps[j]).astype(f32)
        after = advance(state, first)
        gain = gain_ref[2 * j + core]
        for slot, start, base, gate in (
            (0, jnp.where(late, after, state), base_ref.at[j], gate_ref.at[j]),
            (1, jnp.where(late, state, after), both_in.at[0, j], both_in.at[1, j]),
        ):
            heads_out = base[...].astype(f32) + dot(gate[...], start.astype(bf16))
            scale = lax.rsqrt(jnp.mean(heads_out * heads_out, axis=-1, keepdims=True) + EPS)
            normed[slot, :, j * DK : (j + 1) * DK] = (heads_out * scale * gain).astype(bf16)
    rows = mine_ref.shape[1]
    for s, ref in enumerate((mine_ref, one, two, three)):
        start = pl.multiple_of((here + s) % 4 * rows, rows)
        for slot in range(2):
            ref[slot] = normed[slot, pl.ds(start, rows), :]


def finish(states, maps, inner, inner_in, norm_gain):
    length = inner[0].shape[1]
    part = shape((2, length // 4, 2 * DK), bf16)
    return small_call(
        finish_kernel, [part] * 4, "finish", [pltpu.VMEM((2, length, 2 * DK), bf16)]
    )(*states, *maps, *inner, inner_in, norm_gain.reshape(4, 1, DK))


def merge_kernel(
    mine_ref, one, two, three, w_own, w_one, w_two0, w_two1, w_three, keep_ref, send_ref
):
    _, rows, width = mine_ref.shape
    total = None
    for ref, weight in ((mine_ref, w_own), (one, w_one), (three, w_three)):
        term = dot(ref[...].reshape(2 * rows, width), weight[...].reshape(width, -1))
        total = term if total is None else total + term
    both = jnp.concatenate([w_two0[...], w_two1[...]], axis=0)
    total = total + dot(two[...].reshape(2 * rows, width), both)
    keep_ref[...] = total[:rows]
    send_ref[...] = total[rows:].astype(bf16)


def merge(parts, weights):
    rows, width = parts[0].shape[1], weights[0].shape[-1]
    return small_call(
        merge_kernel, [shape((rows, width), f32), shape((rows, width), bf16)], "merge"
    )(*parts, *weights)


def swapped(x, by):
    return lax.ppermute(x, "ctx", [(i, i ^ by) for i in range(lax.axis_size("ctx"))])


def turned(x, axis, by):
    count = lax.axis_size(axis)
    return lax.ppermute(x, axis, [(i, (i + by) % count) for i in range(count)])


def per_device(tokens_in, w_qkv, conv_weight, beta_weight, beta_bias, norm_gain, w_out):
    edge = turned(tokens_in[-EDGE:], "ctx", 1)
    projected, weights, logits = project(tokens_in, w_qkv, beta_weight)
    queries, keys_t, uw, maps, send, w_own = local_maps(
        projected, weights, edge, conv_weight, logits, beta_bias, w_out
    )
    w_one, w_three = turned(w_own, "head", 1), turned(w_own, "head", 3)
    sibling = swapped(send, 1)
    chip, send = small_call(
        chip_kernel, [MAP, MAP], "chip_map", [pltpu.VMEM((2, DK, 2 * DK), bf16)], LONG
    )(maps, sibling)
    pair, across, diagonal = swapped(send, 2), swapped(chip, 4), swapped(send, 6)
    four, near = small_call(four_kernel, [MAP, MAP], "four_map")(chip, pair, across, diagonal)
    row, before = small_call(far_kernel, [MAP, MAP], "far_map")(four, swapped(four, 12), near)
    other_row = swapped(row, 16)
    base, gate, both = inner_outputs(queries, keys_t, uw)
    inner_in = swapped(both, 1)
    (two_rows,) = small_call(rows_kernel, [STATE], "rows_state")(row, other_row)
    _, w_one, w_three = lax.optimization_barrier((two_rows, w_one, w_three))
    w_two = turned(w_one[0], "head", 1), turned(w_three[1], "head", 3)
    rows = swapped(two_rows, 48)
    state, send = small_call(pair_start_kernel, [STATE, STATE], "pair_start", (), LONG)(
        rows, other_row, before, chip, pair
    )
    back = swapped(send, 2)
    mine, one, two, three = finish(
        (state, back), (maps, sibling), (base, gate), inner_in, norm_gain
    )
    one, three, two = turned(one, "head", 1), turned(three, "head", 3), turned(two, "head", 2)
    keep, send = merge([mine, one, two, three], [w_own, w_one, *w_two, w_three])
    return (keep + swapped(send, 1).astype(f32)).astype(bf16)


def solution(mesh):
    return jax.shard_map(
        per_device,
        mesh=mesh,
        in_specs=(
            P("ctx", None),
            P(None, None, "head"),
            P(None, None, "head"),
            P("head", None),
            P("head"),
            P("head"),
            P("head", None),
        ),
        out_specs=P(("ctx", "head"), None),
        check_vma=False,
    )
```

```python
import jax
import jax.numpy as jnp
from jax import lax
from jax.experimental import pallas as pl
from jax.experimental.pallas import tpu as pltpu
from jax.sharding import PartitionSpec as P

DK = 128
BLOCK = 128
WIDTH = 2 * BLOCK
EDGE = 8
EPS = 1e-06
FAN = 4

f32 = jnp.float32
bf16 = jnp.bfloat16


def dot(a, b):
    return lax.dot_general(a, b, (((1,), (0,)), ((), ())), preferred_element_type=f32)


def dot_t(a, b):
    return lax.dot_general(a, b, (((1,), (1,)), ((), ())), preferred_element_type=f32)


def params(megabytes=24):
    return pltpu.CompilerParams(vmem_limit_bytes=megabytes << 20)


def whole(count):
    return [pl.BlockSpec(memory_space=pltpu.VMEM)] * count


def shape(dims, kind):
    return jax.ShapeDtypeStruct(dims, kind)


LONG = pl.CostEstimate(flops=60_000_000_000, bytes_accessed=1 << 20, transcendentals=0)


def project_kernel(
    tokens_hbm, w_hbm, beta_w_hbm, w_out_hbm, out_ref, w_ref, logits_ref, w_own_ref,
    tokens_ref, beta_w_ref, small_sems, w_sems
):
    first = pltpu.make_async_copy(tokens_hbm, tokens_ref, small_sems.at[0])
    last = pltpu.make_async_copy(beta_w_hbm, beta_w_ref, small_sems.at[1])
    copies = [pltpu.make_async_copy(w_hbm.at[s], w_ref.at[s], w_sems.at[s]) for s in range(3)]
    rows = [
        pltpu.make_async_copy(
            w_out_hbm.at[pl.ds(pl.multiple_of((2 * j + bit(1)) * DK, DK), DK)],
            w_own_ref.at[j],
            small_sems.at[2 + j],
        )
        for j in range(2)
    ]
    first.start()
    last.start()
    copies[0].start()
    copies[1].start()
    last.wait()
    first.wait()
    logits_ref[...] = dot_t(tokens_ref[...], beta_w_ref[...])
    for s in range(3):
        copies[s].wait()
        if s == 0:
            copies[2].start()
        if s == 1:
            rows[0].start()
            rows[1].start()
        out_ref[s] = dot(tokens_ref[...], w_ref[s]).astype(bf16)
    rows[0].wait()
    rows[1].wait()


def project(tokens, w_qkv, beta_weight, w_out):
    length, depth = tokens.shape
    columns = w_qkv.shape[2]
    heads = beta_weight.shape[0]
    operands = [
        pltpu.with_memory_space_constraint(x, pltpu.HBM) for x in (tokens, w_qkv, beta_weight, w_out)
    ]
    return pl.pallas_call(
        project_kernel,
        in_specs=[pl.BlockSpec(memory_space=pltpu.HBM)] * 4,
        out_specs=whole(4),
        out_shape=[
            shape((3, length, columns), bf16),
            shape(w_qkv.shape, bf16),
            shape((length, heads), f32),
            shape((2, DK, w_out.shape[1]), bf16),
        ],
        scratch_shapes=[
            pltpu.VMEM(tokens.shape, bf16),
            pltpu.VMEM(beta_weight.shape, bf16),
            pltpu.SemaphoreType.DMA((4,)),
            pltpu.SemaphoreType.DMA((3,)),
        ],
        compiler_params=params(),
        cost_estimate=LONG,
        name="project",
    )(*operands)


def grid_index(rows, columns):
    row = lax.broadcasted_iota(jnp.int32, (rows, columns), 0)
    column = lax.broadcasted_iota(jnp.int32, (rows, columns), 1)
    return row, column


def on_diagonal(pair, left):
    zero = jnp.zeros_like(pair)
    return jnp.concatenate([jnp.where(left, pair, zero), jnp.where(left, zero, pair)], axis=0)


def inverse_pairs(systems):
    row, wide = grid_index(BLOCK, 2 * BLOCK)
    column = wide % BLOCK
    left = wide < BLOCK
    eye = jnp.where(row == column, 1.0, 0.0).astype(f32)

    def below(size):
        same = (row // (2 * size)) == (column // (2 * size))
        return same & ((row % (2 * size)) >= size) & ((column % (2 * size)) < size)

    found = [eye - jnp.where(below(1), system, 0.0) for system in systems]
    size = 2
    while size < BLOCK:
        mask = below(size)
        steps = [jnp.where(mask, system, 0.0).astype(bf16) for system in systems]
        small = [x.astype(bf16) for x in found]
        half = [dot(x, on_diagonal(n, left)).astype(bf16) for x, n in zip(small, steps)]
        found = [
            x - dot(y, on_diagonal(b, left)) for x, y, b in zip(found, half, small)
        ]
        size *= 2
    small = [x.astype(bf16) for x in found]
    high = [system.astype(bf16) for system in systems]
    low = [(system - h.astype(f32)).astype(bf16) for system, h in zip(systems, high)]
    rest = [
        (eye - x.astype(f32)) - dot(x, on_diagonal(h, left)) - dot(x, on_diagonal(l, left))
        for x, h, l in zip(small, high, low)
    ]
    fixed = [
        x.astype(f32) + dot(r.astype(bf16), on_diagonal(x, left)) for x, r in zip(small, rest)
    ]
    return [x - eye for x in fixed]


def local_kernel(
    proj_ref, w_ref, edge_ref, conv_ref, logits_ref, bias_ref,
    queries_ref, keys_t_ref, uw_ref, keep_ref, send_ref, padded, maps
):
    length = proj_ref.shape[1]
    heads = logits_ref.shape[1]
    betas = 1.0 / (1.0 + jnp.exp(-(logits_ref[...] + bias_ref[...])))
    core = lax.axis_index("ctx") % 2
    first = lax.axis_index("ctx") == 0
    for s in range(3):
        edge = dot(edge_ref[...], w_ref[s]).astype(bf16).astype(f32)
        padded[s, :EDGE] = jnp.where(first, jnp.zeros_like(edge), edge)
        padded[s, EDGE:] = proj_ref[s].astype(f32)
    row, column = grid_index(length, length)
    strict = row > column
    systems, corners, right, keys_t = [], [], [], []
    for h in range(heads):
        lanes = slice(h * DK, (h + 1) * DK)
        mixed = []
        for s in range(3):
            total = jnp.zeros((length, DK), f32)
            for j in range(4):
                start = EDGE - 3 + j
                total = total + conv_ref[s, j : j + 1, lanes] * padded[s, start : start + length, lanes]
            mixed.append(total / (1.0 + jnp.exp(-total)))
        query, key, value = mixed
        query = query * lax.rsqrt(jnp.sum(query * query, axis=-1, keepdims=True) + EPS)
        key = key * lax.rsqrt(jnp.sum(key * key, axis=-1, keepdims=True) + EPS)
        queries_ref[h] = query.astype(bf16)
        small = key.astype(bf16)
        small_t = key.T.astype(bf16)
        keys_t_ref[h] = small_t
        keys_t.append(small_t)
        beta = betas[:, h : h + 1]
        system = jnp.where(strict, beta * dot(small, small_t), 0.0)
        systems.append(jnp.concatenate([system[:BLOCK, :BLOCK], system[BLOCK:, BLOCK:]], axis=1))
        corners.append(system[BLOCK:, :BLOCK].astype(bf16))
        right.append(beta * jnp.concatenate([value, small.astype(f32)], axis=1))
    lowers = [x.astype(bf16) for x in inverse_pairs(systems)]
    firsts = [
        r[:BLOCK] + dot(low[:, :BLOCK], r[:BLOCK].astype(bf16)) for low, r in zip(lowers, right)
    ]
    seconds = [
        r[BLOCK:] - dot(corner, first.astype(bf16))
        for corner, r, first in zip(corners, right, firsts)
    ]
    seconds = [r + dot(low[:, BLOCK:], r.astype(bf16)) for low, r in zip(lowers, seconds)]
    for h in range(heads):
        uw = jnp.concatenate([firsts[h], seconds[h]], axis=0).astype(bf16)
        uw_ref[h] = uw
        maps[h] = dot(keys_t[h], uw).astype(bf16)
    for j in range(heads // 2):
        keep_ref[j] = maps[2 * j + core]
        send_ref[j] = maps[2 * j + 1 - core]


def local_maps(projected, weights, edge, conv_weight, logits, beta_bias):
    length, columns = projected.shape[1:]
    heads = logits.shape[1]
    two = shape((heads // 2, DK, 2 * DK), bf16)
    return pl.pallas_call(
        local_kernel,
        in_specs=whole(6),
        out_specs=whole(5),
        out_shape=[
            shape((heads, length, DK), bf16),
            shape((heads, DK, length), bf16),
            shape((heads, length, 2 * DK), bf16),
            two, two,
        ],
        scratch_shapes=[
            pltpu.VMEM((3, EDGE + length, columns), f32),
            pltpu.VMEM((heads, DK, 2 * DK), bf16),
        ],
        compiler_params=params(),
        cost_estimate=LONG,
        name="local_maps",
    )(projected, weights, edge, conv_weight, logits, beta_bias[None, :])


def inner_kernel(queries_ref, keys_t_ref, uw_ref, base_ref, gate_ref, both_out):
    length = queries_ref.shape[1]
    row, column = grid_index(length, length)
    core = bit(1)
    for j in range(2):
        for h, base, gate in (
            (2 * j + core, base_ref.at[j], gate_ref.at[j]),
            (2 * j + 1 - core, both_out.at[0, j], both_out.at[1, j]),
        ):
            query = queries_ref[h]
            scores = jnp.where(row >= column, dot(query, keys_t_ref[h]), 0.0).astype(bf16)
            both = dot(scores, uw_ref[h])
            base[...] = both[:, :DK].astype(base.dtype)
            gate[...] = (query.astype(f32) - both[:, DK:]).astype(bf16)


def inner_outputs(queries, keys_t, uw):
    heads, length, _ = queries.shape
    outs = [shape((2, length, DK), f32), shape((2, length, DK), bf16)]
    outs.append(shape((2, 2, length, DK), bf16))
    return pl.pallas_call(
        inner_kernel,
        in_specs=whole(3),
        out_specs=whole(3),
        out_shape=outs,
        compiler_params=params(),
        cost_estimate=pl.CostEstimate(
            flops=2 * heads * length * length * 3 * DK, bytes_accessed=2 << 20, transcendentals=0
        ),
        name="inner_outputs",
    )(queries, keys_t, uw)


def then(earlier, later):
    return earlier + later - dot(later[:, DK:].astype(bf16), earlier.astype(bf16))


def advance(state, later):
    return state + later[:, :DK] - dot(later[:, DK:].astype(bf16), state.astype(bf16))


MAP = shape((DK, 2 * DK), bf16)
STATE = shape((DK, DK), bf16)


def small_call(kernel, outs, name, scratch=(), cost=None):
    return pl.pallas_call(
        kernel,
        out_specs=whole(len(outs)),
        out_shape=list(outs),
        scratch_shapes=list(scratch),
        compiler_params=params(),
        cost_estimate=cost,
        name=name,
    )


def ordered(mine, other, late):
    return jnp.where(late, other, mine), jnp.where(late, mine, other)


def bit(position):
    return (lax.axis_index("ctx") // position) % 2


def chip_kernel(own_ref, other_ref, keep_ref, send_ref, kept):
    late = bit(1) == 1
    for j in range(2):
        first, second = ordered(own_ref[j].astype(f32), other_ref[j].astype(f32), late)
        kept[j] = then(first, second).astype(bf16)
    keep_ref[...] = kept[bit(2)]
    send_ref[...] = kept[1 - bit(2)]


def four_kernel(own_ref, pair_ref, across_ref, diagonal_ref, total_ref, before_ref):
    upper, late = bit(2) == 1, bit(4) == 1
    own, pair, across, diagonal = (
        ref[...].astype(f32) for ref in (own_ref, pair_ref, across_ref, diagonal_ref)
    )
    mine = then(*ordered(own, pair, upper))
    other = then(*ordered(across, diagonal, upper))
    total_ref[...] = then(*ordered(mine, other, late)).astype(bf16)
    before_ref[...] = jnp.where(late, other, jnp.zeros_like(other)).astype(bf16)


def far_kernel(own_ref, other_ref, near_ref, total_ref, before_ref):
    late = bit(8) == 1
    own, other = own_ref[...].astype(f32), other_ref[...].astype(f32)
    near = near_ref[...].astype(f32)
    first, second = ordered(own, other, late)
    total_ref[...] = then(first, second).astype(bf16)
    before_ref[...] = jnp.where(late, then(other, near), near).astype(bf16)


def rows_kernel(own_ref, other_ref, total_ref):
    late = bit(16) == 1
    first, second = ordered(own_ref[...].astype(f32), other_ref[...].astype(f32), late)
    total_ref[...] = advance(first[:, :DK], second).astype(bf16)


def pair_start_kernel(rows_ref, row_ref, before_ref, own_ref, other_ref, keep_ref, send_ref):
    state = rows_ref[...].astype(f32)
    state = jnp.where(bit(32) == 1, state, jnp.zeros_like(state))
    late_row = bit(16) == 1
    row = row_ref[...].astype(f32)
    state = jnp.where(late_row, advance(state, row), state)
    state = advance(state, before_ref[...].astype(f32))
    late = bit(2) == 1
    first = jnp.where(late, other_ref[...], own_ref[...]).astype(f32)
    after = advance(state, first)
    keep_ref[...] = jnp.where(late, after, state).astype(bf16)
    send_ref[...] = jnp.where(late, state, after).astype(bf16)


def finish_kernel(
    own_state, other_state, own_maps, other_maps, base_ref, gate_ref, both_in, gain_ref,
    mine_ref, one, two, three, normed
):
    late, upper = bit(1) == 1, bit(2) == 1
    core = bit(1)
    here = lax.axis_index("head")
    own, other = own_state[...].astype(f32), other_state[...].astype(f32)
    for j, state in enumerate(ordered(own, other, upper)):
        first = jnp.where(late, other_maps[j], own_maps[j]).astype(f32)
        after = advance(state, first)
        gain = gain_ref[2 * j + core]
        for slot, start, base, gate in (
            (0, jnp.where(late, after, state), base_ref.at[j], gate_ref.at[j]),
            (1, jnp.where(late, state, after), both_in.at[0, j], both_in.at[1, j]),
        ):
            heads_out = base[...].astype(f32) + dot(gate[...], start.astype(bf16))
            scale = lax.rsqrt(jnp.mean(heads_out * heads_out, axis=-1, keepdims=True) + EPS)
            normed[slot, :, j * DK : (j + 1) * DK] = (heads_out * scale * gain).astype(bf16)
    rows = mine_ref.shape[1]
    for s, ref in enumerate((mine_ref, one, two, three)):
        start = pl.multiple_of((here + s) % 4 * rows, rows)
        for slot in range(2):
            ref[slot] = normed[slot, pl.ds(start, rows), :]


def finish(states, maps, inner, inner_in, norm_gain):
    length = inner[0].shape[1]
    part = shape((2, length // 4, 2 * DK), bf16)
    return small_call(
        finish_kernel, [part] * 4, "finish", [pltpu.VMEM((2, length, 2 * DK), bf16)]
    )(*states, *maps, *inner, inner_in, norm_gain.reshape(4, 1, DK))


def merge_kernel(
    mine_ref, one, two, three, w_own, w_one, w_two0, w_two1, w_three, keep_ref, send_ref
):
    _, rows, width = mine_ref.shape
    total = None
    for ref, weight in ((mine_ref, w_own), (one, w_one), (three, w_three)):
        term = dot(ref[...].reshape(2 * rows, width), weight[...].reshape(width, -1))
        total = term if total is None else total + term
    both = jnp.concatenate([w_two0[...], w_two1[...]], axis=0)
    total = total + dot(two[...].reshape(2 * rows, width), both)
    keep_ref[...] = total[:rows]
    send_ref[...] = total[rows:].astype(bf16)


def merge(parts, weights):
    rows, width = parts[0].shape[1], weights[0].shape[-1]
    return small_call(
        merge_kernel, [shape((rows, width), f32), shape((rows, width), bf16)], "merge"
    )(*parts, *weights)


def swapped(x, by):
    return lax.ppermute(x, "ctx", [(i, i ^ by) for i in range(lax.axis_size("ctx"))])


def turned(x, axis, by):
    count = lax.axis_size(axis)
    return lax.ppermute(x, axis, [(i, (i + by) % count) for i in range(count)])


def per_device(tokens_in, w_qkv, conv_weight, beta_weight, beta_bias, norm_gain, w_out):
    edge = turned(tokens_in[-EDGE:], "ctx", 1)
    projected, weights, logits, w_own = project(tokens_in, w_qkv, beta_weight, w_out)
    w_one, w_three = turned(w_own, "head", 1), turned(w_own, "head", 3)
    queries, keys_t, uw, maps, send = local_maps(
        projected, weights, edge, conv_weight, logits, beta_bias
    )
    sibling = swapped(send, 1)
    base, gate, both = inner_outputs(queries, keys_t, uw)
    inner_in = swapped(both, 1)
    chip, send = small_call(
        chip_kernel, [MAP, MAP], "chip_map", [pltpu.VMEM((2, DK, 2 * DK), bf16)]
    )(maps, sibling)
    pair, across, diagonal = swapped(send, 2), swapped(chip, 4), swapped(send, 6)
    four, near = small_call(four_kernel, [MAP, MAP], "four_map")(chip, pair, across, diagonal)
    row, before = small_call(far_kernel, [MAP, MAP], "far_map")(four, swapped(four, 12), near)
    other_row = swapped(row, 16)
    (two_rows,) = small_call(rows_kernel, [STATE], "rows_state")(row, other_row)
    _, w_one, w_three = lax.optimization_barrier((two_rows, w_one, w_three))
    w_two = turned(w_one[0], "head", 1), turned(w_three[1], "head", 3)
    rows = swapped(two_rows, 48)
    state, send = small_call(pair_start_kernel, [STATE, STATE], "pair_start", (), LONG)(
        rows, other_row, before, chip, pair
    )
    back = swapped(send, 2)
    mine, one, two, three = finish(
        (state, back), (maps, sibling), (base, gate), inner_in, norm_gain
    )
    one, three, two = turned(one, "head", 1), turned(three, "head", 3), turned(two, "head", 2)
    keep, send = merge([mine, one, two, three], [w_own, w_one, *w_two, w_three])
    return (keep + swapped(send, 1).astype(f32)).astype(bf16)


def solution(mesh):
    return jax.shard_map(
        per_device,
        mesh=mesh,
        in_specs=(
            P("ctx", None),
            P(None, None, "head"),
            P(None, None, "head"),
            P("head", None),
            P("head"),
            P("head"),
            P("head", None),
        ),
        out_specs=P(("ctx", "head"), None),
        check_vma=False,
    )
```

```python
import functools

import jax
import jax.numpy as jnp
from jax import lax
from jax.experimental import pallas as pl
from jax.experimental.pallas import tpu as pltpu
from jax.sharding import PartitionSpec as P

DK = 128
BLOCK = 128
WIDTH = 2 * BLOCK
EDGE = 8
EPS = 1e-06
FAN = 4

f32 = jnp.float32
bf16 = jnp.bfloat16


def dot(a, b):
    return lax.dot_general(a, b, (((1,), (0,)), ((), ())), preferred_element_type=f32)


def dot_t(a, b):
    return lax.dot_general(a, b, (((1,), (1,)), ((), ())), preferred_element_type=f32)


def params(megabytes=24):
    return pltpu.CompilerParams(vmem_limit_bytes=megabytes << 20)


def whole(count):
    return [pl.BlockSpec(memory_space=pltpu.VMEM)] * count


def shape(dims, kind):
    return jax.ShapeDtypeStruct(dims, kind)


LONG = pl.CostEstimate(flops=60_000_000_000, bytes_accessed=1 << 20, transcendentals=0)


def project_kernel(
    tokens_hbm, w_hbm, beta_w_hbm, w_out_hbm, out_ref, w_ref, logits_ref, w_own_ref,
    tokens_ref, beta_w_ref, small_sems, w_sems
):
    first = pltpu.make_async_copy(tokens_hbm, tokens_ref, small_sems.at[0])
    last = pltpu.make_async_copy(beta_w_hbm, beta_w_ref, small_sems.at[1])
    copies = [pltpu.make_async_copy(w_hbm.at[s], w_ref.at[s], w_sems.at[s]) for s in range(3)]
    rows = [
        pltpu.make_async_copy(
            w_out_hbm.at[pl.ds(pl.multiple_of((2 * j + bit(1)) * DK, DK), DK)],
            w_own_ref.at[j],
            small_sems.at[2 + j],
        )
        for j in range(2)
    ]
    first.start()
    last.start()
    copies[0].start()
    copies[1].start()
    last.wait()
    first.wait()
    logits_ref[...] = dot_t(tokens_ref[...], beta_w_ref[...])
    for s in range(3):
        copies[s].wait()
        if s == 0:
            copies[2].start()
        if s == 1:
            rows[0].start()
            rows[1].start()
        out_ref[s] = dot(tokens_ref[...], w_ref[s]).astype(bf16)
    rows[0].wait()
    rows[1].wait()


def project(tokens, w_qkv, beta_weight, w_out):
    length, depth = tokens.shape
    columns = w_qkv.shape[2]
    heads = beta_weight.shape[0]
    operands = [
        pltpu.with_memory_space_constraint(x, pltpu.HBM) for x in (tokens, w_qkv, beta_weight, w_out)
    ]
    return pl.pallas_call(
        project_kernel,
        in_specs=[pl.BlockSpec(memory_space=pltpu.HBM)] * 4,
        out_specs=whole(4),
        out_shape=[
            shape((3, length, columns), bf16),
            shape(w_qkv.shape, bf16),
            shape((length, heads), f32),
            shape((2, DK, w_out.shape[1]), bf16),
        ],
        scratch_shapes=[
            pltpu.VMEM(tokens.shape, bf16),
            pltpu.VMEM(beta_weight.shape, bf16),
            pltpu.SemaphoreType.DMA((4,)),
            pltpu.SemaphoreType.DMA((3,)),
        ],
        compiler_params=params(),
        cost_estimate=LONG,
        name="project",
    )(*operands)


def grid_index(rows, columns):
    row = lax.broadcasted_iota(jnp.int32, (rows, columns), 0)
    column = lax.broadcasted_iota(jnp.int32, (rows, columns), 1)
    return row, column


def on_diagonal(pair, left):
    zero = jnp.zeros_like(pair)
    return jnp.concatenate([jnp.where(left, pair, zero), jnp.where(left, zero, pair)], axis=0)


def inverse_pairs(systems):
    row, wide = grid_index(BLOCK, 2 * BLOCK)
    column = wide & (BLOCK - 1)
    left = wide < BLOCK
    eye = jnp.where(row == column, 1.0, 0.0).astype(f32)

    apart = row ^ column

    def below(size):
        return (apart >= size) & (apart < 2 * size)

    found = [eye - jnp.where(below(1), system, 0.0) for system in systems]
    size = 2
    while size < BLOCK:
        mask = below(size)
        steps = [jnp.where(mask, system, 0.0).astype(bf16) for system in systems]
        small = [x.astype(bf16) for x in found]
        half = [dot(x, on_diagonal(n, left)).astype(bf16) for x, n in zip(small, steps)]
        found = [
            x - dot(y, on_diagonal(b, left)) for x, y, b in zip(found, half, small)
        ]
        size *= 2
    small = [x.astype(bf16) for x in found]
    high = [system.astype(bf16) for system in systems]
    low = [(system - h.astype(f32)).astype(bf16) for system, h in zip(systems, high)]
    rest = [
        (eye - x.astype(f32)) - dot(x, on_diagonal(h, left)) - dot(x, on_diagonal(l, left))
        for x, h, l in zip(small, high, low)
    ]
    fixed = [
        x.astype(f32) + dot(r.astype(bf16), on_diagonal(x, left)) for x, r in zip(small, rest)
    ]
    return [x - eye for x in fixed]


def conv_silu(padded, taps, lanes, length):
    total = jnp.zeros((length, DK), f32)
    for j in range(4):
        start = EDGE - 3 + j
        total = total + taps[j : j + 1, lanes] * padded[start : start + length, lanes]
    return total / (1.0 + jnp.exp(-total))


def unit_rows(x):
    return x * lax.rsqrt(jnp.sum(x * x, axis=-1, keepdims=True) + EPS)


def local_kernel(
    proj_ref, w_ref, edge_ref, conv_ref, logits_ref, bias_ref,
    edge_out_ref, keys_t_ref, uw_ref, keep_ref, send_ref, padded, maps
):
    length = proj_ref.shape[1]
    heads = logits_ref.shape[1]
    betas = 1.0 / (1.0 + jnp.exp(-(logits_ref[...] + bias_ref[...])))
    core = lax.axis_index("ctx") % 2
    first = lax.axis_index("ctx") == 0
    for s in range(3):
        edge = dot(edge_ref[...], w_ref[s]).astype(bf16).astype(f32)
        edge = jnp.where(first, jnp.zeros_like(edge), edge)
        if s == 0:
            edge_out_ref[...] = edge
        else:
            padded[s - 1, :EDGE] = edge
            padded[s - 1, EDGE:] = proj_ref[s].astype(f32)
    row, column = grid_index(length, length)
    strict = row > column
    systems, corners, right, keys_t = [], [], [], []
    for h in range(heads):
        lanes = slice(h * DK, (h + 1) * DK)
        key, value = (
            conv_silu(padded.at[s - 1], conv_ref.at[s], lanes, length) for s in (1, 2)
        )
        key = unit_rows(key)
        small = key.astype(bf16)
        small_t = key.T.astype(bf16)
        keys_t_ref[h] = small_t
        keys_t.append(small_t)
        beta = betas[:, h : h + 1]
        system = jnp.where(strict, beta * dot(small, small_t), 0.0)
        systems.append(jnp.concatenate([system[:BLOCK, :BLOCK], system[BLOCK:, BLOCK:]], axis=1))
        corners.append(system[BLOCK:, :BLOCK].astype(bf16))
        right.append(beta * jnp.concatenate([value, small.astype(f32)], axis=1))
    lowers = [x.astype(bf16) for x in inverse_pairs(systems)]
    firsts = [
        r[:BLOCK] + dot(low[:, :BLOCK], r[:BLOCK].astype(bf16)) for low, r in zip(lowers, right)
    ]
    seconds = [
        r[BLOCK:] - dot(corner, first.astype(bf16))
        for corner, r, first in zip(corners, right, firsts)
    ]
    seconds = [r + dot(low[:, BLOCK:], r.astype(bf16)) for low, r in zip(lowers, seconds)]
    for h in range(heads):
        uw = jnp.concatenate([firsts[h], seconds[h]], axis=0).astype(bf16)
        uw_ref[h] = uw
        maps[h] = dot(keys_t[h], uw).astype(bf16)
    for j in range(heads // 2):
        keep_ref[j] = maps[2 * j + core]
        send_ref[j] = maps[2 * j + 1 - core]


def local_maps(projected, weights, edge, conv_weight, logits, beta_bias):
    length, columns = projected.shape[1:]
    heads = logits.shape[1]
    two = shape((heads // 2, DK, 2 * DK), bf16)
    return pl.pallas_call(
        local_kernel,
        in_specs=whole(6),
        out_specs=whole(5),
        out_shape=[
            shape((EDGE, columns), f32),
            shape((heads, DK, length), bf16),
            shape((heads, length, 2 * DK), bf16),
            two, two,
        ],
        scratch_shapes=[
            pltpu.VMEM((2, EDGE + length, columns), f32),
            pltpu.VMEM((heads, DK, 2 * DK), bf16),
        ],
        compiler_params=params(),
        cost_estimate=LONG,
        name="local_maps",
    )(projected, weights, edge, conv_weight, logits, beta_bias[None, :])


def inner_kernel(
    proj_ref, edge_ref, conv_ref, keys_t_ref, uw_ref, base_ref, gate_ref, both_out, padded, queries
):
    length = proj_ref.shape[1]
    padded[:EDGE] = edge_ref[...]
    padded[EDGE:] = proj_ref[0].astype(f32)
    for h in range(4):
        lanes = slice(h * DK, (h + 1) * DK)
        queries[h] = unit_rows(conv_silu(padded, conv_ref.at[0], lanes, length)).astype(bf16)
    row, column = grid_index(length, length)
    core = bit(1)
    for j in range(2):
        for h, base, gate in (
            (2 * j + core, base_ref.at[j], gate_ref.at[j]),
            (2 * j + 1 - core, both_out.at[0, j], both_out.at[1, j]),
        ):
            query = queries[h]
            scores = jnp.where(row >= column, dot(query, keys_t_ref[h]), 0.0).astype(bf16)
            both = dot(scores, uw_ref[h])
            base[...] = both[:, :DK].astype(base.dtype)
            gate[...] = (query.astype(f32) - both[:, DK:]).astype(bf16)


def inner_outputs(projected, edge, conv_weight, keys_t, uw):
    length, columns = projected.shape[1:]
    heads = keys_t.shape[0]
    outs = [shape((2, length, DK), f32), shape((2, length, DK), bf16)]
    outs.append(shape((2, 2, length, DK), bf16))
    return pl.pallas_call(
        inner_kernel,
        in_specs=whole(5),
        out_specs=whole(3),
        out_shape=outs,
        scratch_shapes=[
            pltpu.VMEM((EDGE + length, columns), f32),
            pltpu.VMEM((heads, length, DK), bf16),
        ],
        compiler_params=params(),
        cost_estimate=pl.CostEstimate(
            flops=2 * heads * length * length * 3 * DK, bytes_accessed=2 << 20, transcendentals=0
        ),
        name="inner_outputs",
    )(projected, edge, conv_weight, keys_t, uw)


def then(earlier, later):
    return earlier + later - dot(later[:, DK:].astype(bf16), earlier.astype(bf16))


def advance(state, later):
    return state + later[:, :DK] - dot(later[:, DK:].astype(bf16), state.astype(bf16))


MAP = shape((DK, 2 * DK), bf16)
STATE = shape((DK, DK), bf16)


def small_call(kernel, outs, name, scratch=(), cost=None):
    return pl.pallas_call(
        kernel,
        out_specs=whole(len(outs)),
        out_shape=list(outs),
        scratch_shapes=list(scratch),
        compiler_params=params(),
        cost_estimate=cost,
        name=name,
    )


def ordered(mine, other, late):
    return jnp.where(late, other, mine), jnp.where(late, mine, other)


def bit(position):
    return (lax.axis_index("ctx") // position) % 2


def chip_kernel(own_ref, other_ref, keep_ref, send_ref, kept):
    late = bit(1) == 1
    for j in range(2):
        first, second = ordered(own_ref[j].astype(f32), other_ref[j].astype(f32), late)
        kept[j] = then(first, second).astype(bf16)
    keep_ref[...] = kept[bit(2)]
    send_ref[...] = kept[1 - bit(2)]


def four_kernel(own_ref, pair_ref, across_ref, diagonal_ref, total_ref, before_ref):
    upper, late = bit(2) == 1, bit(4) == 1
    own, pair, across, diagonal = (
        ref[...].astype(f32) for ref in (own_ref, pair_ref, across_ref, diagonal_ref)
    )
    mine = then(*ordered(own, pair, upper))
    other = then(*ordered(across, diagonal, upper))
    total_ref[...] = then(*ordered(mine, other, late)).astype(bf16)
    before_ref[...] = jnp.where(late, other, jnp.zeros_like(other)).astype(bf16)


def far_kernel(own_ref, other_ref, near_ref, total_ref, before_ref):
    late = bit(8) == 1
    own, other = own_ref[...].astype(f32), other_ref[...].astype(f32)
    near = near_ref[...].astype(f32)
    first, second = ordered(own, other, late)
    total_ref[...] = then(first, second).astype(bf16)
    before_ref[...] = jnp.where(late, then(other, near), near).astype(bf16)


def rows_kernel(own_ref, other_ref, total_ref):
    late = bit(16) == 1
    first, second = ordered(own_ref[...].astype(f32), other_ref[...].astype(f32), late)
    total_ref[...] = advance(first[:, :DK], second).astype(bf16)


def pair_start_kernel(rows_ref, row_ref, before_ref, own_ref, other_ref, keep_ref, send_ref):
    state = rows_ref[...].astype(f32)
    state = jnp.where(bit(32) == 1, state, jnp.zeros_like(state))
    late_row = bit(16) == 1
    row = row_ref[...].astype(f32)
    state = jnp.where(late_row, advance(state, row), state)
    state = advance(state, before_ref[...].astype(f32))
    late = bit(2) == 1
    first = jnp.where(late, other_ref[...], own_ref[...]).astype(f32)
    after = advance(state, first)
    keep_ref[...] = jnp.where(late, after, state).astype(bf16)
    send_ref[...] = jnp.where(late, state, after).astype(bf16)


def finish_kernel(
    own_state, other_state, own_maps, other_maps, base_ref, gate_ref, both_in, gain_ref,
    mine_ref, one, three, two, normed
):
    late, upper = bit(1) == 1, bit(2) == 1
    core = bit(1)
    here = lax.axis_index("head")
    own, other = own_state[...].astype(f32), other_state[...].astype(f32)
    for j, state in enumerate(ordered(own, other, upper)):
        first = jnp.where(late, other_maps[j], own_maps[j]).astype(f32)
        after = advance(state, first)
        gain = gain_ref[2 * j + core]
        for slot, start, base, gate in (
            (0, jnp.where(late, after, state), base_ref.at[j], gate_ref.at[j]),
            (1, jnp.where(late, state, after), both_in.at[0, j], both_in.at[1, j]),
        ):
            heads_out = base[...].astype(f32) + dot(gate[...], start.astype(bf16))
            scale = lax.rsqrt(jnp.mean(heads_out * heads_out, axis=-1, keepdims=True) + EPS)
            normed[slot, :, j * DK : (j + 1) * DK] = (heads_out * scale * gain).astype(bf16)
    rows = mine_ref.shape[1]
    for s, ref in ((0, mine_ref), (1, one), (3, three), (2, two)):
        start = pl.multiple_of((here + s) % 4 * rows, rows)
        for slot in range(2):
            ref[slot] = normed[slot, pl.ds(start, rows), :]


def finish(states, maps, inner, inner_in, norm_gain):
    length = inner[0].shape[1]
    part = shape((2, length // 4, 2 * DK), bf16)
    return small_call(
        finish_kernel, [part] * 4, "finish", [pltpu.VMEM((2, length, 2 * DK), bf16)]
    )(*states, *maps, *inner, inner_in, norm_gain.reshape(4, 1, DK))


def merge_kernel(
    mine_ref, one, two, three, w_own, w_one, w_two0, w_two1, w_three, *rest, slot
):
    rows, width = mine_ref.shape[1:]
    total = None
    for ref, weight in ((mine_ref, w_own), (one, w_one), (three, w_three)):
        term = dot(ref[slot], weight[...].reshape(width, -1))
        total = term if total is None else total + term
    both = jnp.concatenate([w_two0[...], w_two1[...]], axis=0)
    total = total + dot(two[slot], both)
    out_ref = rest[-1]
    out_ref[...] = total.astype(out_ref.dtype)


def merge(parts, weights, slot, kind, name, cost=None):
    rows, width = parts[0].shape[1], weights[0].shape[-1]
    kernel = functools.partial(merge_kernel, slot=slot)
    return small_call(kernel, [shape((rows, width), kind)], name, (), cost)(*parts, *weights)[0]


def swapped(x, by):
    return lax.ppermute(x, "ctx", [(i, i ^ by) for i in range(lax.axis_size("ctx"))])


def turned(x, axis, by):
    count = lax.axis_size(axis)
    return lax.ppermute(x, axis, [(i, (i + by) % count) for i in range(count)])


def per_device(tokens_in, w_qkv, conv_weight, beta_weight, beta_bias, norm_gain, w_out):
    edge = turned(tokens_in[-EDGE:], "ctx", 1)
    projected, weights, logits, w_own = project(tokens_in, w_qkv, beta_weight, w_out)
    w_one, w_three = turned(w_own, "head", 1), turned(w_own, "head", 3)
    edge, keys_t, uw, maps, send = local_maps(
        projected, weights, edge, conv_weight, logits, beta_bias
    )
    sibling = swapped(send, 1)
    base, gate, both = inner_outputs(projected, edge, conv_weight, keys_t, uw)
    inner_in = swapped(both, 1)
    chip, send = small_call(
        chip_kernel, [MAP, MAP], "chip_map", [pltpu.VMEM((2, DK, 2 * DK), bf16)]
    )(maps, sibling)
    pair, across, diagonal = swapped(send, 2), swapped(chip, 4), swapped(send, 6)
    four, near = small_call(four_kernel, [MAP, MAP], "four_map")(chip, pair, across, diagonal)
    row, before = small_call(far_kernel, [MAP, MAP], "far_map")(four, swapped(four, 12), near)
    other_row = swapped(row, 16)
    (two_rows,) = small_call(rows_kernel, [STATE], "rows_state")(row, other_row)
    _, w_one, w_three = lax.optimization_barrier((two_rows, w_one, w_three))
    w_two = turned(w_one[0], "head", 1), turned(w_three[1], "head", 3)
    rows = swapped(two_rows, 48)
    state, send = small_call(pair_start_kernel, [STATE, STATE], "pair_start", (), LONG)(
        rows, other_row, before, chip, pair
    )
    back = swapped(send, 2)
    mine, one, three, two = finish(
        (state, back), (maps, sibling), (base, gate), inner_in, norm_gain
    )
    one, three, two = turned(one, "head", 1), turned(three, "head", 3), turned(two, "head", 2)
    parts, weights = [mine, one, two, three], [w_own, w_one, *w_two, w_three]
    arrived = swapped(merge(parts, weights, 1, bf16, "merge_other"), 1)
    return (merge(parts, weights, 0, f32, "merge_own") + arrived.astype(f32)).astype(bf16)


def solution(mesh):
    return jax.shard_map(
        per_device,
        mesh=mesh,
        in_specs=(
            P("ctx", None),
            P(None, None, "head"),
            P(None, None, "head"),
            P("head", None),
            P("head"),
            P("head"),
            P("head", None),
        ),
        out_specs=P(("ctx", "head"), None),
        check_vma=False,
    )
```

```python
import jax
import jax.numpy as jnp
from jax import lax
from jax.experimental import pallas as pl
from jax.experimental.pallas import tpu as pltpu
from jax.sharding import PartitionSpec as P

DK = 128
BLOCK = 128
WIDTH = 2 * BLOCK
EDGE = 8
EPS = 1e-06
FAN = 4

f32 = jnp.float32
bf16 = jnp.bfloat16


def dot(a, b):
    return lax.dot_general(a, b, (((1,), (0,)), ((), ())), preferred_element_type=f32)


def dot_t(a, b):
    return lax.dot_general(a, b, (((1,), (1,)), ((), ())), preferred_element_type=f32)


def params(megabytes=24):
    return pltpu.CompilerParams(vmem_limit_bytes=megabytes << 20)


def whole(count):
    return [pl.BlockSpec(memory_space=pltpu.VMEM)] * count


def shape(dims, kind):
    return jax.ShapeDtypeStruct(dims, kind)


SHORT = pl.CostEstimate(flops=4_000_000_000, bytes_accessed=1 << 20, transcendentals=0)
LONG = pl.CostEstimate(flops=60_000_000_000, bytes_accessed=1 << 20, transcendentals=0)


def project_kernel(
    tokens_hbm, w_hbm, beta_w_hbm, w_out_hbm, out_ref, w_ref, logits_ref, w_own_ref,
    tokens_ref, beta_w_ref, small_sems, w_sems
):
    first = pltpu.make_async_copy(tokens_hbm, tokens_ref, small_sems.at[0])
    last = pltpu.make_async_copy(beta_w_hbm, beta_w_ref, small_sems.at[1])
    copies = [pltpu.make_async_copy(w_hbm.at[s], w_ref.at[s], w_sems.at[s]) for s in range(3)]
    rows = [
        pltpu.make_async_copy(
            w_out_hbm.at[pl.ds(pl.multiple_of((2 * j + bit(1)) * DK, DK), DK)],
            w_own_ref.at[j],
            small_sems.at[2 + j],
        )
        for j in range(2)
    ]
    first.start()
    last.start()
    copies[0].start()
    copies[1].start()
    last.wait()
    first.wait()
    logits_ref[...] = dot_t(tokens_ref[...], beta_w_ref[...])
    for s in range(3):
        copies[s].wait()
        if s == 0:
            copies[2].start()
        if s == 1:
            rows[0].start()
            rows[1].start()
        out_ref[s] = dot(tokens_ref[...], w_ref[s]).astype(bf16)
    rows[0].wait()
    rows[1].wait()


def project(tokens, w_qkv, beta_weight, w_out):
    length, depth = tokens.shape
    columns = w_qkv.shape[2]
    heads = beta_weight.shape[0]
    operands = [
        pltpu.with_memory_space_constraint(x, pltpu.HBM) for x in (tokens, w_qkv, beta_weight, w_out)
    ]
    return pl.pallas_call(
        project_kernel,
        in_specs=[pl.BlockSpec(memory_space=pltpu.HBM)] * 4,
        out_specs=whole(4),
        out_shape=[
            shape((3, length, columns), bf16),
            shape(w_qkv.shape, bf16),
            shape((length, heads), f32),
            shape((2, DK, w_out.shape[1]), bf16),
        ],
        scratch_shapes=[
            pltpu.VMEM(tokens.shape, bf16),
            pltpu.VMEM(beta_weight.shape, bf16),
            pltpu.SemaphoreType.DMA((4,)),
            pltpu.SemaphoreType.DMA((3,)),
        ],
        compiler_params=params(),
        cost_estimate=LONG,
        name="project",
    )(*operands)


def grid_index(rows, columns):
    row = lax.broadcasted_iota(jnp.int32, (rows, columns), 0)
    column = lax.broadcasted_iota(jnp.int32, (rows, columns), 1)
    return row, column


def on_diagonal(pair, left):
    zero = jnp.zeros_like(pair)
    return jnp.concatenate([jnp.where(left, pair, zero), jnp.where(left, zero, pair)], axis=0)


def inverse_pairs(systems):
    row, wide = grid_index(BLOCK, 2 * BLOCK)
    column = wide & (BLOCK - 1)
    left = wide < BLOCK
    eye = jnp.where(row == column, 1.0, 0.0).astype(f32)

    apart = row ^ column

    def below(size):
        return (apart >= size) & (apart < 2 * size)

    found = [eye - jnp.where(below(1), system, 0.0) for system in systems]
    size = 2
    while size < BLOCK:
        mask = below(size)
        steps = [jnp.where(mask, system, 0.0).astype(bf16) for system in systems]
        small = [x.astype(bf16) for x in found]
        half = [dot(x, on_diagonal(n, left)).astype(bf16) for x, n in zip(small, steps)]
        found = [
            x - dot(y, on_diagonal(b, left)) for x, y, b in zip(found, half, small)
        ]
        size *= 2
    small = [x.astype(bf16) for x in found]
    high = [system.astype(bf16) for system in systems]
    low = [(system - h.astype(f32)).astype(bf16) for system, h in zip(systems, high)]
    rest = [
        (eye - x.astype(f32)) - dot(x, on_diagonal(h, left)) - dot(x, on_diagonal(l, left))
        for x, h, l in zip(small, high, low)
    ]
    fixed = [
        x.astype(f32) + dot(r.astype(bf16), on_diagonal(x, left)) for x, r in zip(small, rest)
    ]
    return [x - eye for x in fixed]


def conv_silu(padded, taps, lanes, length):
    total = jnp.zeros((length, DK), f32)
    for j in range(4):
        start = EDGE - 3 + j
        total = total + taps[j : j + 1, lanes] * padded[start : start + length, lanes]
    return total / (1.0 + jnp.exp(-total))


def unit_rows(x):
    return x * lax.rsqrt(jnp.sum(x * x, axis=-1, keepdims=True) + EPS)


def local_kernel(
    proj_ref, w_ref, edge_ref, conv_ref, logits_ref, bias_ref,
    edge_out_ref, keys_t_ref, uw_ref, keep_ref, send_ref, padded, maps
):
    length = proj_ref.shape[1]
    heads = logits_ref.shape[1]
    betas = 1.0 / (1.0 + jnp.exp(-(logits_ref[...] + bias_ref[...])))
    core = lax.axis_index("ctx") % 2
    first = lax.axis_index("ctx") == 0
    for s in range(3):
        edge = dot(edge_ref[...], w_ref[s]).astype(bf16).astype(f32)
        edge = jnp.where(first, jnp.zeros_like(edge), edge)
        if s == 0:
            edge_out_ref[...] = edge
        else:
            padded[s - 1, :EDGE] = edge
            padded[s - 1, EDGE:] = proj_ref[s].astype(f32)
    row, column = grid_index(length, length)
    strict = row > column
    systems, corners, right, keys_t = [], [], [], []
    for h in range(heads):
        lanes = slice(h * DK, (h + 1) * DK)
        key, value = (
            conv_silu(padded.at[s - 1], conv_ref.at[s], lanes, length) for s in (1, 2)
        )
        key = unit_rows(key)
        small = key.astype(bf16)
        small_t = key.T.astype(bf16)
        keys_t_ref[h] = small_t
        keys_t.append(small_t)
        beta = betas[:, h : h + 1]
        system = jnp.where(strict, beta * dot(small, small_t), 0.0)
        systems.append(jnp.concatenate([system[:BLOCK, :BLOCK], system[BLOCK:, BLOCK:]], axis=1))
        corners.append(system[BLOCK:, :BLOCK].astype(bf16))
        right.append(beta * jnp.concatenate([value, small.astype(f32)], axis=1))
    lowers = [x.astype(bf16) for x in inverse_pairs(systems)]
    firsts = [
        r[:BLOCK] + dot(low[:, :BLOCK], r[:BLOCK].astype(bf16)) for low, r in zip(lowers, right)
    ]
    seconds = [
        r[BLOCK:] - dot(corner, first.astype(bf16))
        for corner, r, first in zip(corners, right, firsts)
    ]
    seconds = [r + dot(low[:, BLOCK:], r.astype(bf16)) for low, r in zip(lowers, seconds)]
    for h in range(heads):
        uw = jnp.concatenate([firsts[h], seconds[h]], axis=0).astype(bf16)
        uw_ref[h] = uw
        maps[h] = dot(keys_t[h], uw).astype(bf16)
    for j in range(heads // 2):
        keep_ref[j] = maps[2 * j + core]
        send_ref[j] = maps[2 * j + 1 - core]


def local_maps(projected, weights, edge, conv_weight, logits, beta_bias):
    length, columns = projected.shape[1:]
    heads = logits.shape[1]
    two = shape((heads // 2, DK, 2 * DK), bf16)
    return pl.pallas_call(
        local_kernel,
        in_specs=whole(6),
        out_specs=whole(5),
        out_shape=[
            shape((EDGE, columns), f32),
            shape((heads, DK, length), bf16),
            shape((heads, length, 2 * DK), bf16),
            two, two,
        ],
        scratch_shapes=[
            pltpu.VMEM((2, EDGE + length, columns), f32),
            pltpu.VMEM((heads, DK, 2 * DK), bf16),
        ],
        compiler_params=params(),
        cost_estimate=LONG,
        name="local_maps",
    )(projected, weights, edge, conv_weight, logits, beta_bias[None, :])


def inner_kernel(
    proj_ref, edge_ref, conv_ref, keys_t_ref, uw_ref, base_ref, gate_ref, both_out, padded, queries
):
    length = proj_ref.shape[1]
    padded[:EDGE] = edge_ref[...]
    padded[EDGE:] = proj_ref[0].astype(f32)
    for h in range(4):
        lanes = slice(h * DK, (h + 1) * DK)
        queries[h] = unit_rows(conv_silu(padded, conv_ref.at[0], lanes, length)).astype(bf16)
    row, column = grid_index(length, length)
    core = bit(1)
    for j in range(2):
        for h, base, gate in (
            (2 * j + core, base_ref.at[j], gate_ref.at[j]),
            (2 * j + 1 - core, both_out.at[0, j], both_out.at[1, j]),
        ):
            query = queries[h]
            scores = jnp.where(row >= column, dot(query, keys_t_ref[h]), 0.0).astype(bf16)
            both = dot(scores, uw_ref[h])
            base[...] = both[:, :DK].astype(base.dtype)
            gate[...] = (query.astype(f32) - both[:, DK:]).astype(bf16)


def inner_outputs(projected, edge, conv_weight, keys_t, uw):
    length, columns = projected.shape[1:]
    heads = keys_t.shape[0]
    outs = [shape((2, length, DK), f32), shape((2, length, DK), bf16)]
    outs.append(shape((2, 2, length, DK), bf16))
    return pl.pallas_call(
        inner_kernel,
        in_specs=whole(5),
        out_specs=whole(3),
        out_shape=outs,
        scratch_shapes=[
            pltpu.VMEM((EDGE + length, columns), f32),
            pltpu.VMEM((heads, length, DK), bf16),
        ],
        compiler_params=params(),
        cost_estimate=pl.CostEstimate(
            flops=2 * heads * length * length * 3 * DK, bytes_accessed=2 << 20, transcendentals=0
        ),
        name="inner_outputs",
    )(projected, edge, conv_weight, keys_t, uw)


def then(earlier, later):
    return earlier + later - dot(later[:, DK:].astype(bf16), earlier.astype(bf16))


def advance(state, later):
    return state + later[:, :DK] - dot(later[:, DK:].astype(bf16), state.astype(bf16))


MAP = shape((DK, 2 * DK), bf16)
STATE = shape((DK, DK), bf16)


def small_call(kernel, outs, name, scratch=(), cost=None):
    return pl.pallas_call(
        kernel,
        out_specs=whole(len(outs)),
        out_shape=list(outs),
        scratch_shapes=list(scratch),
        compiler_params=params(),
        cost_estimate=cost,
        name=name,
    )


def ordered(mine, other, late):
    return jnp.where(late, other, mine), jnp.where(late, mine, other)


def bit(position):
    return (lax.axis_index("ctx") // position) % 2


def chip_kernel(own_ref, other_ref, keep_ref, send_ref, kept):
    late = bit(1) == 1
    for j in range(2):
        first, second = ordered(own_ref[j].astype(f32), other_ref[j].astype(f32), late)
        kept[j] = then(first, second).astype(bf16)
    keep_ref[...] = kept[bit(2)]
    send_ref[...] = kept[1 - bit(2)]


def four_kernel(own_ref, pair_ref, across_ref, diagonal_ref, total_ref, before_ref):
    upper, late = bit(2) == 1, bit(4) == 1
    own, pair, across, diagonal = (
        ref[...].astype(f32) for ref in (own_ref, pair_ref, across_ref, diagonal_ref)
    )
    mine = then(*ordered(own, pair, upper))
    other = then(*ordered(across, diagonal, upper))
    total_ref[...] = then(*ordered(mine, other, late)).astype(bf16)
    before_ref[...] = jnp.where(late, other, jnp.zeros_like(other)).astype(bf16)


def far_kernel(own_ref, other_ref, near_ref, total_ref, before_ref):
    late = bit(8) == 1
    own, other = own_ref[...].astype(f32), other_ref[...].astype(f32)
    near = near_ref[...].astype(f32)
    first, second = ordered(own, other, late)
    total_ref[...] = then(first, second).astype(bf16)
    before_ref[...] = jnp.where(late, then(other, near), near).astype(bf16)


def rows_kernel(own_ref, other_ref, total_ref):
    late = bit(16) == 1
    first, second = ordered(own_ref[...].astype(f32), other_ref[...].astype(f32), late)
    total_ref[...] = advance(first[:, :DK], second).astype(bf16)


def pair_start_kernel(rows_ref, row_ref, before_ref, own_ref, other_ref, keep_ref, send_ref):
    state = rows_ref[...].astype(f32)
    state = jnp.where(bit(32) == 1, state, jnp.zeros_like(state))
    late_row = bit(16) == 1
    row = row_ref[...].astype(f32)
    state = jnp.where(late_row, advance(state, row), state)
    state = advance(state, before_ref[...].astype(f32))
    late = bit(2) == 1
    first = jnp.where(late, other_ref[...], own_ref[...]).astype(f32)
    after = advance(state, first)
    keep_ref[...] = jnp.where(late, after, state).astype(bf16)
    send_ref[...] = jnp.where(late, state, after).astype(bf16)


def finish_kernel(
    own_state, other_state, own_maps, other_maps, base_ref, gate_ref, both_in, gain_ref,
    mine_ref, one, three, two, normed
):
    late, upper = bit(1) == 1, bit(2) == 1
    core = bit(1)
    here = lax.axis_index("head")
    own, other = own_state[...].astype(f32), other_state[...].astype(f32)
    for j, state in enumerate(ordered(own, other, upper)):
        first = jnp.where(late, other_maps[j], own_maps[j]).astype(f32)
        after = advance(state, first)
        gain = gain_ref[2 * j + core]
        for slot, start, base, gate in (
            (0, jnp.where(late, after, state), base_ref.at[j], gate_ref.at[j]),
            (1, jnp.where(late, state, after), both_in.at[0, j], both_in.at[1, j]),
        ):
            heads_out = base[...].astype(f32) + dot(gate[...], start.astype(bf16))
            scale = lax.rsqrt(jnp.mean(heads_out * heads_out, axis=-1, keepdims=True) + EPS)
            normed[slot, :, j * DK : (j + 1) * DK] = (heads_out * scale * gain).astype(bf16)
    rows = mine_ref.shape[1]
    for s, ref in ((0, mine_ref), (1, one), (3, three), (2, two)):
        start = pl.multiple_of((here + s) % 4 * rows, rows)
        for slot in range(2):
            ref[slot] = normed[slot, pl.ds(start, rows), :]


def finish(states, maps, inner, inner_in, norm_gain):
    length = inner[0].shape[1]
    part = shape((2, length // 4, 2 * DK), bf16)
    return small_call(
        finish_kernel, [part] * 4, "finish", [pltpu.VMEM((2, length, 2 * DK), bf16)]
    )(*states, *maps, *inner, inner_in, norm_gain.reshape(4, 1, DK))


def merge_kernel(
    mine_ref, one, two, three, w_own, w_one, w_two0, w_two1, w_three, keep_ref, send_ref
):
    _, rows, width = mine_ref.shape
    total = None
    for ref, weight in ((mine_ref, w_own), (one, w_one), (three, w_three)):
        term = dot(ref[...].reshape(2 * rows, width), weight[...].reshape(width, -1))
        total = term if total is None else total + term
    both = jnp.concatenate([w_two0[...], w_two1[...]], axis=0)
    total = total + dot(two[...].reshape(2 * rows, width), both)
    keep_ref[...] = total[:rows]
    send_ref[...] = total[rows:].astype(bf16)


def merge(parts, weights):
    rows, width = parts[0].shape[1], weights[0].shape[-1]
    return small_call(
        merge_kernel, [shape((rows, width), f32), shape((rows, width), bf16)], "merge"
    )(*parts, *weights)


def swapped(x, by):
    return lax.ppermute(x, "ctx", [(i, i ^ by) for i in range(lax.axis_size("ctx"))])


def turned(x, axis, by):
    count = lax.axis_size(axis)
    return lax.ppermute(x, axis, [(i, (i + by) % count) for i in range(count)])


def per_device(tokens_in, w_qkv, conv_weight, beta_weight, beta_bias, norm_gain, w_out):
    edge = turned(tokens_in[-EDGE:], "ctx", 1)
    projected, weights, logits, w_own = project(tokens_in, w_qkv, beta_weight, w_out)
    w_one, w_three = turned(w_own, "head", 1), turned(w_own, "head", 3)
    edge, keys_t, uw, maps, send = local_maps(
        projected, weights, edge, conv_weight, logits, beta_bias
    )
    sibling = swapped(send, 1)
    chip, send = small_call(
        chip_kernel, [MAP, MAP], "chip_map", [pltpu.VMEM((2, DK, 2 * DK), bf16)]
    )(maps, sibling)
    pair, across, diagonal = swapped(send, 2), swapped(chip, 4), swapped(send, 6)
    four, near = small_call(four_kernel, [MAP, MAP], "four_map")(chip, pair, across, diagonal)
    row, before = small_call(far_kernel, [MAP, MAP], "far_map")(four, swapped(four, 12), near)
    _, w_one, w_three = lax.optimization_barrier((row, w_one, w_three))
    w_two = turned(w_one[0], "head", 1), turned(w_three[1], "head", 3)
    other_row = swapped(row, 16)
    (two_rows,) = small_call(rows_kernel, [STATE], "rows_state", (), LONG)(row, other_row)
    _, edge = lax.optimization_barrier((two_rows, edge))
    base, gate, both = inner_outputs(projected, edge, conv_weight, keys_t, uw)
    inner_in = swapped(both, 1)
    rows = swapped(two_rows, 48)
    state, send = small_call(pair_start_kernel, [STATE, STATE], "pair_start", (), SHORT)(
        rows, other_row, before, chip, pair
    )
    back = swapped(send, 2)
    mine, one, three, two = finish(
        (state, back), (maps, sibling), (base, gate), inner_in, norm_gain
    )
    one, three, two = turned(one, "head", 1), turned(three, "head", 3), turned(two, "head", 2)
    keep, send = merge([mine, one, two, three], [w_own, w_one, *w_two, w_three])
    return (keep + swapped(send, 1).astype(f32)).astype(bf16)


def solution(mesh):
    return jax.shard_map(
        per_device,
        mesh=mesh,
        in_specs=(
            P("ctx", None),
            P(None, None, "head"),
            P(None, None, "head"),
            P("head", None),
            P("head"),
            P("head"),
            P("head", None),
        ),
        out_specs=P(("ctx", "head"), None),
        check_vma=False,
    )
```

```python
import jax
import jax.numpy as jnp
from jax import lax
from jax.experimental import pallas as pl
from jax.experimental.pallas import tpu as pltpu
from jax.sharding import PartitionSpec as P

DK = 128
BLOCK = 128
WIDTH = 2 * BLOCK
EDGE = 8
EPS = 1e-06
FAN = 4

f32 = jnp.float32
bf16 = jnp.bfloat16


def dot(a, b):
    return lax.dot_general(a, b, (((1,), (0,)), ((), ())), preferred_element_type=f32)


def dot_t(a, b):
    return lax.dot_general(a, b, (((1,), (1,)), ((), ())), preferred_element_type=f32)


def params(megabytes=24):
    return pltpu.CompilerParams(vmem_limit_bytes=megabytes << 20)


def whole(count):
    return [pl.BlockSpec(memory_space=pltpu.VMEM)] * count


def shape(dims, kind):
    return jax.ShapeDtypeStruct(dims, kind)


SHORT = pl.CostEstimate(flops=4_000_000_000, bytes_accessed=1 << 20, transcendentals=0)
LONG = pl.CostEstimate(flops=60_000_000_000, bytes_accessed=1 << 20, transcendentals=0)


def project_kernel(
    tokens_hbm, w_hbm, beta_w_hbm, w_out_hbm, out_ref, w_ref, logits_ref, w_own_ref,
    tokens_ref, beta_w_ref, small_sems, w_sems
):
    first = pltpu.make_async_copy(tokens_hbm, tokens_ref, small_sems.at[0])
    last = pltpu.make_async_copy(beta_w_hbm, beta_w_ref, small_sems.at[1])
    copies = [pltpu.make_async_copy(w_hbm.at[s], w_ref.at[s], w_sems.at[s]) for s in range(3)]
    rows = [
        pltpu.make_async_copy(
            w_out_hbm.at[pl.ds(pl.multiple_of((2 * j + bit(1)) * DK, DK), DK)],
            w_own_ref.at[j],
            small_sems.at[2 + j],
        )
        for j in range(2)
    ]
    first.start()
    last.start()
    copies[0].start()
    copies[1].start()
    last.wait()
    first.wait()
    logits_ref[...] = dot_t(tokens_ref[...], beta_w_ref[...])
    for s in range(3):
        copies[s].wait()
        if s == 0:
            copies[2].start()
        if s == 1:
            rows[0].start()
            rows[1].start()
        out_ref[s] = dot(tokens_ref[...], w_ref[s]).astype(bf16)
    rows[0].wait()
    rows[1].wait()


def project(tokens, w_qkv, beta_weight, w_out):
    length, depth = tokens.shape
    columns = w_qkv.shape[2]
    heads = beta_weight.shape[0]
    operands = [
        pltpu.with_memory_space_constraint(x, pltpu.HBM) for x in (tokens, w_qkv, beta_weight, w_out)
    ]
    return pl.pallas_call(
        project_kernel,
        in_specs=[pl.BlockSpec(memory_space=pltpu.HBM)] * 4,
        out_specs=whole(4),
        out_shape=[
            shape((3, length, columns), bf16),
            shape(w_qkv.shape, bf16),
            shape((length, heads), f32),
            shape((2, DK, w_out.shape[1]), bf16),
        ],
        scratch_shapes=[
            pltpu.VMEM(tokens.shape, bf16),
            pltpu.VMEM(beta_weight.shape, bf16),
            pltpu.SemaphoreType.DMA((4,)),
            pltpu.SemaphoreType.DMA((3,)),
        ],
        compiler_params=params(),
        cost_estimate=LONG,
        name="project",
    )(*operands)


def grid_index(rows, columns):
    row = lax.broadcasted_iota(jnp.int32, (rows, columns), 0)
    column = lax.broadcasted_iota(jnp.int32, (rows, columns), 1)
    return row, column


def on_diagonal(pair, left):
    zero = jnp.zeros_like(pair)
    return jnp.concatenate([jnp.where(left, pair, zero), jnp.where(left, zero, pair)], axis=0)


def inverse_pairs(systems):
    row, wide = grid_index(BLOCK, 2 * BLOCK)
    column = wide & (BLOCK - 1)
    left = wide < BLOCK
    eye = jnp.where(row == column, 1.0, 0.0).astype(f32)

    apart = row ^ column

    def below(size):
        return (apart >= size) & (apart < 2 * size)

    found = [eye - jnp.where(below(1), system, 0.0) for system in systems]
    size = 2
    while size < BLOCK:
        mask = below(size)
        steps = [jnp.where(mask, system, 0.0).astype(bf16) for system in systems]
        small = [x.astype(bf16) for x in found]
        half = [dot(x, on_diagonal(n, left)).astype(bf16) for x, n in zip(small, steps)]
        found = [
            x - dot(y, on_diagonal(b, left)) for x, y, b in zip(found, half, small)
        ]
        size *= 2
    small = [x.astype(bf16) for x in found]
    high = [system.astype(bf16) for system in systems]
    low = [(system - h.astype(f32)).astype(bf16) for system, h in zip(systems, high)]
    rest = [
        (eye - x.astype(f32)) - dot(x, on_diagonal(h, left)) - dot(x, on_diagonal(l, left))
        for x, h, l in zip(small, high, low)
    ]
    fixed = [
        x.astype(f32) + dot(r.astype(bf16), on_diagonal(x, left)) for x, r in zip(small, rest)
    ]
    return [x - eye for x in fixed]


def conv_silu(padded, taps, lanes, length):
    total = jnp.zeros((length, DK), f32)
    for j in range(4):
        start = EDGE - 3 + j
        total = total + taps[j : j + 1, lanes] * padded[start : start + length, lanes]
    return total / (1.0 + jnp.exp(-total))


def unit_rows(x):
    return x * lax.rsqrt(jnp.sum(x * x, axis=-1, keepdims=True) + EPS)


def local_kernel(
    proj_ref, w_ref, edge_ref, conv_ref, logits_ref, bias_ref,
    edge_out_ref, keys_t_ref, uw_ref, keep_ref, send_ref, padded, maps
):
    length = proj_ref.shape[1]
    heads = logits_ref.shape[1]
    betas = 1.0 / (1.0 + jnp.exp(-(logits_ref[...] + bias_ref[...])))
    core = lax.axis_index("ctx") % 2
    first = lax.axis_index("ctx") == 0
    for s in range(3):
        edge = dot(edge_ref[...], w_ref[s]).astype(bf16).astype(f32)
        edge = jnp.where(first, jnp.zeros_like(edge), edge)
        if s == 0:
            edge_out_ref[...] = edge
        else:
            padded[s - 1, :EDGE] = edge
            padded[s - 1, EDGE:] = proj_ref[s].astype(f32)
    row, column = grid_index(length, length)
    strict = row > column
    systems, corners, right, keys_t = [], [], [], []
    for h in range(heads):
        lanes = slice(h * DK, (h + 1) * DK)
        key, value = (
            conv_silu(padded.at[s - 1], conv_ref.at[s], lanes, length) for s in (1, 2)
        )
        key = unit_rows(key)
        small = key.astype(bf16)
        small_t = key.T.astype(bf16)
        keys_t_ref[h] = small_t
        keys_t.append(small_t)
        beta = betas[:, h : h + 1]
        system = jnp.where(strict, beta * dot(small, small_t), 0.0)
        systems.append(jnp.concatenate([system[:BLOCK, :BLOCK], system[BLOCK:, BLOCK:]], axis=1))
        corners.append(system[BLOCK:, :BLOCK].astype(bf16))
        right.append(beta * jnp.concatenate([value, small.astype(f32)], axis=1))
    lowers = [x.astype(bf16) for x in inverse_pairs(systems)]
    firsts = [
        r[:BLOCK] + dot(low[:, :BLOCK], r[:BLOCK].astype(bf16)) for low, r in zip(lowers, right)
    ]
    seconds = [
        r[BLOCK:] - dot(corner, first.astype(bf16))
        for corner, r, first in zip(corners, right, firsts)
    ]
    seconds = [r + dot(low[:, BLOCK:], r.astype(bf16)) for low, r in zip(lowers, seconds)]
    for h in range(heads):
        uw = jnp.concatenate([firsts[h], seconds[h]], axis=0).astype(bf16)
        uw_ref[h] = uw
        maps[h] = dot(keys_t[h], uw).astype(bf16)
    for j in range(heads // 2):
        keep_ref[j] = maps[2 * j + core]
        send_ref[j] = maps[2 * j + 1 - core]


def local_maps(projected, weights, edge, conv_weight, logits, beta_bias):
    length, columns = projected.shape[1:]
    heads = logits.shape[1]
    two = shape((heads // 2, DK, 2 * DK), bf16)
    return pl.pallas_call(
        local_kernel,
        in_specs=whole(6),
        out_specs=whole(5),
        out_shape=[
            shape((EDGE, columns), f32),
            shape((heads, DK, length), bf16),
            shape((heads, length, 2 * DK), bf16),
            two, two,
        ],
        scratch_shapes=[
            pltpu.VMEM((2, EDGE + length, columns), f32),
            pltpu.VMEM((heads, DK, 2 * DK), bf16),
        ],
        compiler_params=params(),
        cost_estimate=LONG,
        name="local_maps",
    )(projected, weights, edge, conv_weight, logits, beta_bias[None, :])


def inner_kernel(
    proj_ref, edge_ref, conv_ref, keys_t_ref, uw_ref, base_ref, gate_ref, both_out, padded, queries
):
    length = proj_ref.shape[1]
    padded[:EDGE] = edge_ref[...]
    padded[EDGE:] = proj_ref[0].astype(f32)
    for h in range(4):
        lanes = slice(h * DK, (h + 1) * DK)
        queries[h] = unit_rows(conv_silu(padded, conv_ref.at[0], lanes, length)).astype(bf16)
    row, column = grid_index(length, length)
    core = bit(1)
    for j in range(2):
        for h, base, gate in (
            (2 * j + core, base_ref.at[j], gate_ref.at[j]),
            (2 * j + 1 - core, both_out.at[0, j], both_out.at[1, j]),
        ):
            query = queries[h]
            scores = jnp.where(row >= column, dot(query, keys_t_ref[h]), 0.0).astype(bf16)
            both = dot(scores, uw_ref[h])
            base[...] = both[:, :DK].astype(base.dtype)
            gate[...] = (query.astype(f32) - both[:, DK:]).astype(bf16)


def inner_outputs(projected, edge, conv_weight, keys_t, uw):
    length, columns = projected.shape[1:]
    heads = keys_t.shape[0]
    outs = [shape((2, length, DK), f32), shape((2, length, DK), bf16)]
    outs.append(shape((2, 2, length, DK), bf16))
    return pl.pallas_call(
        inner_kernel,
        in_specs=whole(5),
        out_specs=whole(3),
        out_shape=outs,
        scratch_shapes=[
            pltpu.VMEM((EDGE + length, columns), f32),
            pltpu.VMEM((heads, length, DK), bf16),
        ],
        compiler_params=params(),
        cost_estimate=pl.CostEstimate(
            flops=2 * heads * length * length * 3 * DK, bytes_accessed=2 << 20, transcendentals=0
        ),
        name="inner_outputs",
    )(projected, edge, conv_weight, keys_t, uw)


def then(earlier, later):
    return earlier + later - dot(later[:, DK:].astype(bf16), earlier.astype(bf16))


def advance(state, later):
    return state + later[:, :DK] - dot(later[:, DK:].astype(bf16), state.astype(bf16))


MAP = shape((DK, 2 * DK), bf16)
STATE = shape((DK, DK), bf16)


def small_call(kernel, outs, name, scratch=(), cost=None):
    return pl.pallas_call(
        kernel,
        out_specs=whole(len(outs)),
        out_shape=list(outs),
        scratch_shapes=list(scratch),
        compiler_params=params(),
        cost_estimate=cost,
        name=name,
    )


def ordered(mine, other, late):
    return jnp.where(late, other, mine), jnp.where(late, mine, other)


def bit(position):
    return (lax.axis_index("ctx") // position) % 2


def chip_kernel(own_ref, other_ref, keep_ref, send_ref, kept):
    late = bit(1) == 1
    for j in range(2):
        first, second = ordered(own_ref[j].astype(f32), other_ref[j].astype(f32), late)
        kept[j] = then(first, second).astype(bf16)
    keep_ref[...] = kept[bit(2)]
    send_ref[...] = kept[1 - bit(2)]


def four_kernel(own_ref, diagonal_ref, across_ref, pair_ref, total_ref, before_ref):
    upper, late = bit(2) == 1, bit(4) == 1
    own, pair, across, diagonal = (
        ref[...].astype(f32) for ref in (own_ref, pair_ref, across_ref, diagonal_ref)
    )
    mine = then(*ordered(own, pair, upper))
    other = then(*ordered(across, diagonal, upper))
    total_ref[...] = then(*ordered(mine, other, late)).astype(bf16)
    before_ref[...] = jnp.where(late, other, jnp.zeros_like(other)).astype(bf16)


def far_kernel(own_ref, other_ref, near_ref, total_ref, before_ref):
    late = bit(8) == 1
    own, other = own_ref[...].astype(f32), other_ref[...].astype(f32)
    near = near_ref[...].astype(f32)
    first, second = ordered(own, other, late)
    total_ref[...] = then(first, second).astype(bf16)
    before_ref[...] = jnp.where(late, then(other, near), near).astype(bf16)


def rows_kernel(own_ref, other_ref, total_ref):
    late = bit(16) == 1
    first, second = ordered(own_ref[...].astype(f32), other_ref[...].astype(f32), late)
    total_ref[...] = advance(first[:, :DK], second).astype(bf16)


def pair_start_kernel(rows_ref, row_ref, before_ref, own_ref, other_ref, keep_ref, send_ref):
    state = rows_ref[...].astype(f32)
    state = jnp.where(bit(32) == 1, state, jnp.zeros_like(state))
    late_row = bit(16) == 1
    row = row_ref[...].astype(f32)
    state = jnp.where(late_row, advance(state, row), state)
    state = advance(state, before_ref[...].astype(f32))
    late = bit(2) == 1
    first = jnp.where(late, other_ref[...], own_ref[...]).astype(f32)
    after = advance(state, first)
    keep_ref[...] = jnp.where(late, after, state).astype(bf16)
    send_ref[...] = jnp.where(late, state, after).astype(bf16)


def finish_kernel(
    own_state, other_state, own_maps, other_maps, base_ref, gate_ref, both_in, gain_ref,
    mine_ref, one, three, two, normed
):
    late, upper = bit(1) == 1, bit(2) == 1
    core = bit(1)
    here = lax.axis_index("head")
    own, other = own_state[...].astype(f32), other_state[...].astype(f32)
    for j, state in enumerate(ordered(own, other, upper)):
        first = jnp.where(late, other_maps[j], own_maps[j]).astype(f32)
        after = advance(state, first)
        gain = gain_ref[2 * j + core]
        for slot, start, base, gate in (
            (0, jnp.where(late, after, state), base_ref.at[j], gate_ref.at[j]),
            (1, jnp.where(late, state, after), both_in.at[0, j], both_in.at[1, j]),
        ):
            heads_out = base[...].astype(f32) + dot(gate[...], start.astype(bf16))
            scale = lax.rsqrt(jnp.mean(heads_out * heads_out, axis=-1, keepdims=True) + EPS)
            normed[slot, :, j * DK : (j + 1) * DK] = (heads_out * scale * gain).astype(bf16)
    rows = mine_ref.shape[1]
    for s, ref in ((0, mine_ref), (1, one), (3, three), (2, two)):
        start = pl.multiple_of((here + s) % 4 * rows, rows)
        for slot in range(2):
            ref[slot] = normed[slot, pl.ds(start, rows), :]


def finish(states, maps, inner, inner_in, norm_gain):
    length = inner[0].shape[1]
    part = shape((2, length // 4, 2 * DK), bf16)
    return small_call(
        finish_kernel, [part] * 4, "finish", [pltpu.VMEM((2, length, 2 * DK), bf16)]
    )(*states, *maps, *inner, inner_in, norm_gain.reshape(4, 1, DK))


def merge_kernel(
    mine_ref, one, three, two, w_own, w_one, w_three, w_two0, w_two1, keep_ref, send_ref
):
    _, rows, width = mine_ref.shape
    total = None
    for ref, weight in ((mine_ref, w_own), (one, w_one), (three, w_three)):
        term = dot(ref[...].reshape(2 * rows, width), weight[...].reshape(width, -1))
        total = term if total is None else total + term
    both = jnp.concatenate([w_two0[...], w_two1[...]], axis=0)
    total = total + dot(two[...].reshape(2 * rows, width), both)
    keep_ref[...] = total[:rows]
    send_ref[...] = total[rows:].astype(bf16)


def merge(parts, weights):
    rows, width = parts[0].shape[1], weights[0].shape[-1]
    return small_call(
        merge_kernel, [shape((rows, width), f32), shape((rows, width), bf16)], "merge"
    )(*parts, *weights)


def swapped(x, by):
    return lax.ppermute(x, "ctx", [(i, i ^ by) for i in range(lax.axis_size("ctx"))])


def turned(x, axis, by):
    count = lax.axis_size(axis)
    return lax.ppermute(x, axis, [(i, (i + by) % count) for i in range(count)])


def per_device(tokens_in, w_qkv, conv_weight, beta_weight, beta_bias, norm_gain, w_out):
    edge = turned(tokens_in[-EDGE:], "ctx", 1)
    projected, weights, logits, w_own = project(tokens_in, w_qkv, beta_weight, w_out)
    w_one, w_three = turned(w_own, "head", 1), turned(w_own, "head", 3)
    edge, keys_t, uw, maps, send = local_maps(
        projected, weights, edge, conv_weight, logits, beta_bias
    )
    sibling = swapped(send, 1)
    chip, send = small_call(
        chip_kernel, [MAP, MAP], "chip_map", [pltpu.VMEM((2, DK, 2 * DK), bf16)]
    )(maps, sibling)
    pair, across, diagonal = swapped(send, 2), swapped(chip, 4), swapped(send, 6)
    four, near = small_call(four_kernel, [MAP, MAP], "four_map")(
        chip, diagonal, across, pair
    )
    row, before = small_call(far_kernel, [MAP, MAP], "far_map")(four, swapped(four, 12), near)
    _, w_one, w_three = lax.optimization_barrier((row, w_one, w_three))
    w_two = turned(w_one[0], "head", 1), turned(w_three[1], "head", 3)
    other_row = swapped(row, 16)
    (two_rows,) = small_call(rows_kernel, [STATE], "rows_state", (), LONG)(row, other_row)
    _, edge = lax.optimization_barrier((two_rows, edge))
    base, gate, both = inner_outputs(projected, edge, conv_weight, keys_t, uw)
    inner_in = swapped(both, 1)
    rows = swapped(two_rows, 48)
    state, send = small_call(pair_start_kernel, [STATE, STATE], "pair_start", (), SHORT)(
        rows, other_row, before, chip, pair
    )
    back = swapped(send, 2)
    mine, one, three, two = finish(
        (state, back), (maps, sibling), (base, gate), inner_in, norm_gain
    )
    one, three, two = turned(one, "head", 1), turned(three, "head", 3), turned(two, "head", 2)
    keep, send = merge([mine, one, three, two], [w_own, w_one, w_three, *w_two])
    return (keep + swapped(send, 1).astype(f32)).astype(bf16)


def solution(mesh):
    return jax.shard_map(
        per_device,
        mesh=mesh,
        in_specs=(
            P("ctx", None),
            P(None, None, "head"),
            P(None, None, "head"),
            P("head", None),
            P("head"),
            P("head"),
            P("head", None),
        ),
        out_specs=P(("ctx", "head"), None),
        check_vma=False,
    )
```

```python
import jax
import jax.numpy as jnp
from jax import lax
from jax.experimental import pallas as pl
from jax.experimental.pallas import tpu as pltpu
from jax.sharding import PartitionSpec as P

DK = 128
BLOCK = 128
WIDTH = 2 * BLOCK
EDGE = 8
EPS = 1e-06
FAN = 4

f32 = jnp.float32
bf16 = jnp.bfloat16


def dot(a, b):
    return lax.dot_general(a, b, (((1,), (0,)), ((), ())), preferred_element_type=f32)


def dot_t(a, b):
    return lax.dot_general(a, b, (((1,), (1,)), ((), ())), preferred_element_type=f32)


def params(megabytes=24):
    return pltpu.CompilerParams(vmem_limit_bytes=megabytes << 20)


def whole(count):
    return [pl.BlockSpec(memory_space=pltpu.VMEM)] * count


def shape(dims, kind):
    return jax.ShapeDtypeStruct(dims, kind)


LONG = pl.CostEstimate(flops=60_000_000_000, bytes_accessed=1 << 20, transcendentals=0)


def project_kernel(
    tokens_hbm, w_hbm, beta_w_hbm, w_out_hbm, out_ref, w_ref, logits_ref, w_own_ref,
    tokens_ref, beta_w_ref, small_sems, w_sems
):
    first = pltpu.make_async_copy(tokens_hbm, tokens_ref, small_sems.at[0])
    last = pltpu.make_async_copy(beta_w_hbm, beta_w_ref, small_sems.at[1])
    copies = [pltpu.make_async_copy(w_hbm.at[s], w_ref.at[s], w_sems.at[s]) for s in range(3)]
    rows = [
        pltpu.make_async_copy(
            w_out_hbm.at[pl.ds(pl.multiple_of((2 * j + bit(1)) * DK, DK), DK)],
            w_own_ref.at[j],
            small_sems.at[2 + j],
        )
        for j in range(2)
    ]
    first.start()
    last.start()
    copies[0].start()
    copies[1].start()
    last.wait()
    first.wait()
    logits_ref[...] = dot_t(tokens_ref[...], beta_w_ref[...])
    for s in range(3):
        copies[s].wait()
        if s == 0:
            copies[2].start()
        if s == 1:
            rows[0].start()
            rows[1].start()
        out_ref[s] = dot(tokens_ref[...], w_ref[s]).astype(bf16)
    rows[0].wait()
    rows[1].wait()


def project(tokens, w_qkv, beta_weight, w_out):
    length, depth = tokens.shape
    columns = w_qkv.shape[2]
    heads = beta_weight.shape[0]
    operands = [
        pltpu.with_memory_space_constraint(x, pltpu.HBM) for x in (tokens, w_qkv, beta_weight, w_out)
    ]
    return pl.pallas_call(
        project_kernel,
        in_specs=[pl.BlockSpec(memory_space=pltpu.HBM)] * 4,
        out_specs=whole(4),
        out_shape=[
            shape((3, length, columns), bf16),
            shape(w_qkv.shape, bf16),
            shape((length, heads), f32),
            shape((2, DK, w_out.shape[1]), bf16),
        ],
        scratch_shapes=[
            pltpu.VMEM(tokens.shape, bf16),
            pltpu.VMEM(beta_weight.shape, bf16),
            pltpu.SemaphoreType.DMA((4,)),
            pltpu.SemaphoreType.DMA((3,)),
        ],
        compiler_params=params(),
        cost_estimate=LONG,
        name="project",
    )(*operands)


def grid_index(rows, columns):
    row = lax.broadcasted_iota(jnp.int32, (rows, columns), 0)
    column = lax.broadcasted_iota(jnp.int32, (rows, columns), 1)
    return row, column


def on_diagonal(pair, left):
    zero = jnp.zeros_like(pair)
    return jnp.concatenate([jnp.where(left, pair, zero), jnp.where(left, zero, pair)], axis=0)


def inverse_pairs(systems):
    row, wide = grid_index(BLOCK, 2 * BLOCK)
    column = wide & (BLOCK - 1)
    left = wide < BLOCK
    eye = jnp.where(row == column, 1.0, 0.0).astype(f32)

    apart = row ^ column

    def below(size):
        return (apart >= size) & (apart < 2 * size)

    found = [eye - jnp.where(below(1), system, 0.0) for system in systems]
    size = 2
    while size < BLOCK:
        mask = below(size)
        steps = [jnp.where(mask, system, 0.0).astype(bf16) for system in systems]
        small = [x.astype(bf16) for x in found]
        half = [dot(x, on_diagonal(n, left)).astype(bf16) for x, n in zip(small, steps)]
        found = [
            x - dot(y, on_diagonal(b, left)) for x, y, b in zip(found, half, small)
        ]
        size *= 2
    small = [x.astype(bf16) for x in found]
    high = [system.astype(bf16) for system in systems]
    low = [(system - h.astype(f32)).astype(bf16) for system, h in zip(systems, high)]
    rest = [
        (eye - x.astype(f32)) - dot(x, on_diagonal(h, left)) - dot(x, on_diagonal(l, left))
        for x, h, l in zip(small, high, low)
    ]
    fixed = [
        x.astype(f32) + dot(r.astype(bf16), on_diagonal(x, left)) for x, r in zip(small, rest)
    ]
    return [x - eye for x in fixed]


def conv_silu(padded, taps, lanes, length):
    total = jnp.zeros((length, DK), f32)
    for j in range(4):
        start = EDGE - 3 + j
        total = total + taps[j : j + 1, lanes] * padded[start : start + length, lanes]
    return total / (1.0 + jnp.exp(-total))


def unit_rows(x):
    return x * lax.rsqrt(jnp.sum(x * x, axis=-1, keepdims=True) + EPS)


def local_kernel(
    proj_ref, w_ref, edge_ref, conv_ref, logits_ref, bias_ref,
    edge_out_ref, keys_t_ref, uw_ref, keep_ref, send_ref, padded, maps
):
    length = proj_ref.shape[1]
    heads = logits_ref.shape[1]
    betas = 1.0 / (1.0 + jnp.exp(-(logits_ref[...] + bias_ref[...])))
    core = lax.axis_index("ctx") % 2
    first = lax.axis_index("ctx") == 0
    for s in range(3):
        edge = dot(edge_ref[...], w_ref[s]).astype(bf16).astype(f32)
        edge = jnp.where(first, jnp.zeros_like(edge), edge)
        if s == 0:
            edge_out_ref[...] = edge
        else:
            padded[s - 1, :EDGE] = edge
            padded[s - 1, EDGE:] = proj_ref[s].astype(f32)
    row, column = grid_index(length, length)
    strict = row > column
    systems, corners, right, keys_t = [], [], [], []
    for h in range(heads):
        lanes = slice(h * DK, (h + 1) * DK)
        key, value = (
            conv_silu(padded.at[s - 1], conv_ref.at[s], lanes, length) for s in (1, 2)
        )
        key = unit_rows(key)
        small = key.astype(bf16)
        small_t = key.T.astype(bf16)
        keys_t_ref[h] = small_t
        keys_t.append(small_t)
        beta = betas[:, h : h + 1]
        system = jnp.where(strict, beta * dot(small, small_t), 0.0)
        systems.append(jnp.concatenate([system[:BLOCK, :BLOCK], system[BLOCK:, BLOCK:]], axis=1))
        corners.append(system[BLOCK:, :BLOCK].astype(bf16))
        right.append(beta * jnp.concatenate([value, small.astype(f32)], axis=1))
    lowers = [x.astype(bf16) for x in inverse_pairs(systems)]
    firsts = [
        r[:BLOCK] + dot(low[:, :BLOCK], r[:BLOCK].astype(bf16)) for low, r in zip(lowers, right)
    ]
    seconds = [
        r[BLOCK:] - dot(corner, first.astype(bf16))
        for corner, r, first in zip(corners, right, firsts)
    ]
    seconds = [r + dot(low[:, BLOCK:], r.astype(bf16)) for low, r in zip(lowers, seconds)]
    for h in range(heads):
        uw = jnp.concatenate([firsts[h], seconds[h]], axis=0).astype(bf16)
        uw_ref[h] = uw
        maps[h] = dot(keys_t[h], uw).astype(bf16)
    for j in range(heads // 2):
        keep_ref[j] = maps[2 * j + core]
        send_ref[j] = maps[2 * j + 1 - core]


def local_maps(projected, weights, edge, conv_weight, logits, beta_bias):
    length, columns = projected.shape[1:]
    heads = logits.shape[1]
    two = shape((heads // 2, DK, 2 * DK), bf16)
    return pl.pallas_call(
        local_kernel,
        in_specs=whole(6),
        out_specs=whole(5),
        out_shape=[
            shape((EDGE, columns), f32),
            shape((heads, DK, length), bf16),
            shape((heads, length, 2 * DK), bf16),
            two, two,
        ],
        scratch_shapes=[
            pltpu.VMEM((2, EDGE + length, columns), f32),
            pltpu.VMEM((heads, DK, 2 * DK), bf16),
        ],
        compiler_params=params(),
        cost_estimate=LONG,
        name="local_maps",
    )(projected, weights, edge, conv_weight, logits, beta_bias[None, :])


def inner_kernel(
    proj_ref, edge_ref, conv_ref, keys_t_ref, uw_ref, base_ref, gate_ref, both_out, padded, queries
):
    length = proj_ref.shape[1]
    padded[:EDGE] = edge_ref[...]
    padded[EDGE:] = proj_ref[0].astype(f32)
    for h in range(4):
        lanes = slice(h * DK, (h + 1) * DK)
        queries[h] = unit_rows(conv_silu(padded, conv_ref.at[0], lanes, length)).astype(bf16)
    row, column = grid_index(length, length)
    core = bit(1)
    for j in range(2):
        for h, base, gate in (
            (2 * j + core, base_ref.at[j], gate_ref.at[j]),
            (2 * j + 1 - core, both_out.at[0, j], both_out.at[1, j]),
        ):
            query = queries[h]
            scores = jnp.where(row >= column, dot(query, keys_t_ref[h]), 0.0).astype(bf16)
            both = dot(scores, uw_ref[h])
            base[...] = both[:, :DK].astype(base.dtype)
            gate[...] = (query.astype(f32) - both[:, DK:]).astype(bf16)


def inner_outputs(projected, edge, conv_weight, keys_t, uw):
    length, columns = projected.shape[1:]
    heads = keys_t.shape[0]
    outs = [shape((2, length, DK), f32), shape((2, length, DK), bf16)]
    outs.append(shape((2, 2, length, DK), bf16))
    return pl.pallas_call(
        inner_kernel,
        in_specs=whole(5),
        out_specs=whole(3),
        out_shape=outs,
        scratch_shapes=[
            pltpu.VMEM((EDGE + length, columns), f32),
            pltpu.VMEM((heads, length, DK), bf16),
        ],
        compiler_params=params(),
        cost_estimate=pl.CostEstimate(
            flops=2 * heads * length * length * 3 * DK, bytes_accessed=2 << 20, transcendentals=0
        ),
        name="inner_outputs",
    )(projected, edge, conv_weight, keys_t, uw)


def then(earlier, later):
    return earlier + later - dot(later[:, DK:].astype(bf16), earlier.astype(bf16))


def advance(state, later):
    return state + later[:, :DK] - dot(later[:, DK:].astype(bf16), state.astype(bf16))


MAP = shape((DK, 2 * DK), bf16)
STATE = shape((DK, DK), bf16)


def small_call(kernel, outs, name, scratch=(), cost=None):
    return pl.pallas_call(
        kernel,
        out_specs=whole(len(outs)),
        out_shape=list(outs),
        scratch_shapes=list(scratch),
        compiler_params=params(),
        cost_estimate=cost,
        name=name,
    )


def ordered(mine, other, late):
    return jnp.where(late, other, mine), jnp.where(late, mine, other)


def bit(position):
    return (lax.axis_index("ctx") // position) % 2


def chip_kernel(own_ref, other_ref, keep_ref, send_ref, kept):
    late = bit(1) == 1
    for j in range(2):
        first, second = ordered(own_ref[j].astype(f32), other_ref[j].astype(f32), late)
        kept[j] = then(first, second).astype(bf16)
    keep_ref[...] = kept[bit(2)]
    send_ref[...] = kept[1 - bit(2)]


def four_kernel(own_ref, diagonal_ref, across_ref, pair_ref, total_ref, before_ref):
    upper, late = bit(2) == 1, bit(4) == 1
    own, pair, across, diagonal = (
        ref[...].astype(f32) for ref in (own_ref, pair_ref, across_ref, diagonal_ref)
    )
    mine = then(*ordered(own, pair, upper))
    other = then(*ordered(across, diagonal, upper))
    total_ref[...] = then(*ordered(mine, other, late)).astype(bf16)
    before_ref[...] = jnp.where(late, other, jnp.zeros_like(other)).astype(bf16)


def far_kernel(own_ref, other_ref, near_ref, total_ref, before_ref):
    late = bit(8) == 1
    own, other = own_ref[...].astype(f32), other_ref[...].astype(f32)
    near = near_ref[...].astype(f32)
    first, second = ordered(own, other, late)
    total_ref[...] = then(first, second).astype(bf16)
    before_ref[...] = jnp.where(late, then(other, near), near).astype(bf16)


def rows_kernel(own_ref, other_ref, total_ref):
    late = bit(16) == 1
    first, second = ordered(own_ref[...].astype(f32), other_ref[...].astype(f32), late)
    total_ref[...] = advance(first[:, :DK], second).astype(bf16)


def pair_start_kernel(rows_ref, row_ref, before_ref, own_ref, other_ref, keep_ref, send_ref):
    state = rows_ref[...].astype(f32)
    state = jnp.where(bit(32) == 1, state, jnp.zeros_like(state))
    late_row = bit(16) == 1
    row = row_ref[...].astype(f32)
    state = jnp.where(late_row, advance(state, row), state)
    state = advance(state, before_ref[...].astype(f32))
    late = bit(2) == 1
    first = jnp.where(late, other_ref[...], own_ref[...]).astype(f32)
    after = advance(state, first)
    keep_ref[...] = jnp.where(late, after, state).astype(bf16)
    send_ref[...] = jnp.where(late, state, after).astype(bf16)


def finish_kernel(
    own_state, other_state, own_maps, other_maps, base_ref, gate_ref, both_in, gain_ref,
    mine_ref, one, three, two, normed
):
    late, upper = bit(1) == 1, bit(2) == 1
    core = bit(1)
    here = lax.axis_index("head")
    own, other = own_state[...].astype(f32), other_state[...].astype(f32)
    for j, state in enumerate(ordered(own, other, upper)):
        first = jnp.where(late, other_maps[j], own_maps[j]).astype(f32)
        after = advance(state, first)
        gain = gain_ref[2 * j + core]
        for slot, start, base, gate in (
            (0, jnp.where(late, after, state), base_ref.at[j], gate_ref.at[j]),
            (1, jnp.where(late, state, after), both_in.at[0, j], both_in.at[1, j]),
        ):
            heads_out = base[...].astype(f32) + dot(gate[...], start.astype(bf16))
            scale = lax.rsqrt(jnp.mean(heads_out * heads_out, axis=-1, keepdims=True) + EPS)
            normed[slot, :, j * DK : (j + 1) * DK] = (heads_out * scale * gain).astype(bf16)
    rows = mine_ref.shape[1]
    for s, ref in ((0, mine_ref), (1, one), (3, three), (2, two)):
        start = pl.multiple_of((here + s) % 4 * rows, rows)
        for slot in range(2):
            ref[slot] = normed[slot, pl.ds(start, rows), :]


def finish(states, maps, inner, inner_in, norm_gain):
    length = inner[0].shape[1]
    part = shape((2, length // 4, 2 * DK), bf16)
    return small_call(
        finish_kernel, [part] * 4, "finish", [pltpu.VMEM((2, length, 2 * DK), bf16)]
    )(*states, *maps, *inner, inner_in, norm_gain.reshape(4, 1, DK))


def merge_kernel(
    mine_ref, one, three, two, w_own, w_one, w_three, w_two0, w_two1, keep_ref, send_ref
):
    _, rows, width = mine_ref.shape
    total = None
    for ref, weight in ((mine_ref, w_own), (one, w_one), (three, w_three)):
        term = dot(ref[...].reshape(2 * rows, width), weight[...].reshape(width, -1))
        total = term if total is None else total + term
    both = jnp.concatenate([w_two0[...], w_two1[...]], axis=0)
    total = total + dot(two[...].reshape(2 * rows, width), both)
    keep_ref[...] = total[:rows]
    send_ref[...] = total[rows:].astype(bf16)


def merge(parts, weights):
    rows, width = parts[0].shape[1], weights[0].shape[-1]
    return small_call(
        merge_kernel, [shape((rows, width), f32), shape((rows, width), bf16)], "merge"
    )(*parts, *weights)


def swapped(x, by):
    return lax.ppermute(x, "ctx", [(i, i ^ by) for i in range(lax.axis_size("ctx"))])


def turned(x, axis, by):
    count = lax.axis_size(axis)
    return lax.ppermute(x, axis, [(i, (i + by) % count) for i in range(count)])


def per_device(tokens_in, w_qkv, conv_weight, beta_weight, beta_bias, norm_gain, w_out):
    edge = turned(tokens_in[-EDGE:], "ctx", 1)
    projected, weights, logits, w_own = project(tokens_in, w_qkv, beta_weight, w_out)
    w_one, w_three = turned(w_own, "head", 1), turned(w_own, "head", 3)
    edge, keys_t, uw, maps, send = local_maps(
        projected, weights, edge, conv_weight, logits, beta_bias
    )
    sibling = swapped(send, 1)
    base, gate, both = inner_outputs(projected, edge, conv_weight, keys_t, uw)
    inner_in = swapped(both, 1)
    chip, send = small_call(
        chip_kernel, [MAP, MAP], "chip_map", [pltpu.VMEM((2, DK, 2 * DK), bf16)]
    )(maps, sibling)
    pair, across, diagonal = swapped(send, 2), swapped(chip, 4), swapped(send, 6)
    four, near = small_call(four_kernel, [MAP, MAP], "four_map")(
        chip, diagonal, across, pair
    )
    row, before = small_call(far_kernel, [MAP, MAP], "far_map")(four, swapped(four, 12), near)
    other_row = swapped(row, 16)
    (two_rows,) = small_call(rows_kernel, [STATE], "rows_state")(row, other_row)
    _, w_one, w_three = lax.optimization_barrier((two_rows, w_one, w_three))
    w_two = turned(w_one[0], "head", 1), turned(w_three[1], "head", 3)
    rows = swapped(two_rows, 48)
    state, send = small_call(pair_start_kernel, [STATE, STATE], "pair_start", (), LONG)(
        rows, other_row, before, chip, pair
    )
    back = swapped(send, 2)
    mine, one, three, two = finish(
        (state, back), (maps, sibling), (base, gate), inner_in, norm_gain
    )
    one, three, two = turned(one, "head", 1), turned(three, "head", 3), turned(two, "head", 2)
    keep, send = merge([mine, one, three, two], [w_own, w_one, w_three, *w_two])
    return (keep + swapped(send, 1).astype(f32)).astype(bf16)


def solution(mesh):
    return jax.shard_map(
        per_device,
        mesh=mesh,
        in_specs=(
            P("ctx", None),
            P(None, None, "head"),
            P(None, None, "head"),
            P("head", None),
            P("head"),
            P("head"),
            P("head", None),
        ),
        out_specs=P(("ctx", "head"), None),
        check_vma=False,
    )
```
